32 devices in a mesh: surf: 8 (over y, x, core), norm: 4 (over z).
Axes of the slice: x: 2, y: 2, z: 4, core: 2. Of those that a mesh axis runs over, the one named last changes fastest.
Arguments:
- mode_shapes: bfloat16 [128, 64, 3, 256], P('surf'), may hold values from -6 to 6
- amplitude: float32 [128], replicated, may hold values from -0.046875 to 0.046875
- mode_patch: int32 [128], replicated, may hold values from 0 to 3
- column_patch: int32 [64, 256], replicated, may hold values from 0 to 3
- wall_mask: int32 [64, 256], P('surf'), may hold values 0 or 1
- offsets: int32 [64, 256], P('surf'), may hold values from 0 to 127
- coupling: float32 [64, 64, 256], P('norm', 'surf'), may hold values from 0.5 to 2
- pivot_inv: float32 [64, 64, 9, 256], P('norm', 'surf'), may hold values from -2 to 2
- stiffness: float32 [64, 64, 256], P('norm', 'surf'), may hold values from 0.00021972656 to 0.0005126953
Outputs:
- displacement: float32 [64, 64, 3, 256], P('norm', 'surf')
The draws below stay inside these ranges and needn't reach their ends.
All inputs are finite; a program needn't handle non-finite values. No bound on the sum of `wall_mask` on one device may be relied on, other than what follows from the above.
Results may differ from the reference program's by a relative error of at most 0.0006.
Values may be sent and summed in bfloat16 or wider, within the bound.
A program may use at most 64 MiB of HBM per device.

```python
import math
import jax
import jax.numpy as jnp
from jax import lax

MODES = 128
PATCHES = 4
SWEEPS = 3
SPAN_COUNT_B = 256
SPAN_COUNT_A = 64
DEPTH_COUNT = 64


def coupling_values(key):
    return jnp.exp(jax.random.uniform(key, (DEPTH_COUNT, SPAN_COUNT_A, SPAN_COUNT_B), jnp.float32, math.log(0.5), math.log(2.0)))


def draw_coupling(key, part):
    return coupling_values(jax.random.fold_in(key, 11))


def euler_rotation(angle_a, angle_b, angle_g):
    cos_a, sin_a = (jnp.cos(angle_a), jnp.sin(angle_a))
    cos_b, sin_b = (jnp.cos(angle_b), jnp.sin(angle_b))
    cos_g, sin_g = (jnp.cos(angle_g), jnp.sin(angle_g))
    return [[cos_a * cos_b * cos_g - sin_a * sin_g, -cos_a * cos_b * sin_g - sin_a * cos_g, cos_a * sin_b], [sin_a * cos_b * cos_g + cos_a * sin_g, -sin_a * cos_b * sin_g + cos_a * cos_g, sin_a * sin_b], [-sin_b * cos_g, sin_b * sin_g, cos_b]]


def draw_pivot_inv(key, part):
    links = coupling_values(jax.random.fold_in(key, 11))
    generator_seeds = jax.random.split(jax.random.fold_in(key, 23), 6)
    slow_share = 0.5
    slow_flag = jax.random.uniform(generator_seeds[0], (SPAN_COUNT_A, 3, SPAN_COUNT_B), jnp.float32) < slow_share
    base_gap = jnp.where(slow_flag, 0.5 / DEPTH_COUNT, 0.05)
    roughness = jax.random.uniform(generator_seeds[1], (DEPTH_COUNT, SPAN_COUNT_A, 3, SPAN_COUNT_B), jnp.float32, 0.5, 1.5)
    damping_ratio = 1.0 - base_gap[None] * roughness
    pulse_hit_share = jax.random.randint(generator_seeds[2], (DEPTH_COUNT, SPAN_COUNT_A, 1, SPAN_COUNT_B), 0, DEPTH_COUNT) < 2
    pulse_keep_share = jax.random.uniform(generator_seeds[3], (DEPTH_COUNT, SPAN_COUNT_A, 1, SPAN_COUNT_B), jnp.float32, 0.5, 0.8)
    damping_ratio = damping_ratio * jnp.where(pulse_hit_share, pulse_keep_share, 1.0)
    angles = jax.random.uniform(generator_seeds[4], (3, SPAN_COUNT_A, SPAN_COUNT_B), jnp.float32, -math.pi, math.pi)
    rotation = euler_rotation(angles[0], angles[1], angles[2])
    turn_angles = jax.random.uniform(generator_seeds[5], (3, DEPTH_COUNT, SPAN_COUNT_A, SPAN_COUNT_B), jnp.float32, -0.06, 0.06)
    turning = euler_rotation(turn_angles[0], turn_angles[1], turn_angles[2])
    symmetric = []
    for row_index in range(3):
        symmetric_row = []
        for col_index in range(3):
            value = jnp.zeros((DEPTH_COUNT, SPAN_COUNT_A, SPAN_COUNT_B), jnp.float32)
            for inner_index in range(3):
                value = value + rotation[row_index][inner_index][None] * damping_ratio[:, :, inner_index, :] * rotation[col_index][inner_index][None]
            symmetric_row.append(value)
        symmetric.append(symmetric_row)
    entries = []
    for row_index in range(3):
        for col_index in range(3):
            value = jnp.zeros((DEPTH_COUNT, SPAN_COUNT_A, SPAN_COUNT_B), jnp.float32)
            for inner_index in range(3):
                value = value + symmetric[row_index][inner_index] * turning[inner_index][col_index]
            entries.append(value / links)
    return jnp.stack(entries, axis=2)


def plant(result, stream_key, low, largest):
    longest = result.shape.index(max(result.shape))
    spots = []
    for shift in (0, 1):
        where = [jax.random.randint(jax.random.fold_in(stream_key, axis), (), 0, length) for axis, length in enumerate(result.shape)]
        where[longest] = (where[longest] + shift) % result.shape[longest]
        spots.append(tuple(where))
    return result.at[spots[0]].set(low).at[spots[1]].set(largest)


def levels(key, dims, shards, smallest, high):
    def one(position, shards_of):
        heights = jax.random.uniform(jax.random.fold_in(jax.random.fold_in(key, 6), position), (shards_of,), jnp.float32, smallest / len(shards), high / len(shards))
        return jnp.repeat(jnp.exp(heights), dims[position] // shards_of).reshape((-1,) + (1,) * (len(dims) - position - 1))

    factor_of = one(*shards[0])
    for cut in shards[1:]:
        factor_of = factor_of * one(*cut)
    return factor_of


def noise(own_key, shape, scale, limit, cuts=(), kind=jnp.bfloat16):
    result = scale * jax.random.normal(own_key, shape, jnp.float32)
    if cuts:
        result = result * levels(own_key, shape, cuts, -0.22, 0.18)
    return jnp.clip(result, -limit, limit).astype(kind)


def setup_inputs(seed: int = 0) -> dict:
    splits = jax.random.split(jax.random.key(seed), 10)
    mode_shapes = noise(splits[0], (MODES, SPAN_COUNT_A, 3, SPAN_COUNT_B), 1.0, 6.0, ((0, 8),))
    amplitude = noise(splits[1], (MODES,), (0.5 / DEPTH_COUNT), 0.046875, (), jnp.float32)
    mode_patch = plant(jax.random.randint(splits[2], (MODES,), 0, PATCHES), jax.random.fold_in(splits[2], 1), 0, PATCHES - 1).astype(jnp.int32)
    column_patch = plant(jax.random.randint(splits[3], (SPAN_COUNT_A, SPAN_COUNT_B), 0, PATCHES), jax.random.fold_in(splits[3], 1), 0, PATCHES - 1).astype(jnp.int32)
    wall_mask = plant((jax.random.randint(splits[4], (SPAN_COUNT_A, SPAN_COUNT_B), 0, 4) < 3).astype(jnp.int32), jax.random.fold_in(splits[4], 1), 0, 1)
    offsets = plant(jax.random.randint(splits[5], (SPAN_COUNT_A, SPAN_COUNT_B), 0, 2 * DEPTH_COUNT), jax.random.fold_in(splits[5], 1), 0, (2 * DEPTH_COUNT) - 1).astype(jnp.int32)
    coupling = draw_coupling(jax.random.fold_in(splits[9], 71), 0)
    pivot_inv = draw_pivot_inv(jax.random.fold_in(splits[9], 71), 0)
    stiffness = jnp.clip(jnp.exp(math.log(0.0005126953) - 0.84729784 * jax.random.uniform(splits[8], (DEPTH_COUNT, SPAN_COUNT_A, SPAN_COUNT_B), jnp.float32) ** levels(splits[8], (DEPTH_COUNT, SPAN_COUNT_A, SPAN_COUNT_B), ((0, 4), (1, 8)), -0.2, 0.2)), 0.00021972656, 0.0005126953)
    return dict(mode_shapes=mode_shapes, amplitude=amplitude, mode_patch=mode_patch, column_patch=column_patch, wall_mask=wall_mask, offsets=offsets, coupling=coupling, pivot_inv=pivot_inv, stiffness=stiffness)


def mat_vec(matrix, vector):
    blocks = matrix.reshape(matrix.shape[:-2] + (3, 3, matrix.shape[-1]))
    return jnp.sum(blocks * vector[..., None, :, :], axis=-2)


def forward(pivots, lower_link, right_side, inflow):
    def advance(state_now, layer_data):
        pivot_block, link_row, source_row = layer_data
        updated = mat_vec(pivot_block, source_row + link_row[:, None, :] * state_now)
        return updated, updated

    last_value, forward_values = lax.scan(advance, inflow, (pivots, lower_link, right_side))
    return forward_values, last_value


def backward(pivots, upper_link, forward_values, outflow):
    def advance(state_now, layer_data):
        pivot_block, link_row, value_row = layer_data
        updated = value_row + mat_vec(pivot_block, link_row[:, None, :] * state_now)
        return updated, updated

    first_value, solved = lax.scan(advance, outflow, (pivots, upper_link, forward_values), reverse=True)
    return solved, first_value


def neighbours(displaced):
    zero_column = jnp.zeros_like(displaced[..., :1])
    neighbour_sum = jnp.roll(displaced, 1, axis=1) + jnp.roll(displaced, -1, axis=1)
    neighbour_sum = neighbour_sum + jnp.concatenate([displaced[..., 1:], zero_column], axis=-1)
    return neighbour_sum + jnp.concatenate([zero_column, displaced[..., :-1]], axis=-1)


def reference(mode_shapes, amplitude, mode_patch, column_patch, wall_mask, offsets, coupling, pivot_inv, stiffness):
    select = (mode_patch[:, None, None] == column_patch[None]).astype(jnp.float32)
    weights = amplitude[:, None, None] * select
    wall_shift = jnp.einsum("mij,micj->icj", weights, mode_shapes.astype(jnp.float32))
    wall_shift = wall_shift * wall_mask[:, None, :].astype(jnp.float32)
    depth_index = jnp.arange(DEPTH_COUNT, dtype=jnp.int32)
    lower_link = jnp.where(depth_index[:, None, None] == offsets[None], jnp.zeros_like(coupling), coupling)
    upper_link = jnp.concatenate([lower_link[1:], jnp.zeros_like(lower_link[:1])], axis=0)
    blend_weight = 1.0 - depth_index.astype(jnp.float32) / DEPTH_COUNT
    displaced = blend_weight[:, None, None, None] * wall_shift[None]
    wall_term = lower_link[0][:, None, :] * wall_shift
    zero_state = jnp.zeros((SPAN_COUNT_A, 3, SPAN_COUNT_B), jnp.float32)
    for sweep_index in range(SWEEPS):
        right_side = stiffness[:, :, None, :] * neighbours(displaced)
        right_side = right_side.at[0].add(wall_term)
        forward_values = forward(pivot_inv, lower_link, right_side, zero_state)[0]
        displaced = backward(pivot_inv, upper_link, forward_values, zero_state)[0]
    return displaced
```

```python
import functools

import jax
import jax.numpy as jnp
from jax import lax
from jax.experimental import pallas as pl
from jax.experimental.pallas import tpu as pltpu
from jax.sharding import PartitionSpec as P

SWEEPS = 3
MESH = pl.DeviceIdType.MESH


def loop(count, body, init, unroll=4):
    if count % unroll:
        unroll = 1

    def outer(step, carry):
        for part in range(unroll):
            carry = body(step * unroll + part, carry)
        return carry

    return lax.fori_loop(0, count // unroll, outer, init)


def later(count, body, init, unroll=5):
    return loop(count - 1, lambda step, carry: body(step + 1, carry), init, unroll)


def mat_vec(matrix, vector):
    return [
        matrix[3 * a] * vector[0] + matrix[3 * a + 1] * vector[1] + matrix[3 * a + 2] * vector[2]
        for a in range(3)
    ]


def mat_mat(left, right):
    return [
        left[3 * a] * right[b] + left[3 * a + 1] * right[3 + b] + left[3 * a + 2] * right[6 + b]
        for a in range(3)
        for b in range(3)
    ]


def added(left, right):
    return [a + b for a, b in zip(left, right)]


def planes(ref, index, count=3):
    return [ref[index, c] for c in range(count)]


def put(ref, index, values):
    for c, value in enumerate(values):
        ref[index, c] = value


def kernel(
    surf_size,
    norm_size,
    amplitude,
    mode_patch,
    column_patch,
    wall_mask,
    offsets,
    modes_hbm,
    coupling_hbm,
    pivot_hbm,
    stiffness_hbm,
    out,
    modes,
    coupling,
    pivot,
    stiffness,
    link,
    link_next,
    maps,
    end_map,
    part,
    got,
    mask_edge,
    wall,
    values,
    enter,
    edge_out,
    edge_in,
    halo,
    f_in,
    f_out,
    o_in,
    o_out,
    h_in,
    h_out,
    up_in,
    up_out,
    down_in,
    down_out,
    load_sem,
    part_send,
    part_recv,
    mask_send,
    mask_recv,
    link_send,
    link_recv,
    h_send,
    h_recv,
    up_send,
    up_recv,
    down_send,
    down_recv,
    f_send,
    f_recv,
    o_send,
    o_recv,
    edge_send,
    edge_recv,
):
    S, N = surf_size, norm_size
    K, _, R, W = pivot.shape
    M = modes.shape[0]
    B = 2 * R
    blocks = modes.shape[2] // B
    me = lax.axis_index("surf")
    place = lax.axis_index("norm")
    before = lax.rem(me + S - 1, S)
    after = lax.rem(me + 1, S)
    first, last = place == 0, place == N - 1

    def to_surf(src, dst, send, recv, target):
        return pltpu.make_async_remote_copy(
            src_ref=src, dst_ref=dst, send_sem=send, recv_sem=recv,
            device_id={"surf": target}, device_id_type=MESH,
        )

    def to_norm(src, dst, send, recv, target):
        return pltpu.make_async_remote_copy(
            src_ref=src, dst_ref=dst, send_sem=send, recv_sem=recv,
            device_id={"norm": target}, device_id_type=MESH,
        )

    mode_loads = [
        pltpu.make_async_copy(
            modes_hbm.at[:, :, pl.ds(b * B, B), :], modes.at[:, :, pl.ds(b * B, B), :], load_sem.at[3 + b]
        )
        for b in range(blocks)
    ]
    loads = [
        pltpu.make_async_copy(coupling_hbm, coupling, load_sem.at[0]),
        pltpu.make_async_copy(pivot_hbm, pivot, load_sem.at[1]),
        pltpu.make_async_copy(stiffness_hbm, stiffness, load_sem.at[2]),
    ]
    for copy in mode_loads + loads:
        copy.start()

    barrier = pltpu.get_barrier_semaphore()
    for hop in range(1, S):
        pl.semaphore_signal(
            barrier, inc=1, device_id={"surf": lax.rem(me + hop, S)}, device_id_type=MESH
        )

    for hop in range(1, N):
        pl.semaphore_signal(
            barrier, inc=1, device_id={"norm": lax.rem(place + hop, N)}, device_id_type=MESH
        )

    own_mode = me * M
    for b in range(blocks):
        mode_loads[b].wait()
        patch = column_patch[b * B : (b + 1) * B, :]

        def mode_step(m, sums):
            weight = jnp.where(
                patch == mode_patch[own_mode + m], amplitude[own_mode + m], jnp.float32(0)
            )
            return [
                sums[c] + weight * modes[m, c, b * B : (b + 1) * B, :].astype(jnp.float32)
                for c in range(3)
            ]

        sums = loop(M, mode_step, [jnp.zeros((B, W), jnp.float32)] * 3)
        for c in range(3):
            for side in range(2):
                dest = 2 * b + side
                block = sums[c][side * R : (side + 1) * R]
                part[dest, c] = block
                part[(dest + 1) % S, 3, c : c + 1, :] = block[R - 1 : R]
                part[(dest - 1) % S, 3, 3 + c : 4 + c, :] = block[0:1]

    pl.semaphore_wait(barrier, S + N - 2)

    def part_copy(hop):
        dest = lax.rem(me + hop, S)
        return to_surf(part.at[dest], got.at[hop], part_send.at[hop], part_recv.at[hop], dest)

    for hop in range(1, S):
        part_copy(hop).start()
    mask_up = to_surf(wall_mask, mask_edge.at[0], mask_send.at[0], mask_recv.at[0], after)
    mask_down = to_surf(wall_mask, mask_edge.at[1], mask_send.at[1], mask_recv.at[1], before)
    mask_up.start()
    mask_down.start()
    link_copy = to_norm(coupling_hbm.at[0], link_next, link_send, link_recv, place - 1)

    @pl.when(jnp.logical_not(first))
    def _():
        link_copy.start()

    for copy in loads:
        copy.wait()
    cut = offsets[...]
    base = place * K

    def link_step(k, carry):
        link[k] = jnp.where(cut == base + k, jnp.float32(0), coupling[k])
        return carry

    loop(K, link_step, 0)

    @pl.when(last)
    def _():
        link[K] = jnp.zeros((R, W), jnp.float32)

    def lower_step(k, state):
        scaled = [p * link[k] for p in planes(pivot, k, 9)]
        state = mat_mat(scaled, state)
        put(maps, k, state)
        return state

    first_map = [p * link[0] for p in planes(pivot, 0, 9)]
    put(maps, 0, first_map)
    ends = lax.fori_loop(1, K, lower_step, first_map)
    for c in range(9):
        end_map[c] = ends[c]

    @pl.when(jnp.logical_not(last))
    def _():
        link_copy.wait_recv()
        link[K] = jnp.where(cut == base + K, jnp.float32(0), link_next[...])

    def upper_step(step, state):
        k = K - 1 - step
        scaled = [p * link[k + 1] for p in planes(pivot, k, 9)]
        state = added(planes(maps, k, 9), mat_mat(scaled, state[:9])) + mat_mat(scaled, state[9:])
        put(maps, k, state)
        return state

    top_link = link[K]
    top_state = planes(maps, K - 1, 9) + [p * top_link for p in planes(pivot, K - 1, 9)]
    put(maps, K - 1, top_state)
    top_state = lax.fori_loop(1, K, upper_step, top_state)

    h_copy = to_norm(h_out, h_in, h_send, h_recv, place - 1)
    inside = jnp.logical_not(jnp.logical_or(first, last))

    def up_map(j):
        return to_norm(up_out.at[j], up_in.at[j], up_send.at[j], up_recv.at[j], place + 1)

    def down_map(j):
        return to_norm(down_out.at[j], down_in.at[j], down_send.at[j], down_recv.at[j], place - 1)

    def sends_up(j):
        return jnp.logical_and(place >= j, jnp.logical_not(last))

    def sends_down(j):
        return jnp.logical_and(N - 1 - place >= j, jnp.logical_not(first))

    @pl.when(last)
    def _():
        h_in[...] = jnp.zeros((9, R, W), jnp.float32)
        for c in range(9):
            h_out[c] = maps[0, c]
        h_copy.start()

    for j in range(1, min(2, N - 1)):

        @pl.when(sends_up(j))
        def _():
            put(up_out, j, [end_map[c] for c in range(9)])
            up_map(j).start()

        @pl.when(sends_down(j))
        def _():
            put(down_out, j, [maps[0, 9 + c] for c in range(9)])
            down_map(j).start()

    @pl.when(inside)
    def _():
        h_copy.wait_recv()
        inner = mat_mat([h_in[c] for c in range(9)], [end_map[c] for c in range(9)])
        whole = added(planes(maps, 0, 9), mat_mat([maps[0, 9 + c] for c in range(9)], inner))
        for c in range(9):
            h_out[c] = whole[c]
        h_copy.start()

    for j in range(2, N):

        @pl.when(place >= j)
        def _():
            up_map(j - 1).wait_recv()

        @pl.when(N - 1 - place >= j)
        def _():
            down_map(j - 1).wait_recv()

        if j < N - 1:

            @pl.when(sends_up(j))
            def _():
                put(up_out, j, mat_mat([end_map[c] for c in range(9)], planes(up_in, j - 1, 9)))
                up_map(j).start()

            @pl.when(sends_down(j))
            def _():
                put(
                    down_out, j,
                    mat_mat([maps[0, 9 + c] for c in range(9)], planes(down_in, j - 1, 9)),
                )
                down_map(j).start()

    total = [part[me, c] for c in range(4)]
    mask_up.wait_recv()
    mask_down.wait_recv()
    for hop in range(1, S):
        part_copy(hop).wait_recv()
        total = [total[c] + got[hop, c] for c in range(4)]
    mask = wall_mask[...].astype(jnp.float32)
    low_mask = mask_edge[0, R - 1 : R, :].astype(jnp.float32)
    high_mask = mask_edge[1, 0:1, :].astype(jnp.float32)
    row = lax.broadcasted_iota(jnp.int32, (R, W), 0)
    lane = lax.broadcasted_iota(jnp.int32, (R, W), 1)

    def around(x, low, high):
        nearby = jnp.where(row == 0, low, pltpu.roll(x, 1, 0))
        nearby += jnp.where(row == R - 1, high, pltpu.roll(x, R - 1, 0))
        nearby += jnp.where(lane == 0, jnp.float32(0), pltpu.roll(x, 1, 1))
        return nearby + jnp.where(lane == W - 1, jnp.float32(0), pltpu.roll(x, W - 1, 1))

    at_wall = jnp.where(first, jnp.float32(1), jnp.float32(0))
    for c in range(3):
        shift = total[c] * mask
        wall[c] = link[0] * shift * at_wall
        wall[3 + c] = around(
            shift, total[3][c : c + 1] * low_mask, total[3][3 + c : 4 + c] * high_mask
        )

    def edge_copies(sweep):
        return [
            to_surf(edge_out.at[sweep, 1], edge_in.at[sweep, 0], edge_send.at[sweep, 0], edge_recv.at[sweep, 0], after),
            to_surf(edge_out.at[sweep, 0], edge_in.at[sweep, 1], edge_send.at[sweep, 1], edge_recv.at[sweep, 1], before),
        ]

    def up_copy(sweep, j):
        return to_norm(
            f_out.at[sweep], f_in.at[sweep, j], f_send.at[sweep, j], f_recv.at[sweep, j], place + j
        )

    def down_copy(sweep, j):
        return to_norm(
            o_out.at[sweep], o_in.at[sweep, j], o_send.at[sweep, j], o_recv.at[sweep, j], place - j
        )

    for sweep in range(SWEEPS):
        if sweep > 0:
            for copy in edge_copies(sweep - 1):
                copy.wait_recv()
            for side in range(2):
                halo[side] = edge_in[sweep - 1, side].astype(jnp.float32)

        def source(k, sweep=sweep):
            if sweep == 0:
                blend = 1.0 - (base + k).astype(jnp.float32) / (K * N)
                factor = stiffness[k] * blend
                return [factor * wall[3 + c] for c in range(3)]
            return [
                stiffness[k]
                * around(out[k, c], halo[0, c, pl.ds(k, 1), :], halo[1, c, pl.ds(k, 1), :])
                for c in range(3)
            ]

        def forward(k, state):
            right = added(source(k), [link[k] * s for s in state])
            state = mat_vec(planes(pivot, k, 9), right)
            put(values, k, state)
            return state

        start = mat_vec(
            planes(pivot, 0, 9), added(source(0), [wall[c] for c in range(3)])
        )
        put(values, 0, start)
        ends = later(K, forward, start)

        def backward(step, state):
            k = K - 1 - step
            state = added(
                planes(values, k), mat_vec(planes(pivot, k, 9), [link[k + 1] * s for s in state])
            )
            put(values, k, state)
            return state

        tops = later(K, backward, ends)
        put(f_out, sweep, ends)
        for j in range(N - 1, 0, -1):

            @pl.when(place + j < N)
            def _():
                up_copy(sweep, j).start()

        if sweep == 0:

            @pl.when(first)
            def _():
                h_copy.wait_recv()

        @pl.when(jnp.logical_not(first))
        def _():
            top = added(
                tops,
                mat_vec(
                    [maps[0, 9 + c] for c in range(9)], mat_vec([h_in[c] for c in range(9)], ends)
                ),
            )
            put(o_out, sweep, top)
            for j in range(N - 1, 0, -1):

                @pl.when(place - j >= 0)
                def _():
                    down_copy(sweep, j).start()

        enter[...] = jnp.zeros(enter.shape, jnp.float32)
        for j in range(1, N):

            @pl.when(place - j >= 0)
            def _():
                up_copy(sweep, j).wait_recv()
                moved = planes(f_in.at[sweep], j)
                if j > 1:
                    moved = mat_vec(planes(up_in, j - 1, 9), moved)
                put(enter, 0, added(planes(enter, 0), moved))

            @pl.when(place + j < N)
            def _():
                down_copy(sweep, j).wait_recv()
                moved = planes(o_in.at[sweep], j)
                if j > 1:
                    moved = mat_vec(planes(down_in, j - 1, 9), moved)
                put(enter, 1, added(planes(enter, 1), moved))

        entering = planes(enter, 0)
        state = added(ends, mat_vec([end_map[c] for c in range(9)], entering))
        above = added(planes(enter, 1), mat_vec([h_in[c] for c in range(9)], state))

        def finish(k, carry, sweep=sweep):
            state = added(planes(values, k), mat_vec(planes(maps, k, 9), entering))
            state = added(state, mat_vec([maps[k, 9 + c] for c in range(9)], above))
            put(out, k, state)
            if sweep < SWEEPS - 1:
                for c in range(3):
                    halo[0, c, pl.ds(k, 1), :] = state[c][0:1]
                    halo[1, c, pl.ds(k, 1), :] = state[c][R - 1 : R]
            return carry

        loop(K, finish, 0, 4)
        if sweep < SWEEPS - 1:
            for side in range(2):
                edge_out[sweep, side] = halo[side].astype(jnp.bfloat16)
            for copy in edge_copies(sweep):
                copy.start()

    for hop in range(1, S):
        part_copy(hop).wait_send()
    mask_up.wait_send()
    mask_down.wait_send()
    for sweep in range(SWEEPS - 1):
        for copy in edge_copies(sweep):
            copy.wait_send()

    @pl.when(jnp.logical_not(first))
    def _():
        link_copy.wait_send()
        h_copy.wait_send()

    for j in range(1, N):
        if j < N - 1:

            @pl.when(sends_up(j))
            def _():
                up_map(j).wait_send()

            @pl.when(sends_down(j))
            def _():
                down_map(j).wait_send()

        for sweep in range(SWEEPS):

            @pl.when(place + j < N)
            def _():
                up_copy(sweep, j).wait_send()

            @pl.when(place - j >= 0)
            def _():
                down_copy(sweep, j).wait_send()


def per_device(
    surf_size, norm_size, mode_shapes, amplitude, mode_patch, column_patch, wall_mask, offsets,
    coupling, pivot_inv, stiffness,
):
    S, N = surf_size, norm_size
    modes = mode_shapes.transpose(0, 2, 1, 3)
    pivot = pivot_inv.transpose(0, 2, 1, 3)
    K, _, R, W = pivot.shape
    f32, bf16 = jnp.float32, jnp.bfloat16
    vmem = pl.BlockSpec(memory_space=pltpu.VMEM)
    smem = pl.BlockSpec(memory_space=pltpu.SMEM)
    hbm = pl.BlockSpec(memory_space=pl.ANY)
    dma = pltpu.SemaphoreType.DMA
    out = pl.pallas_call(
        functools.partial(kernel, surf_size, norm_size),
        out_shape=pltpu.VMEM((K, 3, R, W), f32),
        in_specs=[smem, smem, vmem, vmem, vmem, hbm, hbm, hbm, hbm],
        out_specs=vmem,
        scratch_shapes=[
            pltpu.VMEM(modes.shape, bf16),
            pltpu.VMEM((K, R, W), f32),
            pltpu.VMEM((K, 9, R, W), f32),
            pltpu.VMEM((K, R, W), f32),
            pltpu.VMEM((K + 1, R, W), f32),
            pltpu.VMEM((R, W), f32),
            pltpu.VMEM((K, 18, R, W), f32),
            pltpu.VMEM((9, R, W), f32),
            pltpu.VMEM((S, 4, R, W), f32),
            pltpu.VMEM((S, 4, R, W), f32),
            pltpu.VMEM((2, R, W), jnp.int32),
            pltpu.VMEM((6, R, W), f32),
            pltpu.VMEM((K, 3, R, W), f32),
            pltpu.VMEM((2, 3, R, W), f32),
            pltpu.VMEM((SWEEPS - 1, 2, 3, K, W), bf16),
            pltpu.VMEM((SWEEPS - 1, 2, 3, K, W), bf16),
            pltpu.VMEM((2, 3, K, W), f32),
            pltpu.VMEM((SWEEPS, N, 3, R, W), f32),
            pltpu.VMEM((SWEEPS, 3, R, W), f32),
            pltpu.VMEM((SWEEPS, N, 3, R, W), f32),
            pltpu.VMEM((SWEEPS, 3, R, W), f32),
            pltpu.VMEM((9, R, W), f32),
            pltpu.VMEM((9, R, W), f32),
            pltpu.VMEM((N, 9, R, W), f32),
            pltpu.VMEM((N, 9, R, W), f32),
            pltpu.VMEM((N, 9, R, W), f32),
            pltpu.VMEM((N, 9, R, W), f32),
            dma((3 + modes.shape[2] // (2 * R),)),
            dma((S,)),
            dma((S,)),
            dma((2,)),
            dma((2,)),
            dma,
            dma,
            dma,
            dma,
            dma((N,)),
            dma((N,)),
            dma((N,)),
            dma((N,)),
            dma((SWEEPS, N)),
            dma((SWEEPS, N)),
            dma((SWEEPS, N)),
            dma((SWEEPS, N)),
            dma((SWEEPS - 1, 2)),
            dma((SWEEPS - 1, 2)),
        ],
        compiler_params=pltpu.CompilerParams(collective_id=0, has_side_effects=True),
        name="line_sweeps",
    )(amplitude, mode_patch, column_patch, wall_mask, offsets, modes, coupling, pivot, stiffness)
    return out.transpose(0, 2, 1, 3)


def solution(mesh):
    return jax.shard_map(
        functools.partial(per_device, mesh.shape["surf"], mesh.shape["norm"]),
        mesh=mesh,
        in_specs=(
            P("surf", None, None, None),
            P(),
            P(),
            P(),
            P("surf", None),
            P("surf", None),
            P("norm", "surf", None),
            P("norm", "surf", None, None),
            P("norm", "surf", None),
        ),
        out_specs=P("norm", "surf", None, None),
        check_vma=False,
    )
```

```python
import functools
import types

import jax
import jax.numpy as jnp
from jax import lax
from jax.experimental import pallas as pl
from jax.experimental.pallas import tpu as pltpu
from jax.sharding import PartitionSpec as P

SWEEPS = 3
LANES = 128
MESH = pl.DeviceIdType.MESH


def loop(count, body, init, unroll=4):
    if count % unroll:
        unroll = 1

    def outer(step, carry):
        for part in range(unroll):
            carry = body(step * unroll + part, carry)
        return carry

    return lax.fori_loop(0, count // unroll, outer, init)


def later(count, body, init, unroll=5):
    return loop(count - 1, lambda step, carry: body(step + 1, carry), init, unroll)


def mat_vec(matrix, vector):
    return [
        matrix[3 * a] * vector[0] + matrix[3 * a + 1] * vector[1] + matrix[3 * a + 2] * vector[2]
        for a in range(3)
    ]


def mat_mat(left, right):
    return [
        left[3 * a] * right[b] + left[3 * a + 1] * right[3 + b] + left[3 * a + 2] * right[6 + b]
        for a in range(3)
        for b in range(3)
    ]


def added(left, right):
    return [a + b for a, b in zip(left, right)]


def planes(ref, index, count=3):
    return [ref[index, c] for c in range(count)]


def whole(ref, count=9):
    return [ref[c] for c in range(count)]


def rows(ref, count=3):
    return [ref[c : c + 1, :] for c in range(count)]


def put(ref, index, values):
    for c, value in enumerate(values):
        ref[index, c] = value


def put_rows(ref, values):
    for c, value in enumerate(values):
        ref[c : c + 1, :] = value


def kernel(
    surf_size, norm_size, names,
    amplitude, mode_patch, column_patch, wall_mask, offsets,
    modes_hbm, coupling_hbm, pivot_hbm, stiffness_hbm,
    out, *scratch,
):
    s = types.SimpleNamespace(**dict(zip(names, scratch)))
    modes, coupling, pivot, stiffness = s.modes, s.coupling, s.pivot, s.stiffness
    link, maps, part, got, wall, values, halo = s.link, s.maps, s.part, s.got, s.wall, s.values, s.halo
    S, N = surf_size, norm_size
    K, _, R, W = pivot.shape
    M = modes.shape[0]
    B = 2 * R
    blocks = modes.shape[2] // B
    chunks = W // LANES
    me = lax.axis_index("surf")
    place = lax.axis_index("norm")
    before = lax.rem(me + S - 1, S)
    after = lax.rem(me + 1, S)
    first, last = place == 0, place == N - 1
    inside = jnp.logical_not(jnp.logical_or(first, last))
    base = place * K

    def to(src, dst, send, recv, **target):
        return pltpu.make_async_remote_copy(
            src_ref=src, dst_ref=dst, send_sem=send, recv_sem=recv,
            device_id=target, device_id_type=MESH,
        )

    def toward(side):
        return after if side == 0 else before

    mode_loads = [
        pltpu.make_async_copy(
            modes_hbm.at[:, :, pl.ds(b * B, B), :], modes.at[:, :, pl.ds(b * B, B), :], s.load_sem.at[3 + b]
        )
        for b in range(blocks)
    ]
    loads = [
        pltpu.make_async_copy(coupling_hbm, coupling, s.load_sem.at[0]),
        pltpu.make_async_copy(pivot_hbm, pivot, s.load_sem.at[1]),
        pltpu.make_async_copy(stiffness_hbm, stiffness, s.load_sem.at[2]),
    ]
    for copy in loads + mode_loads:
        copy.start()

    barrier = pltpu.get_barrier_semaphore()

    def greet(**target):
        pl.semaphore_signal(barrier, inc=1, device_id=target, device_id_type=MESH)

    for hop in range(1, S):
        greet(surf=lax.rem(me + hop, S))
    for hop in range(1, N):
        other = lax.rem(place + hop, N)
        greet(norm=other)
        greet(surf=before, norm=other)
        greet(surf=after, norm=other)

    for copy in loads:
        copy.wait()
    cut = offsets[...]

    def link_step(k, carry):
        link[k] = jnp.where(cut == base + k, jnp.float32(0), coupling[k])
        return carry

    loop(K, link_step, 0)

    def lower_step(k, state):
        scaled = [p * link[k] for p in planes(pivot, k, 9)]
        state = mat_mat(scaled, state)
        put(maps, k, state)
        return state

    first_map = [p * link[0] for p in planes(pivot, 0, 9)]
    put(maps, 0, first_map)
    ends = lax.fori_loop(1, K, lower_step, first_map)
    for c in range(9):
        s.end_map[c] = ends[c]

    def upper_step(step, state):
        k = K - 1 - step
        scaled = [p * link[k + 1] for p in planes(pivot, k, 9)]
        state = added(planes(maps, k, 9), mat_mat(scaled, state[:9])) + mat_mat(scaled, state[9:])
        put(maps, k, state)
        return state

    top_state = ends + planes(pivot, K - 1, 9)
    put(maps, K - 1, top_state)
    top_state = lax.fori_loop(1, K, upper_step, top_state)
    for c in range(18):
        s.top_map[c] = link[0] * top_state[c]

    own_mode = me * M
    for b in range(blocks):
        mode_loads[b].wait()
        patch = column_patch[b * B : (b + 1) * B, :]

        def mode_step(m, sums):
            weight = jnp.where(
                patch == mode_patch[own_mode + m], amplitude[own_mode + m], jnp.float32(0)
            )
            return [
                sums[c] + weight * modes[m, c, b * B : (b + 1) * B, :].astype(jnp.float32)
                for c in range(3)
            ]

        sums = loop(M, mode_step, [jnp.zeros((B, W), jnp.float32)] * 3)
        for c in range(3):
            for side in range(2):
                dest = 2 * b + side
                block = sums[c][side * R : (side + 1) * R]
                part[dest, c] = block
                part[(dest + 1) % S, 3, c : c + 1, :] = block[R - 1 : R]
                part[(dest - 1) % S, 3, 3 + c : 4 + c, :] = block[0:1]

    pl.semaphore_wait(barrier, S - 1 + 3 * (N - 1))

    def h_copy(q):
        return to(s.h_out.at[q], s.h_in.at[q], s.h_send.at[q], s.h_recv.at[q], norm=place - 1)

    def chunk(ref, q, start=0):
        return [ref[start + c, :, q * LANES : (q + 1) * LANES] for c in range(9)]

    def h_full():
        return [jnp.concatenate([s.h_in[q, c] for q in range(chunks)], axis=1) for c in range(9)]

    def row_copy(slot, side, step):
        return to(
            s.row_out.at[slot, side], s.row_in.at[slot, side],
            s.row_send.at[slot, side], s.row_recv.at[slot, side],
            surf=toward(side), norm=place + step,
        )

    def send_rows(slot, step, values9):
        put_rows(s.row_out.at[slot, 0], [v[R - 1 : R] for v in values9])
        put_rows(s.row_out.at[slot, 1], [v[0:1] for v in values9])
        for side in range(2):
            row_copy(slot, side, step).start()

    UP, DOWN, ENDS, TOP = 0, N, 0, N

    def up_map(j):
        return to(s.up_out.at[j], s.up_in.at[j], s.up_send.at[j], s.up_recv.at[j], norm=place + 1)

    def down_map(j):
        return to(s.down_out.at[j], s.down_in.at[j], s.down_send.at[j], s.down_recv.at[j], norm=place - 1)

    def sends_up(j):
        return jnp.logical_and(place >= j, jnp.logical_not(last))

    def sends_down(j):
        return jnp.logical_and(N - 1 - place >= j, jnp.logical_not(first))

    @pl.when(last)
    def _():
        s.h_in[...] = jnp.zeros(s.h_in.shape, jnp.float32)
        s.row_in[TOP] = jnp.zeros(s.row_in.shape[1:], jnp.float32)
        for q in range(chunks):
            put(s.h_out, q, chunk(s.top_map, q))
            h_copy(q).start()

    def part_copy(hop):
        dest = lax.rem(me + hop, S)
        return to(part.at[dest], got.at[hop], s.part_send.at[hop], s.part_recv.at[hop], surf=dest)

    for hop in range(1, S):
        part_copy(hop).start()
    mask_up = to(wall_mask, s.mask_edge.at[0], s.mask_send.at[0], s.mask_recv.at[0], surf=after)
    mask_down = to(wall_mask, s.mask_edge.at[1], s.mask_send.at[1], s.mask_recv.at[1], surf=before)
    mask_up.start()
    mask_down.start()

    for j in range(1, min(2, N - 1)):

        @pl.when(sends_up(j))
        def _():
            value = whole(s.end_map)
            put(s.up_out, j, value)
            up_map(j).start()
            send_rows(UP + j, 1, value)

        @pl.when(sends_down(j))
        def _():
            value = [s.top_map[9 + c] for c in range(9)]
            put(s.down_out, j, value)
            down_map(j).start()
            send_rows(DOWN + j, -1, value)

    @pl.when(last)
    def _():
        send_rows(TOP, -1, whole(s.top_map))

    send_rows(ENDS, 0, whole(s.end_map))

    def pack_step(k, carry):
        for c in range(18):
            value = maps[k, c]
            s.side_rows[0, c, pl.ds(k, 1), :] = value[R - 1 : R]
            s.side_rows[1, c, pl.ds(k, 1), :] = value[0:1]
        return carry

    loop(K, pack_step, 0, 2)

    def side_map_copy(side):
        return to(
            s.side_out.at[side], s.side_in.at[side], s.side_send.at[side], s.side_recv.at[side],
            surf=toward(side),
        )

    for side in range(2):
        for c in range(18):
            s.side_out[side, c] = s.side_rows[side, c].astype(jnp.bfloat16)
        side_map_copy(side).start()

    def relay():
        for q in range(chunks):
            h_copy(q).wait_recv()
            inner = mat_mat(whole(s.h_in.at[q]), chunk(s.end_map, q))
            value = added(chunk(s.top_map, q), mat_mat(chunk(s.top_map, q, 9), inner))
            put(s.h_out, q, value)
            h_copy(q).start()
            for c in range(9):
                s.row_out[TOP, 0, c : c + 1, q * LANES : (q + 1) * LANES] = value[c][R - 1 : R]
                s.row_out[TOP, 1, c : c + 1, q * LANES : (q + 1) * LANES] = value[c][0:1]
        for side in range(2):
            row_copy(TOP, side, -1).start()

    early = jnp.logical_and(inside, place == N - 2)

    @pl.when(early)
    def _():
        relay()

    for j in range(2, N - 1):

        @pl.when(sends_up(j))
        def _():
            up_map(j - 1).wait_recv()
            value = mat_mat(whole(s.end_map), planes(s.up_in, j - 1, 9))
            put(s.up_out, j, value)
            up_map(j).start()
            send_rows(UP + j, 1, value)

        @pl.when(sends_down(j))
        def _():
            down_map(j - 1).wait_recv()
            value = mat_mat([s.top_map[9 + c] for c in range(9)], planes(s.down_in, j - 1, 9))
            put(s.down_out, j, value)
            down_map(j).start()
            send_rows(DOWN + j, -1, value)

    total = [part[me, c] for c in range(4)]
    mask_up.wait_recv()
    mask_down.wait_recv()
    for hop in range(1, S):
        part_copy(hop).wait_recv()
        total = [total[c] + got[hop, c] for c in range(4)]
    mask = wall_mask[...].astype(jnp.float32)
    low_mask = s.mask_edge[0, R - 1 : R, :].astype(jnp.float32)
    high_mask = s.mask_edge[1, 0:1, :].astype(jnp.float32)
    row = lax.broadcasted_iota(jnp.int32, (R, W), 0)
    lane = lax.broadcasted_iota(jnp.int32, (R, W), 1)

    def around(x, low, high):
        nearby = jnp.where(row == 0, low, pltpu.roll(x, 1, 0))
        nearby += jnp.where(row == R - 1, high, pltpu.roll(x, R - 1, 0))
        nearby += jnp.where(lane == 0, jnp.float32(0), pltpu.roll(x, 1, 1))
        return nearby + jnp.where(lane == W - 1, jnp.float32(0), pltpu.roll(x, W - 1, 1))

    at_wall = jnp.where(first, jnp.float32(1), jnp.float32(0))
    for c in range(3):
        shift = total[c] * mask
        wall[c] = link[0] * shift * at_wall
        wall[3 + c] = around(
            shift, total[3][c : c + 1] * low_mask, total[3][3 + c : 4 + c] * high_mask
        )

    def edge_copy(sweep, side):
        return to(
            s.edge_out.at[sweep, side], s.edge_in.at[sweep, side],
            s.edge_send.at[sweep, side], s.edge_recv.at[sweep, side], surf=toward(side),
        )

    def up_copy(sweep, j):
        return to(
            s.f_out.at[sweep], s.f_in.at[sweep, j], s.f_send.at[sweep, j], s.f_recv.at[sweep, j],
            norm=place + j,
        )

    def down_copy(sweep, j):
        return to(
            s.o_out.at[sweep], s.o_in.at[sweep, j], s.o_send.at[sweep, j], s.o_recv.at[sweep, j],
            norm=place - j,
        )

    def up_edge(sweep, side, j):
        return to(
            s.fe_out.at[sweep, side], s.fe_in.at[sweep, side, j],
            s.fe_send.at[sweep, side, j], s.fe_recv.at[sweep, side, j],
            surf=toward(side), norm=place + j,
        )

    def down_edge(sweep, side, j):
        return to(
            s.oe_out.at[sweep, side], s.oe_in.at[sweep, side, j],
            s.oe_send.at[sweep, side, j], s.oe_recv.at[sweep, side, j],
            surf=toward(side), norm=place - j,
        )

    for sweep in range(SWEEPS):
        shared = sweep < SWEEPS - 1

        def source(k, sweep=sweep):
            if sweep == 0:
                blend = 1.0 - (base + k).astype(jnp.float32) / (K * N)
                factor = stiffness[k] * blend
                return [factor * wall[3 + c] for c in range(3)]
            return [
                stiffness[k]
                * around(out[k, c], halo[0, c, pl.ds(k, 1), :], halo[1, c, pl.ds(k, 1), :])
                for c in range(3)
            ]

        def forward(k, state):
            right = added(source(k), [link[k] * v for v in state])
            state = mat_vec(planes(pivot, k, 9), right)
            put(values, k, state)
            return state

        start = mat_vec(
            planes(pivot, 0, 9), added(source(0), [wall[c] for c in range(3)])
        )
        put(values, 0, start)
        ends = later(K, forward, start)
        put(s.f_out, sweep, ends)
        for j in range(N - 1, 0, -1):

            @pl.when(place + j < N)
            def _():
                up_copy(sweep, j).start()

        if shared:
            put_rows(s.fe_out.at[sweep, 0], [v[R - 1 : R] for v in ends])
            put_rows(s.fe_out.at[sweep, 1], [v[0:1] for v in ends])
            for j in range(N - 1, -1, -1):

                @pl.when(place + j < N)
                def _():
                    for side in range(2):
                        up_edge(sweep, side, j).start()

        def keep(k, state):
            put(values, k, state)
            if shared:
                for c in range(3):
                    halo[0, c, pl.ds(k, 1), :] = state[c][R - 1 : R]
                    halo[1, c, pl.ds(k, 1), :] = state[c][0:1]

        def backward(step, state):
            k = K - 1 - step
            state = added(
                planes(values, k), mat_vec(planes(pivot, k, 9), [link[k + 1] * v for v in state])
            )
            keep(k, state)
            return state

        keep(K - 1, ends)
        tops = later(K, backward, ends)

        if sweep == 0:

            @pl.when(jnp.logical_and(inside, jnp.logical_not(early)))
            def _():
                relay()

        @pl.when(jnp.logical_not(first))
        def _():
            top = added(
                [link[0] * v for v in tops],
                mat_vec([s.top_map[9 + c] for c in range(9)], mat_vec(h_full(), ends)),
            )
            put(s.o_out, sweep, top)
            for j in range(N - 1, 0, -1):

                @pl.when(place - j >= 0)
                def _():
                    down_copy(sweep, j).start()

            if shared:
                put_rows(s.oe_out.at[sweep, 0], [v[R - 1 : R] for v in top])
                put_rows(s.oe_out.at[sweep, 1], [v[0:1] for v in top])
                for j in range(N - 1, 0, -1):

                    @pl.when(place - j >= 0)
                    def _():
                        for side in range(2):
                            down_edge(sweep, side, j).start()

        if shared:
            for side in range(2):
                s.edge_out[sweep, side] = halo[side].astype(jnp.bfloat16)
                edge_copy(sweep, side).start()

        s.enter[...] = jnp.zeros(s.enter.shape, jnp.float32)
        for j in range(1, N):
            if sweep == 0 and j > 1:

                @pl.when(jnp.logical_and(last, place >= j))
                def _():
                    up_map(j - 1).wait_recv()

                @pl.when(jnp.logical_and(first, N - 1 - place >= j))
                def _():
                    down_map(j - 1).wait_recv()

            @pl.when(place - j >= 0)
            def _():
                up_copy(sweep, j).wait_recv()
                moved = planes(s.f_in.at[sweep], j)
                if j > 1:
                    moved = mat_vec(planes(s.up_in, j - 1, 9), moved)
                put(s.enter, 0, added(planes(s.enter, 0), moved))

            @pl.when(place + j < N)
            def _():
                down_copy(sweep, j).wait_recv()
                moved = planes(s.o_in.at[sweep], j)
                if j > 1:
                    moved = mat_vec(planes(s.down_in, j - 1, 9), moved)
                put(s.enter, 1, added(planes(s.enter, 1), moved))

        if sweep == 0:

            @pl.when(first)
            def _():
                for q in range(chunks):
                    h_copy(q).wait_recv()

        entering = planes(s.enter, 0)
        state = added(ends, mat_vec(whole(s.end_map), entering))
        above = added(planes(s.enter, 1), mat_vec(h_full(), state))

        def finish(k, carry):
            state = added(planes(values, k), mat_vec(planes(maps, k, 9), entering))
            state = added(state, mat_vec([maps[k, 9 + c] for c in range(9)], above))
            put(out, k, state)
            return carry

        loop(K, finish, 0, 4)

        if shared:
            if sweep == 0:
                for side in range(2):
                    side_map_copy(side).wait_recv()
                    row_copy(ENDS, side, 0).wait_recv()

                @pl.when(jnp.logical_not(last))
                def _():
                    for side in range(2):
                        row_copy(TOP, side, 0).wait_recv()

                for j in range(2, N):

                    @pl.when(place >= j)
                    def _():
                        for side in range(2):
                            row_copy(UP + j - 1, side, 0).wait_recv()

                    @pl.when(N - 1 - place >= j)
                    def _():
                        for side in range(2):
                            row_copy(DOWN + j - 1, side, 0).wait_recv()

            s.enter_row[...] = jnp.zeros(s.enter_row.shape, jnp.float32)
            for j in range(1, N):

                @pl.when(place - j >= 0)
                def _():
                    for side in range(2):
                        up_edge(sweep, side, j).wait_recv()
                        moved = rows(s.fe_in.at[sweep, side, j])
                        if j > 1:
                            moved = mat_vec(rows(s.row_in.at[UP + j - 1, side], 9), moved)
                        put_rows(s.enter_row.at[side, 0], added(rows(s.enter_row.at[side, 0]), moved))

                @pl.when(place + j < N)
                def _():
                    for side in range(2):
                        down_edge(sweep, side, j).wait_recv()
                        moved = rows(s.oe_in.at[sweep, side, j])
                        if j > 1:
                            moved = mat_vec(rows(s.row_in.at[DOWN + j - 1, side], 9), moved)
                        put_rows(s.enter_row.at[side, 1], added(rows(s.enter_row.at[side, 1]), moved))

            for side in range(2):
                up_edge(sweep, side, 0).wait_recv()
                edge_copy(sweep, side).wait_recv()
                entered = rows(s.enter_row.at[side, 0])
                state = added(
                    rows(s.fe_in.at[sweep, side, 0]),
                    mat_vec(rows(s.row_in.at[ENDS, side], 9), entered),
                )
                higher = added(
                    rows(s.enter_row.at[side, 1]), mat_vec(rows(s.row_in.at[TOP, side], 9), state)
                )
                for c in range(3):
                    value = s.edge_in[sweep, side, c].astype(jnp.float32)
                    for b in range(3):
                        value += s.side_in[side, 3 * c + b].astype(jnp.float32) * entered[b]
                        value += s.side_in[side, 9 + 3 * c + b].astype(jnp.float32) * higher[b]
                    halo[side, c] = value

    for hop in range(1, S):
        part_copy(hop).wait_send()
    mask_up.wait_send()
    mask_down.wait_send()
    for side in range(2):
        side_map_copy(side).wait_send()
        row_copy(ENDS, side, 0).wait_send()
        for sweep in range(SWEEPS - 1):
            edge_copy(sweep, side).wait_send()

    @pl.when(jnp.logical_not(first))
    def _():
        for q in range(chunks):
            h_copy(q).wait_send()
        for side in range(2):
            row_copy(TOP, side, 0).wait_send()

    for j in range(1, N - 1):

        @pl.when(sends_up(j))
        def _():
            up_map(j).wait_send()
            for side in range(2):
                row_copy(UP + j, side, 0).wait_send()

        @pl.when(sends_down(j))
        def _():
            down_map(j).wait_send()
            for side in range(2):
                row_copy(DOWN + j, side, 0).wait_send()

    for j in range(N):

        @pl.when(place + j < N)
        def _():
            for sweep in range(SWEEPS):
                if j > 0:
                    up_copy(sweep, j).wait_send()
                if sweep < SWEEPS - 1:
                    for side in range(2):
                        up_edge(sweep, side, j).wait_send()

        if j > 0:

            @pl.when(place - j >= 0)
            def _():
                for sweep in range(SWEEPS):
                    down_copy(sweep, j).wait_send()
                    if sweep < SWEEPS - 1:
                        for side in range(2):
                            down_edge(sweep, side, j).wait_send()


def per_device(
    surf_size, norm_size, mode_shapes, amplitude, mode_patch, column_patch, wall_mask, offsets,
    coupling, pivot_inv, stiffness,
):
    S, N = surf_size, norm_size
    modes = mode_shapes.transpose(0, 2, 1, 3)
    pivot = pivot_inv.transpose(0, 2, 1, 3)
    K, _, R, W = pivot.shape
    C = W // LANES
    f32, bf16 = jnp.float32, jnp.bfloat16
    vmem = pl.BlockSpec(memory_space=pltpu.VMEM)
    smem = pl.BlockSpec(memory_space=pltpu.SMEM)
    hbm = pl.BlockSpec(memory_space=pltpu.HBM)
    dma = pltpu.SemaphoreType.DMA

    def room(*shape):
        return pltpu.VMEM(shape, f32)

    def half(*shape):
        return pltpu.VMEM(shape, bf16)

    G = SWEEPS - 1
    scratch = dict(
        modes=half(*modes.shape),
        coupling=room(K, R, W),
        pivot=room(K, 9, R, W),
        stiffness=room(K, R, W),
        link=room(K, R, W),
        maps=room(K, 18, R, W),
        end_map=room(9, R, W),
        top_map=room(18, R, W),
        part=room(S, 4, R, W),
        got=room(S, 4, R, W),
        mask_edge=pltpu.VMEM((2, R, W), jnp.int32),
        wall=room(6, R, W),
        values=room(K, 3, R, W),
        enter=room(2, 3, R, W),
        enter_row=room(2, 2, 3, W),
        halo=room(2, 3, K, W),
        edge_out=half(G, 2, 3, K, W),
        edge_in=half(G, 2, 3, K, W),
        side_rows=room(2, 18, K, W),
        side_out=half(2, 18, K, W),
        side_in=half(2, 18, K, W),
        row_out=room(2 * N, 2, 9, W),
        row_in=room(2 * N, 2, 9, W),
        f_in=room(SWEEPS, N, 3, R, W),
        f_out=room(SWEEPS, 3, R, W),
        o_in=room(SWEEPS, N, 3, R, W),
        o_out=room(SWEEPS, 3, R, W),
        fe_in=room(G, 2, N, 3, W),
        fe_out=room(G, 2, 3, W),
        oe_in=room(G, 2, N, 3, W),
        oe_out=room(G, 2, 3, W),
        h_in=room(C, 9, R, LANES),
        h_out=room(C, 9, R, LANES),
        up_in=room(N, 9, R, W),
        up_out=room(N, 9, R, W),
        down_in=room(N, 9, R, W),
        down_out=room(N, 9, R, W),
        load_sem=dma((3 + modes.shape[2] // (2 * R),)),
    )
    sems = dict(
        part=(S,), mask=(2,), h=(C,), row=(2 * N, 2), side=(2,), up=(N,), down=(N,),
        f=(SWEEPS, N), o=(SWEEPS, N), fe=(G, 2, N), oe=(G, 2, N), edge=(G, 2),
    )
    for name, shape in sems.items():
        scratch[name + "_send"] = dma(shape)
        scratch[name + "_recv"] = dma(shape)
    out = pl.pallas_call(
        functools.partial(kernel, S, N, tuple(scratch)),
        out_shape=pltpu.VMEM((K, 3, R, W), f32),
        in_specs=[smem, smem, vmem, vmem, vmem, hbm, hbm, hbm, hbm],
        out_specs=vmem,
        scratch_shapes=list(scratch.values()),
        compiler_params=pltpu.CompilerParams(
            collective_id=0, has_side_effects=True, vmem_limit_bytes=62 * 1024 * 1024
        ),
        name="line_sweeps",
    )(amplitude, mode_patch, column_patch, wall_mask, offsets, modes, coupling, pivot, stiffness)
    return out.transpose(0, 2, 1, 3)


def solution(mesh):
    return jax.shard_map(
        functools.partial(per_device, mesh.shape["surf"], mesh.shape["norm"]),
        mesh=mesh,
        in_specs=(
            P("surf", None, None, None),
            P(),
            P(),
            P(),
            P("surf", None),
            P("surf", None),
            P("norm", "surf", None),
            P("norm", "surf", None, None),
            P("norm", "surf", None),
        ),
        out_specs=P("norm", "surf", None, None),
        check_vma=False,
    )
```

```python
import functools
import types

import jax
import jax.numpy as jnp
from jax import lax
from jax.experimental import pallas as pl
from jax.experimental.pallas import tpu as pltpu
from jax.sharding import PartitionSpec as P

SWEEPS = 3
LANES = 128
MESH = pl.DeviceIdType.MESH


def loop(count, body, init, unroll=4):
    if count % unroll:
        unroll = 1

    def outer(step, carry):
        for part in range(unroll):
            carry = body(step * unroll + part, carry)
        return carry

    return lax.fori_loop(0, count // unroll, outer, init)


def later(count, body, init, unroll=5):
    return loop(count - 1, lambda step, carry: body(step + 1, carry), init, unroll)


def mat_vec(matrix, vector):
    return [
        matrix[3 * a] * vector[0] + matrix[3 * a + 1] * vector[1] + matrix[3 * a + 2] * vector[2]
        for a in range(3)
    ]


def mat_mat(left, right):
    return [
        left[3 * a] * right[b] + left[3 * a + 1] * right[3 + b] + left[3 * a + 2] * right[6 + b]
        for a in range(3)
        for b in range(3)
    ]


def added(left, right):
    return [a + b for a, b in zip(left, right)]


def planes(ref, index, count=3):
    return [ref[index, c] for c in range(count)]


def whole(ref, count=9):
    return [ref[c] for c in range(count)]


def rows(ref, count=3):
    return [ref[c : c + 1, :] for c in range(count)]


def put(ref, index, values):
    for c, value in enumerate(values):
        ref[index, c] = value


def put_rows(ref, values):
    for c, value in enumerate(values):
        ref[c : c + 1, :] = value


def kernel(
    surf_size, norm_size, names,
    amplitude, mode_patch, column_patch, wall_mask, offsets,
    modes_hbm, coupling_hbm, pivot_hbm, stiffness_hbm,
    out, *scratch,
):
    s = types.SimpleNamespace(**dict(zip(names, scratch)))
    modes, coupling, pivot, stiffness = s.modes, s.coupling, s.pivot, s.stiffness
    link, maps, part, got, wall, values, halo = s.link, s.maps, s.part, s.got, s.wall, s.values, s.halo
    S, N = surf_size, norm_size
    K, _, R, W = pivot.shape
    M = modes.shape[0]
    B = 2 * R
    blocks = modes.shape[2] // B
    chunks = W // LANES
    me = lax.axis_index("surf")
    place = lax.axis_index("norm")
    before = lax.rem(me + S - 1, S)
    after = lax.rem(me + 1, S)
    first, last = place == 0, place == N - 1
    inside = jnp.logical_not(jnp.logical_or(first, last))
    base = place * K

    def to(src, dst, send, recv, **target):
        return pltpu.make_async_remote_copy(
            src_ref=src, dst_ref=dst, send_sem=send, recv_sem=recv,
            device_id=target, device_id_type=MESH,
        )

    def toward(side):
        return after if side == 0 else before

    mode_loads = [
        pltpu.make_async_copy(
            modes_hbm.at[:, :, pl.ds(b * B, B), :], modes.at[:, :, pl.ds(b * B, B), :], s.load_sem.at[3 + b]
        )
        for b in range(blocks)
    ]
    loads = [
        pltpu.make_async_copy(coupling_hbm, coupling, s.load_sem.at[0]),
        pltpu.make_async_copy(pivot_hbm, pivot, s.load_sem.at[1]),
        pltpu.make_async_copy(stiffness_hbm, stiffness, s.load_sem.at[2]),
    ]
    for copy in loads + mode_loads:
        copy.start()

    barrier = pltpu.get_barrier_semaphore()

    def greet(**target):
        pl.semaphore_signal(barrier, inc=1, device_id=target, device_id_type=MESH)

    for hop in range(1, S):
        greet(surf=lax.rem(me + hop, S))
    for hop in range(1, N):
        other = lax.rem(place + hop, N)
        greet(norm=other)
        greet(surf=before, norm=other)
        greet(surf=after, norm=other)

    for copy in loads:
        copy.wait()
    cut = offsets[...]

    def link_step(k, carry):
        link[k] = jnp.where(cut == base + k, jnp.float32(0), coupling[k])
        return carry

    loop(K, link_step, 0)

    def lower_step(k, state):
        scaled = [p * link[k] for p in planes(pivot, k, 9)]
        state = mat_mat(scaled, state)
        put(maps, k, state)
        return state

    first_map = [p * link[0] for p in planes(pivot, 0, 9)]
    put(maps, 0, first_map)
    ends = lax.fori_loop(1, K, lower_step, first_map)
    for c in range(9):
        s.end_map[c] = ends[c]

    def upper_step(step, state):
        k = K - 1 - step
        scaled = [p * link[k + 1] for p in planes(pivot, k, 9)]
        state = added(planes(maps, k, 9), mat_mat(scaled, state[:9])) + mat_mat(scaled, state[9:])
        put(maps, k, state)
        return state

    top_state = ends + planes(pivot, K - 1, 9)
    put(maps, K - 1, top_state)
    top_state = lax.fori_loop(1, K, upper_step, top_state)
    for c in range(18):
        s.top_map[c] = link[0] * top_state[c]

    own_mode = me * M
    for b in range(blocks):
        mode_loads[b].wait()
        patch = column_patch[b * B : (b + 1) * B, :]

        def mode_step(m, sums):
            weight = jnp.where(
                patch == mode_patch[own_mode + m], amplitude[own_mode + m], jnp.float32(0)
            )
            return [
                sums[c] + weight * modes[m, c, b * B : (b + 1) * B, :].astype(jnp.float32)
                for c in range(3)
            ]

        sums = loop(M, mode_step, [jnp.zeros((B, W), jnp.float32)] * 3)
        for c in range(3):
            for side in range(2):
                dest = 2 * b + side
                block = sums[c][side * R : (side + 1) * R]
                part[dest, c] = block
                part[(dest + 1) % S, 3, c : c + 1, :] = block[R - 1 : R]
                part[(dest - 1) % S, 3, 3 + c : 4 + c, :] = block[0:1]

    pl.semaphore_wait(barrier, S - 1 + 3 * (N - 1))

    def h_copy(q):
        return to(s.h_out.at[q], s.h_in.at[q], s.h_send.at[q], s.h_recv.at[q], norm=place - 1)

    def chunk(ref, q, start=0):
        return [ref[start + c, :, q * LANES : (q + 1) * LANES] for c in range(9)]

    def h_full():
        return [jnp.concatenate([s.h_in[q, c] for q in range(chunks)], axis=1) for c in range(9)]

    def row_copy(slot, side, step):
        return to(
            s.row_out.at[slot, side], s.row_in.at[slot, side],
            s.row_send.at[slot, side], s.row_recv.at[slot, side],
            surf=toward(side), norm=place + step,
        )

    def send_rows(slot, step, values9):
        put_rows(s.row_out.at[slot, 0], [v[R - 1 : R] for v in values9])
        put_rows(s.row_out.at[slot, 1], [v[0:1] for v in values9])
        for side in range(2):
            row_copy(slot, side, step).start()

    UP, DOWN, ENDS, TOP = 0, N, 0, N

    def up_map(j):
        return to(s.up_out.at[j], s.up_in.at[j], s.up_send.at[j], s.up_recv.at[j], norm=place + 1)

    def down_map(j):
        return to(s.down_out.at[j], s.down_in.at[j], s.down_send.at[j], s.down_recv.at[j], norm=place - 1)

    def sends_up(j):
        return jnp.logical_and(place >= j, jnp.logical_not(last))

    def sends_down(j):
        return jnp.logical_and(N - 1 - place >= j, jnp.logical_not(first))

    @pl.when(last)
    def _():
        s.h_in[...] = jnp.zeros(s.h_in.shape, jnp.float32)
        s.row_in[TOP] = jnp.zeros(s.row_in.shape[1:], jnp.float32)
        for q in range(chunks):
            put(s.h_out, q, chunk(s.top_map, q))
            h_copy(q).start()

    def part_copy(hop):
        dest = lax.rem(me + hop, S)
        return to(part.at[dest], got.at[hop], s.part_send.at[hop], s.part_recv.at[hop], surf=dest)

    for hop in range(1, S):
        part_copy(hop).start()
    mask_up = to(wall_mask, s.mask_edge.at[0], s.mask_send.at[0], s.mask_recv.at[0], surf=after)
    mask_down = to(wall_mask, s.mask_edge.at[1], s.mask_send.at[1], s.mask_recv.at[1], surf=before)
    mask_up.start()
    mask_down.start()

    for j in range(1, min(2, N - 1)):

        @pl.when(sends_up(j))
        def _():
            value = whole(s.end_map)
            put(s.up_out, j, value)
            up_map(j).start()
            send_rows(UP + j, 1, value)

        @pl.when(sends_down(j))
        def _():
            value = [s.top_map[9 + c] for c in range(9)]
            put(s.down_out, j, value)
            down_map(j).start()
            send_rows(DOWN + j, -1, value)

    @pl.when(last)
    def _():
        send_rows(TOP, -1, whole(s.top_map))

    send_rows(ENDS, 0, whole(s.end_map))

    def pack_step(k, carry):
        for c in range(18):
            value = maps[k, c]
            s.side_rows[0, c, pl.ds(k, 1), :] = value[R - 1 : R]
            s.side_rows[1, c, pl.ds(k, 1), :] = value[0:1]
        return carry

    loop(K, pack_step, 0, 2)

    def side_map_copy(side):
        return to(
            s.side_out.at[side], s.side_in.at[side], s.side_send.at[side], s.side_recv.at[side],
            surf=toward(side),
        )

    for side in range(2):
        for c in range(18):
            s.side_out[side, c] = s.side_rows[side, c].astype(jnp.bfloat16)
        side_map_copy(side).start()

    def relay():
        for q in range(chunks):
            h_copy(q).wait_recv()
            inner = mat_mat(whole(s.h_in.at[q]), chunk(s.end_map, q))
            value = added(chunk(s.top_map, q), mat_mat(chunk(s.top_map, q, 9), inner))
            put(s.h_out, q, value)
            h_copy(q).start()
            for c in range(9):
                s.row_out[TOP, 0, c : c + 1, q * LANES : (q + 1) * LANES] = value[c][R - 1 : R]
                s.row_out[TOP, 1, c : c + 1, q * LANES : (q + 1) * LANES] = value[c][0:1]
        for side in range(2):
            row_copy(TOP, side, -1).start()

    early = jnp.logical_and(inside, place == N - 2)

    @pl.when(early)
    def _():
        relay()

    for j in range(2, N - 1):

        @pl.when(sends_up(j))
        def _():
            up_map(j - 1).wait_recv()
            value = mat_mat(whole(s.end_map), planes(s.up_in, j - 1, 9))
            put(s.up_out, j, value)
            up_map(j).start()
            send_rows(UP + j, 1, value)

        @pl.when(sends_down(j))
        def _():
            down_map(j - 1).wait_recv()
            value = mat_mat([s.top_map[9 + c] for c in range(9)], planes(s.down_in, j - 1, 9))
            put(s.down_out, j, value)
            down_map(j).start()
            send_rows(DOWN + j, -1, value)

    total = [part[me, c] for c in range(4)]
    mask_up.wait_recv()
    mask_down.wait_recv()
    for hop in range(1, S):
        part_copy(hop).wait_recv()
        total = [total[c] + got[hop, c] for c in range(4)]
    mask = wall_mask[...].astype(jnp.float32)
    low_mask = s.mask_edge[0, R - 1 : R, :].astype(jnp.float32)
    high_mask = s.mask_edge[1, 0:1, :].astype(jnp.float32)
    row = lax.broadcasted_iota(jnp.int32, (R, W), 0)
    lane = lax.broadcasted_iota(jnp.int32, (R, W), 1)

    def around(x, low, high):
        nearby = jnp.where(row == 0, low, pltpu.roll(x, 1, 0))
        nearby += jnp.where(row == R - 1, high, pltpu.roll(x, R - 1, 0))
        nearby += jnp.where(lane == 0, jnp.float32(0), pltpu.roll(x, 1, 1))
        return nearby + jnp.where(lane == W - 1, jnp.float32(0), pltpu.roll(x, W - 1, 1))

    at_wall = jnp.where(first, jnp.float32(1), jnp.float32(0))
    for c in range(3):
        shift = total[c] * mask
        wall[c] = link[0] * shift * at_wall
        wall[3 + c] = around(
            shift, total[3][c : c + 1] * low_mask, total[3][3 + c : 4 + c] * high_mask
        )

    def edge_copy(sweep, side):
        return to(
            s.edge_out.at[sweep, side], s.edge_in.at[sweep, side],
            s.edge_send.at[sweep, side], s.edge_recv.at[sweep, side], surf=toward(side),
        )

    def up_copy(sweep, j):
        return to(
            s.f_out.at[sweep], s.f_in.at[sweep, j], s.f_send.at[sweep, j], s.f_recv.at[sweep, j],
            norm=place + j,
        )

    def down_copy(sweep, j):
        return to(
            s.o_out.at[sweep], s.o_in.at[sweep, j], s.o_send.at[sweep, j], s.o_recv.at[sweep, j],
            norm=place - j,
        )

    def up_edge(sweep, side, j):
        return to(
            s.fe_out.at[sweep, side], s.fe_in.at[sweep, side, j],
            s.fe_send.at[sweep, side, j], s.fe_recv.at[sweep, side, j],
            surf=toward(side), norm=place + j,
        )

    def down_edge(sweep, side, j):
        return to(
            s.oe_out.at[sweep, side], s.oe_in.at[sweep, side, j],
            s.oe_send.at[sweep, side, j], s.oe_recv.at[sweep, side, j],
            surf=toward(side), norm=place - j,
        )

    def change(send, sent, sweep, values3):
        for c in range(3):
            known = sent[c] if sweep > 0 else jnp.float32(0)
            step = (values3[c] - known).astype(jnp.bfloat16)
            send[sweep, c] = step
            sent[c] = known + step.astype(jnp.float32)

    def wide(ref, index):
        return [v.astype(jnp.float32) for v in planes(ref, index)]

    for sweep in range(SWEEPS):
        shared = sweep < SWEEPS - 1

        def source(k, sweep=sweep):
            if sweep == 0:
                blend = 1.0 - (base + k).astype(jnp.float32) / (K * N)
                factor = stiffness[k] * blend
                return [factor * wall[3 + c] for c in range(3)]
            return [
                stiffness[k]
                * around(out[k, c], halo[0, c, pl.ds(k, 1), :], halo[1, c, pl.ds(k, 1), :])
                for c in range(3)
            ]

        def forward(k, state):
            right = added(source(k), [link[k] * v for v in state])
            state = mat_vec(planes(pivot, k, 9), right)
            put(values, k, state)
            return state

        start = mat_vec(
            planes(pivot, 0, 9), added(source(0), [wall[c] for c in range(3)])
        )
        put(values, 0, start)
        ends = later(K, forward, start)
        if shared:
            put_rows(s.fe_out.at[sweep, 0], [v[R - 1 : R] for v in ends])
            put_rows(s.fe_out.at[sweep, 1], [v[0:1] for v in ends])
            for j in range(N - 1, 0, -1):

                @pl.when(place + j < N)
                def _():
                    for side in range(2):
                        up_edge(sweep, side, j).start()

        change(s.f_out, s.f_sent, sweep, ends)
        for j in range(N - 1, 0, -1):

            @pl.when(place + j < N)
            def _():
                up_copy(sweep, j).start()

        def keep(k, state):
            put(values, k, state)
            if shared:
                for c in range(3):
                    halo[0, c, pl.ds(k, 1), :] = state[c][R - 1 : R]
                    halo[1, c, pl.ds(k, 1), :] = state[c][0:1]

        def backward(step, state):
            k = K - 1 - step
            state = added(
                planes(values, k), mat_vec(planes(pivot, k, 9), [link[k + 1] * v for v in state])
            )
            keep(k, state)
            return state

        keep(K - 1, ends)
        tops = later(K, backward, ends)

        if sweep == 0:

            @pl.when(jnp.logical_and(inside, jnp.logical_not(early)))
            def _():
                relay()

        @pl.when(jnp.logical_not(first))
        def _():
            top = added(
                [link[0] * v for v in tops],
                mat_vec([s.top_map[9 + c] for c in range(9)], mat_vec(h_full(), ends)),
            )
            if shared:
                put_rows(s.oe_out.at[sweep, 0], [v[R - 1 : R] for v in top])
                put_rows(s.oe_out.at[sweep, 1], [v[0:1] for v in top])
                for j in range(N - 1, 0, -1):

                    @pl.when(place - j >= 0)
                    def _():
                        for side in range(2):
                            down_edge(sweep, side, j).start()

            change(s.o_out, s.o_sent, sweep, top)
            for j in range(N - 1, 0, -1):

                @pl.when(place - j >= 0)
                def _():
                    down_copy(sweep, j).start()

        if shared:
            for side in range(2):
                s.edge_out[sweep, side] = halo[side].astype(jnp.bfloat16)
                edge_copy(sweep, side).start()
                up_edge(sweep, side, 0).start()

        if sweep == 0:
            s.enter[...] = jnp.zeros(s.enter.shape, jnp.float32)

        for j in range(1, N):
            if sweep == 0 and j > 1:

                @pl.when(jnp.logical_and(last, place >= j))
                def _():
                    up_map(j - 1).wait_recv()

                @pl.when(jnp.logical_and(first, N - 1 - place >= j))
                def _():
                    down_map(j - 1).wait_recv()

            @pl.when(place - j >= 0)
            def _():
                up_copy(sweep, j).wait_recv()
                moved = wide(s.f_in.at[sweep], j)
                if j > 1:
                    moved = mat_vec(planes(s.up_in, j - 1, 9), moved)
                put(s.enter, 0, added(planes(s.enter, 0), moved))

            @pl.when(place + j < N)
            def _():
                down_copy(sweep, j).wait_recv()
                moved = wide(s.o_in.at[sweep], j)
                if j > 1:
                    moved = mat_vec(planes(s.down_in, j - 1, 9), moved)
                put(s.enter, 1, added(planes(s.enter, 1), moved))

        if sweep == 0:

            @pl.when(first)
            def _():
                for q in range(chunks):
                    h_copy(q).wait_recv()

        entering = planes(s.enter, 0)
        state = added(ends, mat_vec(whole(s.end_map), entering))
        above = added(planes(s.enter, 1), mat_vec(h_full(), state))

        def finish(k, carry):
            state = added(planes(values, k), mat_vec(planes(maps, k, 9), entering))
            state = added(state, mat_vec([maps[k, 9 + c] for c in range(9)], above))
            put(out, k, state)
            return carry

        loop(K, finish, 0, 4)

        if shared:
            if sweep == 0:
                for side in range(2):
                    side_map_copy(side).wait_recv()
                    row_copy(ENDS, side, 0).wait_recv()

                @pl.when(jnp.logical_not(last))
                def _():
                    for side in range(2):
                        row_copy(TOP, side, 0).wait_recv()

                for j in range(2, N):

                    @pl.when(place >= j)
                    def _():
                        for side in range(2):
                            row_copy(UP + j - 1, side, 0).wait_recv()

                    @pl.when(N - 1 - place >= j)
                    def _():
                        for side in range(2):
                            row_copy(DOWN + j - 1, side, 0).wait_recv()

            s.enter_row[...] = jnp.zeros(s.enter_row.shape, jnp.float32)
            for j in range(1, N):

                @pl.when(place - j >= 0)
                def _():
                    for side in range(2):
                        up_edge(sweep, side, j).wait_recv()
                        moved = rows(s.fe_in.at[sweep, side, j])
                        if j > 1:
                            moved = mat_vec(rows(s.row_in.at[UP + j - 1, side], 9), moved)
                        put_rows(s.enter_row.at[side, 0], added(rows(s.enter_row.at[side, 0]), moved))

                @pl.when(place + j < N)
                def _():
                    for side in range(2):
                        down_edge(sweep, side, j).wait_recv()
                        moved = rows(s.oe_in.at[sweep, side, j])
                        if j > 1:
                            moved = mat_vec(rows(s.row_in.at[DOWN + j - 1, side], 9), moved)
                        put_rows(s.enter_row.at[side, 1], added(rows(s.enter_row.at[side, 1]), moved))

            for side in range(2):
                up_edge(sweep, side, 0).wait_recv()
                edge_copy(sweep, side).wait_recv()
                entered = rows(s.enter_row.at[side, 0])
                state = added(
                    rows(s.fe_in.at[sweep, side, 0]),
                    mat_vec(rows(s.row_in.at[ENDS, side], 9), entered),
                )
                higher = added(
                    rows(s.enter_row.at[side, 1]), mat_vec(rows(s.row_in.at[TOP, side], 9), state)
                )
                for c in range(3):
                    value = s.edge_in[sweep, side, c].astype(jnp.float32)
                    for b in range(3):
                        value += s.side_in[side, 3 * c + b].astype(jnp.float32) * entered[b]
                        value += s.side_in[side, 9 + 3 * c + b].astype(jnp.float32) * higher[b]
                    halo[side, c] = value

    for hop in range(1, S):
        part_copy(hop).wait_send()
    mask_up.wait_send()
    mask_down.wait_send()
    for side in range(2):
        side_map_copy(side).wait_send()
        row_copy(ENDS, side, 0).wait_send()
        for sweep in range(SWEEPS - 1):
            edge_copy(sweep, side).wait_send()

    @pl.when(jnp.logical_not(first))
    def _():
        for q in range(chunks):
            h_copy(q).wait_send()
        for side in range(2):
            row_copy(TOP, side, 0).wait_send()

    for j in range(1, N - 1):

        @pl.when(sends_up(j))
        def _():
            up_map(j).wait_send()
            for side in range(2):
                row_copy(UP + j, side, 0).wait_send()

        @pl.when(sends_down(j))
        def _():
            down_map(j).wait_send()
            for side in range(2):
                row_copy(DOWN + j, side, 0).wait_send()

    for j in range(N):

        @pl.when(place + j < N)
        def _():
            for sweep in range(SWEEPS):
                if j > 0:
                    up_copy(sweep, j).wait_send()
                if sweep < SWEEPS - 1:
                    for side in range(2):
                        up_edge(sweep, side, j).wait_send()

        if j > 0:

            @pl.when(place - j >= 0)
            def _():
                for sweep in range(SWEEPS):
                    down_copy(sweep, j).wait_send()
                    if sweep < SWEEPS - 1:
                        for side in range(2):
                            down_edge(sweep, side, j).wait_send()


def per_device(
    surf_size, norm_size, mode_shapes, amplitude, mode_patch, column_patch, wall_mask, offsets,
    coupling, pivot_inv, stiffness,
):
    S, N = surf_size, norm_size
    modes = mode_shapes.transpose(0, 2, 1, 3)
    pivot = pivot_inv.transpose(0, 2, 1, 3)
    K, _, R, W = pivot.shape
    C = W // LANES
    f32, bf16 = jnp.float32, jnp.bfloat16
    vmem = pl.BlockSpec(memory_space=pltpu.VMEM)
    smem = pl.BlockSpec(memory_space=pltpu.SMEM)
    hbm = pl.BlockSpec(memory_space=pltpu.HBM)
    dma = pltpu.SemaphoreType.DMA

    def room(*shape):
        return pltpu.VMEM(shape, f32)

    def half(*shape):
        return pltpu.VMEM(shape, bf16)

    G = SWEEPS - 1
    scratch = dict(
        modes=half(*modes.shape),
        coupling=room(K, R, W),
        pivot=room(K, 9, R, W),
        stiffness=room(K, R, W),
        link=room(K, R, W),
        maps=room(K, 18, R, W),
        end_map=room(9, R, W),
        top_map=room(18, R, W),
        part=room(S, 4, R, W),
        got=room(S, 4, R, W),
        mask_edge=pltpu.VMEM((2, R, W), jnp.int32),
        wall=room(6, R, W),
        values=room(K, 3, R, W),
        enter=room(2, 3, R, W),
        enter_row=room(2, 2, 3, W),
        halo=room(2, 3, K, W),
        edge_out=half(G, 2, 3, K, W),
        edge_in=half(G, 2, 3, K, W),
        side_rows=room(2, 18, K, W),
        side_out=half(2, 18, K, W),
        side_in=half(2, 18, K, W),
        row_out=room(2 * N, 2, 9, W),
        row_in=room(2 * N, 2, 9, W),
        f_in=half(SWEEPS, N, 3, R, W),
        f_out=half(SWEEPS, 3, R, W),
        f_sent=room(3, R, W),
        o_in=half(SWEEPS, N, 3, R, W),
        o_out=half(SWEEPS, 3, R, W),
        o_sent=room(3, R, W),
        fe_in=room(G, 2, N, 3, W),
        fe_out=room(G, 2, 3, W),
        oe_in=room(G, 2, N, 3, W),
        oe_out=room(G, 2, 3, W),
        h_in=room(C, 9, R, LANES),
        h_out=room(C, 9, R, LANES),
        up_in=room(N, 9, R, W),
        up_out=room(N, 9, R, W),
        down_in=room(N, 9, R, W),
        down_out=room(N, 9, R, W),
        load_sem=dma((3 + modes.shape[2] // (2 * R),)),
    )
    sems = dict(
        part=(S,), mask=(2,), h=(C,), row=(2 * N, 2), side=(2,), up=(N,), down=(N,),
        f=(SWEEPS, N), o=(SWEEPS, N), fe=(G, 2, N), oe=(G, 2, N), edge=(G, 2),
    )
    for name, shape in sems.items():
        scratch[name + "_send"] = dma(shape)
        scratch[name + "_recv"] = dma(shape)
    out = pl.pallas_call(
        functools.partial(kernel, S, N, tuple(scratch)),
        out_shape=pltpu.VMEM((K, 3, R, W), f32),
        in_specs=[smem, smem, vmem, vmem, vmem, hbm, hbm, hbm, hbm],
        out_specs=vmem,
        scratch_shapes=list(scratch.values()),
        compiler_params=pltpu.CompilerParams(
            collective_id=0, has_side_effects=True, vmem_limit_bytes=62 * 1024 * 1024
        ),
        name="line_sweeps",
    )(amplitude, mode_patch, column_patch, wall_mask, offsets, modes, coupling, pivot, stiffness)
    return out.transpose(0, 2, 1, 3)


def solution(mesh):
    return jax.shard_map(
        functools.partial(per_device, mesh.shape["surf"], mesh.shape["norm"]),
        mesh=mesh,
        in_specs=(
            P("surf", None, None, None),
            P(),
            P(),
            P(),
            P("surf", None),
            P("surf", None),
            P("norm", "surf", None),
            P("norm", "surf", None, None),
            P("norm", "surf", None),
        ),
        out_specs=P("norm", "surf", None, None),
        check_vma=False,
    )
```

```python
import functools
import types

import jax
import jax.numpy as jnp
from jax import lax
from jax.experimental import pallas as pl
from jax.experimental.pallas import tpu as pltpu
from jax.sharding import PartitionSpec as P

SWEEPS = 3
LANES = 128
MESH = pl.DeviceIdType.MESH


def loop(count, body, init, unroll=4):
    if count % unroll:
        unroll = 1

    def outer(step, carry):
        for part in range(unroll):
            carry = body(step * unroll + part, carry)
        return carry

    return lax.fori_loop(0, count // unroll, outer, init)


def later(count, body, init, unroll=5):
    return loop(count - 1, lambda step, carry: body(step + 1, carry), init, unroll)


def mat_vec(matrix, vector):
    return [
        matrix[3 * a] * vector[0] + matrix[3 * a + 1] * vector[1] + matrix[3 * a + 2] * vector[2]
        for a in range(3)
    ]


def fold(start, matrix, vector):
    return [
        (start[a] + matrix[3 * a] * vector[0])
        + (matrix[3 * a + 1] * vector[1] + matrix[3 * a + 2] * vector[2])
        for a in range(3)
    ]


def mat_mat(left, right):
    return [
        left[3 * a] * right[b] + left[3 * a + 1] * right[3 + b] + left[3 * a + 2] * right[6 + b]
        for a in range(3)
        for b in range(3)
    ]


def added(left, right):
    return [a + b for a, b in zip(left, right)]


def planes(ref, index, count=3):
    return [ref[index, c] for c in range(count)]


def whole(ref, count=9):
    return [ref[c] for c in range(count)]


def rows(ref, count=3):
    return [ref[c : c + 1, :] for c in range(count)]


def put(ref, index, values):
    for c, value in enumerate(values):
        ref[index, c] = value


def put_rows(ref, values):
    for c, value in enumerate(values):
        ref[c : c + 1, :] = value


def kernel(
    surf_size, norm_size, names,
    amplitude, mode_patch, column_patch, wall_mask, offsets,
    modes_hbm, coupling_hbm, pivot_hbm, stiffness_hbm,
    out, *scratch,
):
    s = types.SimpleNamespace(**dict(zip(names, scratch)))
    modes, coupling, pivot, stiffness = s.modes, s.coupling, s.pivot, s.stiffness
    link, maps, part, got, wall, values, halo = s.link, s.maps, s.part, s.got, s.wall, s.values, s.halo
    S, N = surf_size, norm_size
    K, _, R, W = pivot.shape
    M = modes.shape[0]
    B = 2 * R
    blocks = modes.shape[2] // B
    chunks = W // LANES
    me = lax.axis_index("surf")
    place = lax.axis_index("norm")
    before = lax.rem(me + S - 1, S)
    after = lax.rem(me + 1, S)
    first, last = place == 0, place == N - 1
    inside = jnp.logical_not(jnp.logical_or(first, last))
    base = place * K

    def to(src, dst, send, recv, **target):
        return pltpu.make_async_remote_copy(
            src_ref=src, dst_ref=dst, send_sem=send, recv_sem=recv,
            device_id=target, device_id_type=MESH,
        )

    def toward(side):
        return after if side == 0 else before

    mode_loads = [
        pltpu.make_async_copy(
            modes_hbm.at[:, :, pl.ds(b * B, B), :], modes.at[:, :, pl.ds(b * B, B), :], s.load_sem.at[3 + b]
        )
        for b in range(blocks)
    ]
    loads = [
        pltpu.make_async_copy(coupling_hbm, coupling, s.load_sem.at[0]),
        pltpu.make_async_copy(pivot_hbm, pivot, s.load_sem.at[1]),
        pltpu.make_async_copy(stiffness_hbm, stiffness, s.load_sem.at[2]),
    ]
    for copy in loads + mode_loads:
        copy.start()

    barrier = pltpu.get_barrier_semaphore()

    def greet(**target):
        pl.semaphore_signal(barrier, inc=1, device_id=target, device_id_type=MESH)

    for hop in range(1, S):
        greet(surf=lax.rem(me + hop, S))
    for hop in range(1, N):
        other = lax.rem(place + hop, N)
        greet(norm=other)
        greet(surf=before, norm=other)
        greet(surf=after, norm=other)

    for copy in loads:
        copy.wait()
    cut = offsets[...]

    def link_step(k, carry):
        link[k] = jnp.where(cut == base + k, jnp.float32(0), coupling[k])
        return carry

    loop(K, link_step, 0)

    def lower_step(k, state):
        scaled = [p * link[k] for p in planes(pivot, k, 9)]
        put(s.rise, k, scaled)
        state = mat_mat(scaled, state)
        put(maps, k, state)
        return state

    first_map = [p * link[0] for p in planes(pivot, 0, 9)]
    put(maps, 0, first_map)
    ends = lax.fori_loop(1, K, lower_step, first_map)
    for c in range(9):
        s.end_map[c] = ends[c]

    def upper_step(step, state):
        k = K - 1 - step
        scaled = [p * link[k + 1] for p in planes(pivot, k, 9)]
        put(s.fall, k, scaled)
        state = added(planes(maps, k, 9), mat_mat(scaled, state[:9])) + mat_mat(scaled, state[9:])
        put(maps, k, state)
        return state

    top_state = ends + planes(pivot, K - 1, 9)
    put(maps, K - 1, top_state)
    top_state = lax.fori_loop(1, K, upper_step, top_state)
    for c in range(18):
        s.top_map[c] = link[0] * top_state[c]

    own_mode = me * M
    for b in range(blocks):
        mode_loads[b].wait()
        patch = column_patch[b * B : (b + 1) * B, :]

        def mode_step(m, sums):
            weight = jnp.where(
                patch == mode_patch[own_mode + m], amplitude[own_mode + m], jnp.float32(0)
            )
            return [
                sums[c] + weight * modes[m, c, b * B : (b + 1) * B, :].astype(jnp.float32)
                for c in range(3)
            ]

        sums = loop(M, mode_step, [jnp.zeros((B, W), jnp.float32)] * 3)
        for c in range(3):
            for side in range(2):
                dest = 2 * b + side
                block = sums[c][side * R : (side + 1) * R]
                part[dest, c] = block
                part[(dest + 1) % S, 3, c : c + 1, :] = block[R - 1 : R]
                part[(dest - 1) % S, 3, 3 + c : 4 + c, :] = block[0:1]

    pl.semaphore_wait(barrier, S - 1 + 3 * (N - 1))

    def h_copy(q):
        return to(s.h_out.at[q], s.h_in.at[q], s.h_send.at[q], s.h_recv.at[q], norm=place - 1)

    full_copy = to(s.full_out, s.full_in, s.full_send, s.full_recv, norm=place - 1)

    def chunk(ref, q, start=0):
        return [ref[start + c, :, q * LANES : (q + 1) * LANES] for c in range(9)]

    def h_part(q):
        return [s.h_in[q, c].astype(jnp.float32) for c in range(9)]

    def h_full(sweep):
        if sweep > 0:
            return whole(s.full_in)
        pieces = [h_part(q) for q in range(chunks)]
        return [jnp.concatenate([p[c] for p in pieces], axis=1) for c in range(9)]

    def row_copy(slot, side, step):
        return to(
            s.row_out.at[slot, side], s.row_in.at[slot, side],
            s.row_send.at[slot, side], s.row_recv.at[slot, side],
            surf=toward(side), norm=place + step,
        )

    def send_rows(slot, step, values9):
        put_rows(s.row_out.at[slot, 0], [v[R - 1 : R] for v in values9])
        put_rows(s.row_out.at[slot, 1], [v[0:1] for v in values9])
        for side in range(2):
            row_copy(slot, side, step).start()

    UP, DOWN, ENDS, TOP = 0, N, 0, N

    def up_map(j):
        return to(s.up_out.at[j], s.up_in.at[j], s.up_send.at[j], s.up_recv.at[j], norm=place + 1)

    def down_map(j):
        return to(s.down_out.at[j], s.down_in.at[j], s.down_send.at[j], s.down_recv.at[j], norm=place - 1)

    def sends_up(j):
        return jnp.logical_and(place >= j, jnp.logical_not(last))

    def sends_down(j):
        return jnp.logical_and(N - 1 - place >= j, jnp.logical_not(first))

    @pl.when(last)
    def _():
        s.h_in[...] = jnp.zeros(s.h_in.shape, jnp.bfloat16)
        s.full_in[...] = jnp.zeros(s.full_in.shape, jnp.float32)
        s.row_in[TOP] = jnp.zeros(s.row_in.shape[1:], jnp.float32)
        for q in range(chunks):
            put(s.h_out, q, [v.astype(jnp.bfloat16) for v in chunk(s.top_map, q)])
            h_copy(q).start()

    def part_copy(hop):
        dest = lax.rem(me + hop, S)
        return to(part.at[dest], got.at[hop], s.part_send.at[hop], s.part_recv.at[hop], surf=dest)

    for hop in range(1, S):
        part_copy(hop).start()
    mask_up = to(wall_mask, s.mask_edge.at[0], s.mask_send.at[0], s.mask_recv.at[0], surf=after)
    mask_down = to(wall_mask, s.mask_edge.at[1], s.mask_send.at[1], s.mask_recv.at[1], surf=before)
    mask_up.start()
    mask_down.start()

    for j in range(1, min(2, N - 1)):

        @pl.when(sends_up(j))
        def _():
            value = whole(s.end_map)
            put(s.up_out, j, value)
            up_map(j).start()
            send_rows(UP + j, 1, value)

        @pl.when(sends_down(j))
        def _():
            value = [s.top_map[9 + c] for c in range(9)]
            put(s.down_out, j, value)
            down_map(j).start()
            send_rows(DOWN + j, -1, value)

    @pl.when(last)
    def _():
        send_rows(TOP, -1, whole(s.top_map))
        for c in range(9):
            s.full_out[c] = s.top_map[c]
        full_copy.start()

    send_rows(ENDS, 0, whole(s.end_map))

    def pack_step(k, carry):
        for c in range(18):
            value = maps[k, c]
            s.side_rows[0, c, pl.ds(k, 1), :] = value[R - 1 : R]
            s.side_rows[1, c, pl.ds(k, 1), :] = value[0:1]
        return carry

    loop(K, pack_step, 0, 2)

    def side_map_copy(side):
        return to(
            s.side_out.at[side], s.side_in.at[side], s.side_send.at[side], s.side_recv.at[side],
            surf=toward(side),
        )

    for side in range(2):
        for c in range(18):
            s.side_out[side, c] = s.side_rows[side, c].astype(jnp.bfloat16)
        side_map_copy(side).start()

    def relay():
        for q in range(chunks):
            h_copy(q).wait_recv()
            inner = mat_mat(h_part(q), chunk(s.end_map, q))
            value = added(chunk(s.top_map, q), mat_mat(chunk(s.top_map, q, 9), inner))
            put(s.h_out, q, [v.astype(jnp.bfloat16) for v in value])
            h_copy(q).start()
            for c in range(9):
                s.row_out[TOP, 0, c : c + 1, q * LANES : (q + 1) * LANES] = value[c][R - 1 : R]
                s.row_out[TOP, 1, c : c + 1, q * LANES : (q + 1) * LANES] = value[c][0:1]
        for side in range(2):
            row_copy(TOP, side, -1).start()

    def full_relay():
        full_copy.wait_recv()
        inner = mat_mat(whole(s.full_in), whole(s.end_map))
        outer = mat_mat([s.top_map[9 + c] for c in range(9)], inner)
        for c in range(9):
            s.full_out[c] = s.top_map[c] + outer[c]
        full_copy.start()

    early = jnp.logical_and(inside, place == N - 2)

    @pl.when(early)
    def _():
        relay()

    for j in range(2, N - 1):

        @pl.when(sends_up(j))
        def _():
            up_map(j - 1).wait_recv()
            value = mat_mat(whole(s.end_map), planes(s.up_in, j - 1, 9))
            put(s.up_out, j, value)
            up_map(j).start()
            send_rows(UP + j, 1, value)

        @pl.when(sends_down(j))
        def _():
            down_map(j - 1).wait_recv()
            value = mat_mat([s.top_map[9 + c] for c in range(9)], planes(s.down_in, j - 1, 9))
            put(s.down_out, j, value)
            down_map(j).start()
            send_rows(DOWN + j, -1, value)

    total = [part[me, c] for c in range(4)]
    mask_up.wait_recv()
    mask_down.wait_recv()
    for hop in range(1, S):
        part_copy(hop).wait_recv()
        total = [total[c] + got[hop, c] for c in range(4)]
    mask = wall_mask[...].astype(jnp.float32)
    low_mask = s.mask_edge[0, R - 1 : R, :].astype(jnp.float32)
    high_mask = s.mask_edge[1, 0:1, :].astype(jnp.float32)
    row = lax.broadcasted_iota(jnp.int32, (R, W), 0)
    lane = lax.broadcasted_iota(jnp.int32, (R, W), 1)

    def around(x, low, high):
        nearby = jnp.where(row == 0, low, pltpu.roll(x, 1, 0))
        nearby += jnp.where(row == R - 1, high, pltpu.roll(x, R - 1, 0))
        nearby += jnp.where(lane == 0, jnp.float32(0), pltpu.roll(x, 1, 1))
        return nearby + jnp.where(lane == W - 1, jnp.float32(0), pltpu.roll(x, W - 1, 1))

    at_wall = jnp.where(first, jnp.float32(1), jnp.float32(0))
    for c in range(3):
        shift = total[c] * mask
        wall[c] = link[0] * shift * at_wall
        wall[3 + c] = around(
            shift, total[3][c : c + 1] * low_mask, total[3][3 + c : 4 + c] * high_mask
        )

    def edge_copy(sweep, side):
        return to(
            s.edge_out.at[sweep, side], s.edge_in.at[sweep, side],
            s.edge_send.at[sweep, side], s.edge_recv.at[sweep, side], surf=toward(side),
        )

    def up_copy(sweep, j):
        return to(
            s.f_out.at[sweep], s.f_in.at[sweep, j], s.f_send.at[sweep, j], s.f_recv.at[sweep, j],
            norm=place + j,
        )

    def down_copy(sweep, j):
        return to(
            s.o_out.at[sweep], s.o_in.at[sweep, j], s.o_send.at[sweep, j], s.o_recv.at[sweep, j],
            norm=place - j,
        )

    def up_edge(sweep, side, j):
        return to(
            s.fe_out.at[sweep, side], s.fe_in.at[sweep, side, j],
            s.fe_send.at[sweep, side, j], s.fe_recv.at[sweep, side, j],
            surf=toward(side), norm=place + j,
        )

    def down_edge(sweep, side, j):
        return to(
            s.oe_out.at[sweep, side], s.oe_in.at[sweep, side, j],
            s.oe_send.at[sweep, side, j], s.oe_recv.at[sweep, side, j],
            surf=toward(side), norm=place - j,
        )

    def change(send, sent, sweep, values3):
        for c in range(3):
            known = sent[c] if sweep > 0 else jnp.float32(0)
            step = (values3[c] - known).astype(jnp.bfloat16)
            send[sweep, c] = step
            sent[c] = known + step.astype(jnp.float32)

    def wide(ref, index):
        return [v.astype(jnp.float32) for v in planes(ref, index)]

    for sweep in range(SWEEPS):
        shared = sweep < SWEEPS - 1

        def source(k, sweep=sweep):
            if sweep == 0:
                blend = 1.0 - (base + k).astype(jnp.float32) / (K * N)
                factor = stiffness[k] * blend
                return [factor * wall[3 + c] for c in range(3)]
            return [
                stiffness[k]
                * around(out[k, c], halo[0, c, pl.ds(k, 1), :], halo[1, c, pl.ds(k, 1), :])
                for c in range(3)
            ]

        def forward(k, state):
            state = fold(
                mat_vec(planes(pivot, k, 9), source(k)), planes(s.rise, k, 9), state
            )
            put(values, k, state)
            return state

        start = mat_vec(
            planes(pivot, 0, 9), added(source(0), [wall[c] for c in range(3)])
        )
        put(values, 0, start)
        ends = later(K, forward, start, K - 1)
        if shared:
            put_rows(s.fe_out.at[sweep, 0], [v[R - 1 : R] for v in ends])
            put_rows(s.fe_out.at[sweep, 1], [v[0:1] for v in ends])
            for j in range(N - 1, 0, -1):

                @pl.when(place + j < N)
                def _():
                    for side in range(2):
                        up_edge(sweep, side, j).start()

        change(s.f_out, s.f_sent, sweep, ends)
        for j in range(N - 1, 0, -1):

            @pl.when(place + j < N)
            def _():
                up_copy(sweep, j).start()

        def keep(k, state):
            put(values, k, state)
            if shared:
                for c in range(3):
                    halo[0, c, pl.ds(k, 1), :] = state[c][R - 1 : R]
                    halo[1, c, pl.ds(k, 1), :] = state[c][0:1]

        def backward(step, state):
            k = K - 1 - step
            state = fold(planes(values, k), planes(s.fall, k, 9), state)
            keep(k, state)
            return state

        keep(K - 1, ends)
        tops = later(K, backward, ends, K - 1)

        if sweep == 0:

            @pl.when(jnp.logical_and(inside, jnp.logical_not(early)))
            def _():
                relay()

        @pl.when(jnp.logical_not(first))
        def _():
            top = added(
                [link[0] * v for v in tops],
                mat_vec([s.top_map[9 + c] for c in range(9)], mat_vec(h_full(sweep), ends)),
            )
            if shared:
                put_rows(s.oe_out.at[sweep, 0], [v[R - 1 : R] for v in top])
                put_rows(s.oe_out.at[sweep, 1], [v[0:1] for v in top])
                for j in range(N - 1, 0, -1):

                    @pl.when(place - j >= 0)
                    def _():
                        for side in range(2):
                            down_edge(sweep, side, j).start()

            change(s.o_out, s.o_sent, sweep, top)
            for j in range(N - 1, 0, -1):

                @pl.when(place - j >= 0)
                def _():
                    down_copy(sweep, j).start()

        if shared:
            for side in range(2):
                s.edge_out[sweep, side] = halo[side].astype(jnp.bfloat16)
                edge_copy(sweep, side).start()
                up_edge(sweep, side, 0).start()

        if sweep == 0:

            @pl.when(early)
            def _():
                full_relay()

            s.enter[...] = jnp.zeros(s.enter.shape, jnp.float32)

        for j in range(1, N):
            if sweep == 0 and j > 1:

                @pl.when(jnp.logical_and(last, place >= j))
                def _():
                    up_map(j - 1).wait_recv()

                @pl.when(jnp.logical_and(first, N - 1 - place >= j))
                def _():
                    down_map(j - 1).wait_recv()

            @pl.when(place - j >= 0)
            def _():
                up_copy(sweep, j).wait_recv()
                moved = wide(s.f_in.at[sweep], j)
                if j > 1:
                    moved = mat_vec(planes(s.up_in, j - 1, 9), moved)
                put(s.enter, 0, added(planes(s.enter, 0), moved))

            @pl.when(place + j < N)
            def _():
                down_copy(sweep, j).wait_recv()
                moved = wide(s.o_in.at[sweep], j)
                if j > 1:
                    moved = mat_vec(planes(s.down_in, j - 1, 9), moved)
                put(s.enter, 1, added(planes(s.enter, 1), moved))

        if sweep < 2:

            @pl.when(first)
            def _():
                if sweep == 0:
                    for q in range(chunks):
                        h_copy(q).wait_recv()
                else:
                    full_copy.wait_recv()

        entering = planes(s.enter, 0)
        state = added(ends, mat_vec(whole(s.end_map), entering))
        above = added(planes(s.enter, 1), mat_vec(h_full(sweep), state))

        def finish(k, carry):
            state = added(planes(values, k), mat_vec(planes(maps, k, 9), entering))
            state = added(state, mat_vec([maps[k, 9 + c] for c in range(9)], above))
            put(out, k, state)
            return carry

        loop(K, finish, 0, 4)

        if sweep == 0:

            @pl.when(jnp.logical_and(inside, jnp.logical_not(early)))
            def _():
                full_relay()

        if shared:
            if sweep == 0:
                for side in range(2):
                    side_map_copy(side).wait_recv()
                    row_copy(ENDS, side, 0).wait_recv()

                @pl.when(jnp.logical_not(last))
                def _():
                    for side in range(2):
                        row_copy(TOP, side, 0).wait_recv()

                for j in range(2, N):

                    @pl.when(place >= j)
                    def _():
                        for side in range(2):
                            row_copy(UP + j - 1, side, 0).wait_recv()

                    @pl.when(N - 1 - place >= j)
                    def _():
                        for side in range(2):
                            row_copy(DOWN + j - 1, side, 0).wait_recv()

            s.enter_row[...] = jnp.zeros(s.enter_row.shape, jnp.float32)
            for j in range(1, N):

                @pl.when(place - j >= 0)
                def _():
                    for side in range(2):
                        up_edge(sweep, side, j).wait_recv()
                        moved = rows(s.fe_in.at[sweep, side, j])
                        if j > 1:
                            moved = mat_vec(rows(s.row_in.at[UP + j - 1, side], 9), moved)
                        put_rows(s.enter_row.at[side, 0], added(rows(s.enter_row.at[side, 0]), moved))

                @pl.when(place + j < N)
                def _():
                    for side in range(2):
                        down_edge(sweep, side, j).wait_recv()
                        moved = rows(s.oe_in.at[sweep, side, j])
                        if j > 1:
                            moved = mat_vec(rows(s.row_in.at[DOWN + j - 1, side], 9), moved)
                        put_rows(s.enter_row.at[side, 1], added(rows(s.enter_row.at[side, 1]), moved))

            for side in range(2):
                up_edge(sweep, side, 0).wait_recv()
                edge_copy(sweep, side).wait_recv()
                entered = rows(s.enter_row.at[side, 0])
                state = added(
                    rows(s.fe_in.at[sweep, side, 0]),
                    mat_vec(rows(s.row_in.at[ENDS, side], 9), entered),
                )
                higher = added(
                    rows(s.enter_row.at[side, 1]), mat_vec(rows(s.row_in.at[TOP, side], 9), state)
                )
                for c in range(3):
                    value = s.edge_in[sweep, side, c].astype(jnp.float32)
                    for b in range(3):
                        value += s.side_in[side, 3 * c + b].astype(jnp.float32) * entered[b]
                        value += s.side_in[side, 9 + 3 * c + b].astype(jnp.float32) * higher[b]
                    halo[side, c] = value

    for hop in range(1, S):
        part_copy(hop).wait_send()
    mask_up.wait_send()
    mask_down.wait_send()
    for side in range(2):
        side_map_copy(side).wait_send()
        row_copy(ENDS, side, 0).wait_send()
        for sweep in range(SWEEPS - 1):
            edge_copy(sweep, side).wait_send()

    @pl.when(jnp.logical_not(first))
    def _():
        full_copy.wait_send()
        for q in range(chunks):
            h_copy(q).wait_send()
        for side in range(2):
            row_copy(TOP, side, 0).wait_send()

    for j in range(1, N - 1):

        @pl.when(sends_up(j))
        def _():
            up_map(j).wait_send()
            for side in range(2):
                row_copy(UP + j, side, 0).wait_send()

        @pl.when(sends_down(j))
        def _():
            down_map(j).wait_send()
            for side in range(2):
                row_copy(DOWN + j, side, 0).wait_send()

    for j in range(N):

        @pl.when(place + j < N)
        def _():
            for sweep in range(SWEEPS):
                if j > 0:
                    up_copy(sweep, j).wait_send()
                if sweep < SWEEPS - 1:
                    for side in range(2):
                        up_edge(sweep, side, j).wait_send()

        if j > 0:

            @pl.when(place - j >= 0)
            def _():
                for sweep in range(SWEEPS):
                    down_copy(sweep, j).wait_send()
                    if sweep < SWEEPS - 1:
                        for side in range(2):
                            down_edge(sweep, side, j).wait_send()


def per_device(
    surf_size, norm_size, mode_shapes, amplitude, mode_patch, column_patch, wall_mask, offsets,
    coupling, pivot_inv, stiffness,
):
    S, N = surf_size, norm_size
    modes = mode_shapes.transpose(0, 2, 1, 3)
    pivot = pivot_inv.transpose(0, 2, 1, 3)
    K, _, R, W = pivot.shape
    C = W // LANES
    f32, bf16 = jnp.float32, jnp.bfloat16
    vmem = pl.BlockSpec(memory_space=pltpu.VMEM)
    smem = pl.BlockSpec(memory_space=pltpu.SMEM)
    hbm = pl.BlockSpec(memory_space=pltpu.HBM)
    dma = pltpu.SemaphoreType.DMA

    def room(*shape):
        return pltpu.VMEM(shape, f32)

    def half(*shape):
        return pltpu.VMEM(shape, bf16)

    G = SWEEPS - 1
    scratch = dict(
        modes=half(*modes.shape),
        coupling=room(K, R, W),
        pivot=room(K, 9, R, W),
        stiffness=room(K, R, W),
        link=room(K, R, W),
        rise=room(K, 9, R, W),
        fall=room(K, 9, R, W),
        maps=room(K, 18, R, W),
        end_map=room(9, R, W),
        top_map=room(18, R, W),
        part=room(S, 4, R, W),
        got=room(S, 4, R, W),
        mask_edge=pltpu.VMEM((2, R, W), jnp.int32),
        wall=room(6, R, W),
        values=room(K, 3, R, W),
        enter=room(2, 3, R, W),
        enter_row=room(2, 2, 3, W),
        halo=room(2, 3, K, W),
        edge_out=half(G, 2, 3, K, W),
        edge_in=half(G, 2, 3, K, W),
        side_rows=room(2, 18, K, W),
        side_out=half(2, 18, K, W),
        side_in=half(2, 18, K, W),
        row_out=room(2 * N, 2, 9, W),
        row_in=room(2 * N, 2, 9, W),
        f_in=half(SWEEPS, N, 3, R, W),
        f_out=half(SWEEPS, 3, R, W),
        f_sent=room(3, R, W),
        o_in=half(SWEEPS, N, 3, R, W),
        o_out=half(SWEEPS, 3, R, W),
        o_sent=room(3, R, W),
        fe_in=room(G, 2, N, 3, W),
        fe_out=room(G, 2, 3, W),
        oe_in=room(G, 2, N, 3, W),
        oe_out=room(G, 2, 3, W),
        h_in=half(C, 9, R, LANES),
        h_out=half(C, 9, R, LANES),
        full_in=room(9, R, W),
        full_out=room(9, R, W),
        up_in=room(N, 9, R, W),
        up_out=room(N, 9, R, W),
        down_in=room(N, 9, R, W),
        down_out=room(N, 9, R, W),
        load_sem=dma((3 + modes.shape[2] // (2 * R),)),
    )
    sems = dict(
        part=(S,), mask=(2,), h=(C,), full=(), row=(2 * N, 2), side=(2,), up=(N,), down=(N,),
        f=(SWEEPS, N), o=(SWEEPS, N), fe=(G, 2, N), oe=(G, 2, N), edge=(G, 2),
    )
    for name, shape in sems.items():
        scratch[name + "_send"] = dma(shape) if shape else dma
        scratch[name + "_recv"] = dma(shape) if shape else dma
    out = pl.pallas_call(
        functools.partial(kernel, S, N, tuple(scratch)),
        out_shape=pltpu.VMEM((K, 3, R, W), f32),
        in_specs=[smem, smem, vmem, vmem, vmem, hbm, hbm, hbm, hbm],
        out_specs=vmem,
        scratch_shapes=list(scratch.values()),
        compiler_params=pltpu.CompilerParams(
            collective_id=0, has_side_effects=True, vmem_limit_bytes=62 * 1024 * 1024
        ),
        name="line_sweeps",
    )(amplitude, mode_patch, column_patch, wall_mask, offsets, modes, coupling, pivot, stiffness)
    return out.transpose(0, 2, 1, 3)


def solution(mesh):
    return jax.shard_map(
        functools.partial(per_device, mesh.shape["surf"], mesh.shape["norm"]),
        mesh=mesh,
        in_specs=(
            P("surf", None, None, None),
            P(),
            P(),
            P(),
            P("surf", None),
            P("surf", None),
            P("norm", "surf", None),
            P("norm", "surf", None, None),
            P("norm", "surf", None),
        ),
        out_specs=P("norm", "surf", None, None),
        check_vma=False,
    )
```

```python
import functools
import types

import jax
import jax.numpy as jnp
from jax import lax
from jax.experimental import pallas as pl
from jax.experimental.pallas import tpu as pltpu
from jax.sharding import PartitionSpec as P

SWEEPS = 3
LANES = 128
MESH = pl.DeviceIdType.MESH


def loop(count, body, init, unroll=4):
    if count % unroll:
        unroll = 1

    def outer(step, carry):
        for part in range(unroll):
            carry = body(step * unroll + part, carry)
        return carry

    return lax.fori_loop(0, count // unroll, outer, init)


def later(count, body, init, unroll=5):
    return loop(count - 1, lambda step, carry: body(step + 1, carry), init, unroll)


def mat_vec(matrix, vector):
    return [
        matrix[3 * a] * vector[0] + matrix[3 * a + 1] * vector[1] + matrix[3 * a + 2] * vector[2]
        for a in range(3)
    ]


def fold(start, matrix, vector):
    return [
        (start[a] + matrix[3 * a] * vector[0])
        + (matrix[3 * a + 1] * vector[1] + matrix[3 * a + 2] * vector[2])
        for a in range(3)
    ]


def mat_mat(left, right):
    return [
        left[3 * a] * right[b] + left[3 * a + 1] * right[3 + b] + left[3 * a + 2] * right[6 + b]
        for a in range(3)
        for b in range(3)
    ]


def added(left, right):
    return [a + b for a, b in zip(left, right)]


def planes(ref, index, count=3):
    return [ref[index, c] for c in range(count)]


def whole(ref, count=9):
    return [ref[c] for c in range(count)]


def rows(ref, count=3):
    return [ref[c : c + 1, :] for c in range(count)]


def put(ref, index, values):
    for c, value in enumerate(values):
        ref[index, c] = value


def put_rows(ref, values):
    for c, value in enumerate(values):
        ref[c : c + 1, :] = value


def kernel(
    surf_size, norm_size, names,
    amplitude, mode_patch, column_patch, wall_mask, offsets,
    modes_hbm, coupling_hbm, pivot_hbm, stiffness_hbm,
    out, *scratch,
):
    s = types.SimpleNamespace(**dict(zip(names, scratch)))
    modes, coupling, pivot, stiffness = s.modes, s.coupling, s.pivot, s.stiffness
    link, maps, part, got, wall, values, halo = s.link, s.maps, s.part, s.got, s.wall, s.values, s.halo
    S, N = surf_size, norm_size
    K, _, R, W = pivot.shape
    M = modes.shape[0]
    B = 2 * R
    blocks = modes.shape[2] // B
    chunks = W // LANES
    me = lax.axis_index("surf")
    place = lax.axis_index("norm")
    before = lax.rem(me + S - 1, S)
    after = lax.rem(me + 1, S)
    first, last = place == 0, place == N - 1
    inside = jnp.logical_not(jnp.logical_or(first, last))
    base = place * K

    def to(src, dst, send, recv, **target):
        return pltpu.make_async_remote_copy(
            src_ref=src, dst_ref=dst, send_sem=send, recv_sem=recv,
            device_id=target, device_id_type=MESH,
        )

    def toward(side):
        return after if side == 0 else before

    def settle(ref, sem):
        pltpu.make_async_copy(ref, ref, sem).wait()

    mode_loads = [
        pltpu.make_async_copy(
            modes_hbm.at[:, :, pl.ds(b * B, B), :], modes.at[:, :, pl.ds(b * B, B), :], s.load_sem.at[3 + b]
        )
        for b in range(blocks)
    ]
    loads = [
        pltpu.make_async_copy(coupling_hbm, coupling, s.load_sem.at[0]),
        pltpu.make_async_copy(pivot_hbm, pivot, s.load_sem.at[1]),
        pltpu.make_async_copy(stiffness_hbm, stiffness, s.load_sem.at[2]),
    ]
    for copy in loads + mode_loads:
        copy.start()

    barrier = pltpu.get_barrier_semaphore()

    def greet(**target):
        pl.semaphore_signal(barrier, inc=1, device_id=target, device_id_type=MESH)

    for hop in range(1, S):
        greet(surf=lax.rem(me + hop, S))
    for hop in range(1, N):
        other = lax.rem(place + hop, N)
        greet(norm=other)
        greet(surf=before, norm=other)
        greet(surf=after, norm=other)

    for copy in loads:
        copy.wait()
    cut = offsets[...]

    def link_step(k, carry):
        link[k] = jnp.where(cut == base + k, jnp.float32(0), coupling[k])
        return carry

    loop(K, link_step, 0)

    def lower_step(k, state):
        scaled = [p * link[k] for p in planes(pivot, k, 9)]
        put(s.rise, k, scaled)
        state = mat_mat(scaled, state)
        put(maps, k, state)
        return state

    first_map = [p * link[0] for p in planes(pivot, 0, 9)]
    put(maps, 0, first_map)
    ends = lax.fori_loop(1, K, lower_step, first_map)
    for c in range(9):
        s.end_map[c] = ends[c]

    def upper_step(step, state):
        k = K - 1 - step
        scaled = [p * link[k + 1] for p in planes(pivot, k, 9)]
        put(s.fall, k, scaled)
        state = added(planes(maps, k, 9), mat_mat(scaled, state[:9])) + mat_mat(scaled, state[9:])
        put(maps, k, state)
        return state

    top_state = ends + planes(pivot, K - 1, 9)
    put(maps, K - 1, top_state)
    top_state = lax.fori_loop(1, K, upper_step, top_state)
    for c in range(18):
        s.top_map[c] = link[0] * top_state[c]

    own_mode = me * M
    for b in range(blocks):
        mode_loads[b].wait()
        patch = column_patch[b * B : (b + 1) * B, :]

        def mode_step(m, sums):
            weight = jnp.where(
                patch == mode_patch[own_mode + m], amplitude[own_mode + m], jnp.float32(0)
            )
            return [
                sums[c] + weight * modes[m, c, b * B : (b + 1) * B, :].astype(jnp.float32)
                for c in range(3)
            ]

        sums = loop(M, mode_step, [jnp.zeros((B, W), jnp.float32)] * 3)
        for c in range(3):
            for side in range(2):
                dest = 2 * b + side
                block = sums[c][side * R : (side + 1) * R]
                part[dest, c] = block
                part[(dest + 1) % S, 3, c : c + 1, :] = block[R - 1 : R]
                part[(dest - 1) % S, 3, 3 + c : 4 + c, :] = block[0:1]

    pl.semaphore_wait(barrier, S - 1 + 3 * (N - 1))

    def h_copy(q):
        return to(s.h_out.at[q], s.h_in.at[q], s.h_send.at[q], s.h_recv.at[q], norm=place - 1)

    full_copy = to(s.full_out, s.full_in, s.full_send, s.full_recv, norm=place - 1)

    def chunk(ref, q, start=0):
        return [ref[start + c, :, q * LANES : (q + 1) * LANES] for c in range(9)]

    def h_part(q):
        return [s.h_in[q, c].astype(jnp.float32) for c in range(9)]

    def h_full(sweep):
        if sweep > 0:
            return whole(s.full_in)
        pieces = [h_part(q) for q in range(chunks)]
        return [jnp.concatenate([p[c] for p in pieces], axis=1) for c in range(9)]

    def row_copy(slot, side, step):
        return to(
            s.row_out.at[slot, side], s.row_in.at[slot, side],
            s.row_send.at[slot], s.row_recv.at[slot],
            surf=toward(side), norm=place + step,
        )

    def send_rows(slot, step, values9):
        put_rows(s.row_out.at[slot, 0], [v[R - 1 : R] for v in values9])
        put_rows(s.row_out.at[slot, 1], [v[0:1] for v in values9])
        for side in range(2):
            row_copy(slot, side, step).start()

    UP, DOWN, ENDS, TOP = 0, N - 1, 0, N - 1

    def up_map(j):
        return to(s.up_out.at[j], s.up_in.at[j], s.up_send.at[j - 1], s.up_recv.at[j - 1], norm=place + 1)

    def down_map(j):
        return to(s.down_out.at[j], s.down_in.at[j], s.down_send.at[j - 1], s.down_recv.at[j - 1], norm=place - 1)

    def sends_up(j):
        return jnp.logical_and(place >= j, jnp.logical_not(last))

    def sends_down(j):
        return jnp.logical_and(N - 1 - place >= j, jnp.logical_not(first))

    @pl.when(last)
    def _():
        s.h_in[...] = jnp.zeros(s.h_in.shape, jnp.bfloat16)
        s.full_in[...] = jnp.zeros(s.full_in.shape, jnp.float32)
        s.row_in[TOP] = jnp.zeros(s.row_in.shape[1:], jnp.float32)
        for q in range(chunks):
            put(s.h_out, q, [v.astype(jnp.bfloat16) for v in chunk(s.top_map, q)])
            h_copy(q).start()

    def part_copy(hop):
        dest = lax.rem(me + hop, S)
        return to(part.at[dest], got.at[hop], s.part_send, s.part_recv, surf=dest)

    for hop in range(1, S):
        part_copy(hop).start()
    mask_up = to(wall_mask, s.mask_edge.at[0], s.mask_send, s.mask_recv, surf=after)
    mask_down = to(wall_mask, s.mask_edge.at[1], s.mask_send, s.mask_recv, surf=before)
    mask_up.start()
    mask_down.start()

    for j in range(1, min(2, N - 1)):

        @pl.when(sends_up(j))
        def _():
            value = whole(s.end_map)
            put(s.up_out, j, value)
            up_map(j).start()
            send_rows(UP + j, 1, value)

        @pl.when(sends_down(j))
        def _():
            value = [s.top_map[9 + c] for c in range(9)]
            put(s.down_out, j, value)
            down_map(j).start()
            send_rows(DOWN + j, -1, value)

    @pl.when(last)
    def _():
        send_rows(TOP, -1, whole(s.top_map))
        for c in range(9):
            s.full_out[c] = s.top_map[c]
        full_copy.start()

    send_rows(ENDS, 0, whole(s.end_map))

    def pack_step(k, carry):
        for c in range(18):
            value = maps[k, c]
            s.side_rows[0, c, pl.ds(k, 1), :] = value[R - 1 : R]
            s.side_rows[1, c, pl.ds(k, 1), :] = value[0:1]
        return carry

    loop(K, pack_step, 0, 2)

    def side_map_copy(side):
        return to(
            s.side_out.at[side], s.side_in.at[side], s.side_send, s.side_recv,
            surf=toward(side),
        )

    for side in range(2):
        for c in range(18):
            s.side_out[side, c] = s.side_rows[side, c].astype(jnp.bfloat16)
        side_map_copy(side).start()

    def relay():
        for q in range(chunks):
            h_copy(q).wait_recv()
            inner = mat_mat(h_part(q), chunk(s.end_map, q))
            value = added(chunk(s.top_map, q), mat_mat(chunk(s.top_map, q, 9), inner))
            put(s.h_out, q, [v.astype(jnp.bfloat16) for v in value])
            h_copy(q).start()
            for c in range(9):
                s.row_out[TOP, 0, c : c + 1, q * LANES : (q + 1) * LANES] = value[c][R - 1 : R]
                s.row_out[TOP, 1, c : c + 1, q * LANES : (q + 1) * LANES] = value[c][0:1]
        for side in range(2):
            row_copy(TOP, side, -1).start()

    def full_relay():
        full_copy.wait_recv()
        inner = mat_mat(whole(s.full_in), whole(s.end_map))
        outer = mat_mat([s.top_map[9 + c] for c in range(9)], inner)
        for c in range(9):
            s.full_out[c] = s.top_map[c] + outer[c]
        full_copy.start()

    early = jnp.logical_and(inside, place == N - 2)

    @pl.when(early)
    def _():
        relay()

    for j in range(2, N - 1):

        @pl.when(sends_up(j))
        def _():
            up_map(j - 1).wait_recv()
            value = mat_mat(whole(s.end_map), planes(s.up_in, j - 1, 9))
            put(s.up_out, j, value)
            up_map(j).start()
            send_rows(UP + j, 1, value)

        @pl.when(sends_down(j))
        def _():
            down_map(j - 1).wait_recv()
            value = mat_mat([s.top_map[9 + c] for c in range(9)], planes(s.down_in, j - 1, 9))
            put(s.down_out, j, value)
            down_map(j).start()
            send_rows(DOWN + j, -1, value)

    total = [part[me, c] for c in range(4)]
    settle(s.mask_edge, s.mask_recv)
    settle(got.at[pl.ds(0, S - 1)], s.part_recv)
    for hop in range(1, S):
        total = [total[c] + got[hop, c] for c in range(4)]
    mask = wall_mask[...].astype(jnp.float32)
    low_mask = s.mask_edge[0, R - 1 : R, :].astype(jnp.float32)
    high_mask = s.mask_edge[1, 0:1, :].astype(jnp.float32)
    row = lax.broadcasted_iota(jnp.int32, (R, W), 0)
    lane = lax.broadcasted_iota(jnp.int32, (R, W), 1)

    def around(x, low, high):
        nearby = jnp.where(row == 0, low, pltpu.roll(x, 1, 0))
        nearby += jnp.where(row == R - 1, high, pltpu.roll(x, R - 1, 0))
        nearby += jnp.where(lane == 0, jnp.float32(0), pltpu.roll(x, 1, 1))
        return nearby + jnp.where(lane == W - 1, jnp.float32(0), pltpu.roll(x, W - 1, 1))

    at_wall = jnp.where(first, jnp.float32(1), jnp.float32(0))
    for c in range(3):
        shift = total[c] * mask
        wall[c] = link[0] * shift * at_wall
        wall[3 + c] = around(
            shift, total[3][c : c + 1] * low_mask, total[3][3 + c : 4 + c] * high_mask
        )

    def edge_copy(sweep, side):
        return to(
            s.edge_out.at[sweep, side], s.edge_in.at[sweep, side],
            s.edge_send.at[sweep], s.edge_recv.at[sweep], surf=toward(side),
        )

    def up_copy(sweep, j):
        return to(
            s.f_out.at[sweep], s.z_in.at[sweep, place], s.z_send.at[sweep], s.z_recv.at[sweep],
            norm=place + j,
        )

    def down_copy(sweep, j):
        return to(
            s.o_out.at[sweep], s.z_in.at[sweep, place], s.z_send.at[sweep], s.z_recv.at[sweep],
            norm=place - j,
        )

    def up_edge(sweep, side, j):
        return to(
            s.fe_out.at[sweep, side], s.e_in.at[sweep, side, place],
            s.e_send.at[sweep], s.e_recv.at[sweep],
            surf=toward(side), norm=place + j,
        )

    def down_edge(sweep, side, j):
        return to(
            s.oe_out.at[sweep, side], s.e_in.at[sweep, side, place],
            s.e_send.at[sweep], s.e_recv.at[sweep],
            surf=toward(side), norm=place - j,
        )

    def change(send, sent, sweep, values3):
        for c in range(3):
            known = sent[c] if sweep > 0 else jnp.float32(0)
            step = (values3[c] - known).astype(jnp.bfloat16)
            send[sweep, c] = step
            sent[c] = known + step.astype(jnp.float32)

    def wide(ref, index):
        return [v.astype(jnp.float32) for v in planes(ref, index)]

    for sweep in range(SWEEPS):
        shared = sweep < SWEEPS - 1

        def source(k, sweep=sweep):
            if sweep == 0:
                blend = 1.0 - (base + k).astype(jnp.float32) / (K * N)
                factor = stiffness[k] * blend
                return [factor * wall[3 + c] for c in range(3)]
            return [
                stiffness[k]
                * around(out[k, c], halo[0, c, pl.ds(k, 1), :], halo[1, c, pl.ds(k, 1), :])
                for c in range(3)
            ]

        def forward(k, state):
            state = fold(
                mat_vec(planes(pivot, k, 9), source(k)), planes(s.rise, k, 9), state
            )
            put(values, k, state)
            return state

        start = mat_vec(
            planes(pivot, 0, 9), added(source(0), [wall[c] for c in range(3)])
        )
        put(values, 0, start)
        ends = later(K, forward, start, K - 1)
        if shared:
            put_rows(s.fe_out.at[sweep, 0], [v[R - 1 : R] for v in ends])
            put_rows(s.fe_out.at[sweep, 1], [v[0:1] for v in ends])
            for j in range(N - 1, 0, -1):

                @pl.when(place + j < N)
                def _():
                    for side in range(2):
                        up_edge(sweep, side, j).start()

        change(s.f_out, s.f_sent, sweep, ends)
        for j in range(N - 1, 0, -1):

            @pl.when(place + j < N)
            def _():
                up_copy(sweep, j).start()

        def keep(k, state):
            put(values, k, state)
            if shared:
                for c in range(3):
                    halo[0, c, pl.ds(k, 1), :] = state[c][R - 1 : R]
                    halo[1, c, pl.ds(k, 1), :] = state[c][0:1]

        def backward(step, state):
            k = K - 1 - step
            state = fold(planes(values, k), planes(s.fall, k, 9), state)
            keep(k, state)
            return state

        keep(K - 1, ends)
        tops = later(K, backward, ends, K - 1)

        if sweep == 0:

            @pl.when(jnp.logical_and(inside, jnp.logical_not(early)))
            def _():
                relay()

        @pl.when(jnp.logical_not(first))
        def _():
            top = added(
                [link[0] * v for v in tops],
                mat_vec([s.top_map[9 + c] for c in range(9)], mat_vec(h_full(sweep), ends)),
            )
            if shared:
                put_rows(s.oe_out.at[sweep, 0], [v[R - 1 : R] for v in top])
                put_rows(s.oe_out.at[sweep, 1], [v[0:1] for v in top])
                for j in range(N - 1, 0, -1):

                    @pl.when(place - j >= 0)
                    def _():
                        for side in range(2):
                            down_edge(sweep, side, j).start()

            change(s.o_out, s.o_sent, sweep, top)
            for j in range(N - 1, 0, -1):

                @pl.when(place - j >= 0)
                def _():
                    down_copy(sweep, j).start()

        if shared:
            for side in range(2):
                s.edge_out[sweep, side] = halo[side].astype(jnp.bfloat16)
                edge_copy(sweep, side).start()
                up_edge(sweep, side, 0).start()

        if sweep == 0:

            @pl.when(early)
            def _():
                full_relay()

            s.enter[...] = jnp.zeros(s.enter.shape, jnp.float32)

        settle(s.z_in.at[sweep, pl.ds(0, N - 1)], s.z_recv.at[sweep])
        for j in range(1, N):
            if sweep == 0 and j > 1:

                @pl.when(jnp.logical_and(last, place >= j))
                def _():
                    up_map(j - 1).wait_recv()

                @pl.when(jnp.logical_and(first, N - 1 - place >= j))
                def _():
                    down_map(j - 1).wait_recv()

            @pl.when(place - j >= 0)
            def _():
                moved = wide(s.z_in.at[sweep], place - j)
                if j > 1:
                    moved = mat_vec(planes(s.up_in, j - 1, 9), moved)
                put(s.enter, 0, added(planes(s.enter, 0), moved))

            @pl.when(place + j < N)
            def _():
                moved = wide(s.z_in.at[sweep], place + j)
                if j > 1:
                    moved = mat_vec(planes(s.down_in, j - 1, 9), moved)
                put(s.enter, 1, added(planes(s.enter, 1), moved))

        if sweep < 2:

            @pl.when(first)
            def _():
                if sweep == 0:
                    for q in range(chunks):
                        h_copy(q).wait_recv()
                else:
                    full_copy.wait_recv()

        entering = planes(s.enter, 0)
        state = added(ends, mat_vec(whole(s.end_map), entering))
        above = added(planes(s.enter, 1), mat_vec(h_full(sweep), state))

        def finish(k, carry):
            state = added(planes(values, k), mat_vec(planes(maps, k, 9), entering))
            state = added(state, mat_vec([maps[k, 9 + c] for c in range(9)], above))
            put(out, k, state)
            return carry

        loop(K, finish, 0, 4)

        if sweep == 0:

            @pl.when(jnp.logical_and(inside, jnp.logical_not(early)))
            def _():
                full_relay()

        if shared:
            if sweep == 0:
                settle(s.side_in, s.side_recv)
                settle(s.row_in.at[ENDS], s.row_recv.at[ENDS])

                @pl.when(jnp.logical_not(last))
                def _():
                    settle(s.row_in.at[TOP], s.row_recv.at[TOP])

                for j in range(2, N):

                    @pl.when(place >= j)
                    def _():
                        settle(s.row_in.at[UP + j - 1], s.row_recv.at[UP + j - 1])

                    @pl.when(N - 1 - place >= j)
                    def _():
                        settle(s.row_in.at[DOWN + j - 1], s.row_recv.at[DOWN + j - 1])

            settle(s.e_in.at[sweep], s.e_recv.at[sweep])
            settle(s.edge_in.at[sweep], s.edge_recv.at[sweep])
            s.enter_row[...] = jnp.zeros(s.enter_row.shape, jnp.float32)
            for j in range(1, N):

                @pl.when(place - j >= 0)
                def _():
                    for side in range(2):
                        moved = rows(s.e_in.at[sweep, side, place - j])
                        if j > 1:
                            moved = mat_vec(rows(s.row_in.at[UP + j - 1, side], 9), moved)
                        put_rows(s.enter_row.at[side, 0], added(rows(s.enter_row.at[side, 0]), moved))

                @pl.when(place + j < N)
                def _():
                    for side in range(2):
                        moved = rows(s.e_in.at[sweep, side, place + j])
                        if j > 1:
                            moved = mat_vec(rows(s.row_in.at[DOWN + j - 1, side], 9), moved)
                        put_rows(s.enter_row.at[side, 1], added(rows(s.enter_row.at[side, 1]), moved))

            for side in range(2):
                entered = rows(s.enter_row.at[side, 0])
                state = added(
                    rows(s.e_in.at[sweep, side, place]),
                    mat_vec(rows(s.row_in.at[ENDS, side], 9), entered),
                )
                higher = added(
                    rows(s.enter_row.at[side, 1]), mat_vec(rows(s.row_in.at[TOP, side], 9), state)
                )
                for c in range(3):
                    value = s.edge_in[sweep, side, c].astype(jnp.float32)
                    for b in range(3):
                        value += s.side_in[side, 3 * c + b].astype(jnp.float32) * entered[b]
                        value += s.side_in[side, 9 + 3 * c + b].astype(jnp.float32) * higher[b]
                    halo[side, c] = value

    settle(got.at[pl.ds(0, S - 1)], s.part_send)
    settle(s.mask_edge, s.mask_send)
    settle(s.side_out, s.side_send)
    settle(s.row_out.at[ENDS], s.row_send.at[ENDS])
    for sweep in range(SWEEPS):
        settle(s.z_in.at[sweep, pl.ds(0, N - 1)], s.z_send.at[sweep])
    for sweep in range(SWEEPS - 1):
        settle(s.edge_out.at[sweep], s.edge_send.at[sweep])
        settle(s.e_in.at[sweep], s.e_send.at[sweep])

    @pl.when(jnp.logical_not(first))
    def _():
        full_copy.wait_send()
        for q in range(chunks):
            h_copy(q).wait_send()
        settle(s.row_out.at[TOP], s.row_send.at[TOP])

    for j in range(1, N - 1):

        @pl.when(sends_up(j))
        def _():
            up_map(j).wait_send()
            settle(s.row_out.at[UP + j], s.row_send.at[UP + j])

        @pl.when(sends_down(j))
        def _():
            down_map(j).wait_send()
            settle(s.row_out.at[DOWN + j], s.row_send.at[DOWN + j])


def per_device(
    surf_size, norm_size, mode_shapes, amplitude, mode_patch, column_patch, wall_mask, offsets,
    coupling, pivot_inv, stiffness,
):
    S, N = surf_size, norm_size
    modes = mode_shapes.transpose(0, 2, 1, 3)
    pivot = pivot_inv.transpose(0, 2, 1, 3)
    K, _, R, W = pivot.shape
    C = W // LANES
    f32, bf16 = jnp.float32, jnp.bfloat16
    vmem = pl.BlockSpec(memory_space=pltpu.VMEM)
    smem = pl.BlockSpec(memory_space=pltpu.SMEM)
    hbm = pl.BlockSpec(memory_space=pltpu.HBM)
    dma = pltpu.SemaphoreType.DMA

    def room(*shape):
        return pltpu.VMEM(shape, f32)

    def half(*shape):
        return pltpu.VMEM(shape, bf16)

    G = SWEEPS - 1
    scratch = dict(
        modes=half(*modes.shape),
        coupling=room(K, R, W),
        pivot=room(K, 9, R, W),
        stiffness=room(K, R, W),
        link=room(K, R, W),
        rise=room(K, 9, R, W),
        fall=room(K, 9, R, W),
        maps=room(K, 18, R, W),
        end_map=room(9, R, W),
        top_map=room(18, R, W),
        part=room(S, 4, R, W),
        got=room(S, 4, R, W),
        mask_edge=pltpu.VMEM((2, R, W), jnp.int32),
        wall=room(6, R, W),
        values=room(K, 3, R, W),
        enter=room(2, 3, R, W),
        enter_row=room(2, 2, 3, W),
        halo=room(2, 3, K, W),
        edge_out=half(G, 2, 3, K, W),
        edge_in=half(G, 2, 3, K, W),
        side_rows=room(2, 18, K, W),
        side_out=half(2, 18, K, W),
        side_in=half(2, 18, K, W),
        row_out=room(2 * N - 2, 2, 9, W),
        row_in=room(2 * N - 2, 2, 9, W),
        z_in=half(SWEEPS, N, 3, R, W),
        f_out=half(SWEEPS, 3, R, W),
        f_sent=room(3, R, W),
        o_out=half(SWEEPS, 3, R, W),
        o_sent=room(3, R, W),
        e_in=room(G, 2, N, 3, W),
        fe_out=room(G, 2, 3, W),
        oe_out=room(G, 2, 3, W),
        h_in=half(C, 9, R, LANES),
        h_out=half(C, 9, R, LANES),
        full_in=room(9, R, W),
        full_out=room(9, R, W),
        up_in=room(N, 9, R, W),
        up_out=room(N, 9, R, W),
        down_in=room(N, 9, R, W),
        down_out=room(N, 9, R, W),
        load_sem=dma((3 + modes.shape[2] // (2 * R),)),
    )
    sems = dict(
        part=(), mask=(), h=(C,), full=(), row=(2 * N - 2,), side=(), up=(max(N - 2, 1),),
        down=(max(N - 2, 1),), z=(SWEEPS,), e=(G,), edge=(G,),
    )
    for name, shape in sems.items():
        scratch[name + "_send"] = dma(shape) if shape else dma
        scratch[name + "_recv"] = dma(shape) if shape else dma
    out = pl.pallas_call(
        functools.partial(kernel, S, N, tuple(scratch)),
        out_shape=pltpu.VMEM((K, 3, R, W), f32),
        in_specs=[smem, smem, vmem, vmem, vmem, hbm, hbm, hbm, hbm],
        out_specs=vmem,
        scratch_shapes=list(scratch.values()),
        compiler_params=pltpu.CompilerParams(
            collective_id=0, has_side_effects=True, vmem_limit_bytes=62 * 1024 * 1024
        ),
        name="line_sweeps",
    )(amplitude, mode_patch, column_patch, wall_mask, offsets, modes, coupling, pivot, stiffness)
    return out.transpose(0, 2, 1, 3)


def solution(mesh):
    return jax.shard_map(
        functools.partial(per_device, mesh.shape["surf"], mesh.shape["norm"]),
        mesh=mesh,
        in_specs=(
            P("surf", None, None, None),
            P(),
            P(),
            P(),
            P("surf", None),
            P("surf", None),
            P("norm", "surf", None),
            P("norm", "surf", None, None),
            P("norm", "surf", None),
        ),
        out_specs=P("norm", "surf", None, None),
        check_vma=False,
    )
```

```python
import functools
import types

import jax
import jax.numpy as jnp
from jax import lax
from jax.experimental import pallas as pl
from jax.experimental.pallas import tpu as pltpu
from jax.sharding import PartitionSpec as P

SWEEPS = 3
LANES = 128
MESH = pl.DeviceIdType.MESH


def loop(count, body, init, unroll=4):
    if count % unroll:
        unroll = 1

    def outer(step, carry):
        for part in range(unroll):
            carry = body(step * unroll + part, carry)
        return carry

    return lax.fori_loop(0, count // unroll, outer, init)


def later(count, body, init, unroll=5):
    return loop(count - 1, lambda step, carry: body(step + 1, carry), init, unroll)


def mat_vec(matrix, vector):
    return [
        matrix[3 * a] * vector[0] + matrix[3 * a + 1] * vector[1] + matrix[3 * a + 2] * vector[2]
        for a in range(3)
    ]


def fold(start, matrix, vector):
    return [
        (start[a] + matrix[3 * a] * vector[0])
        + (matrix[3 * a + 1] * vector[1] + matrix[3 * a + 2] * vector[2])
        for a in range(3)
    ]


def mat_mat(left, right):
    return [
        left[3 * a] * right[b] + left[3 * a + 1] * right[3 + b] + left[3 * a + 2] * right[6 + b]
        for a in range(3)
        for b in range(3)
    ]


def added(left, right):
    return [a + b for a, b in zip(left, right)]


def planes(ref, index, count=3):
    return [ref[index, c] for c in range(count)]


def whole(ref, count=9):
    return [ref[c] for c in range(count)]


def rows(ref, count=3):
    return [ref[c : c + 1, :] for c in range(count)]


def put(ref, index, values):
    for c, value in enumerate(values):
        ref[index, c] = value


def put_rows(ref, values):
    for c, value in enumerate(values):
        ref[c : c + 1, :] = value


def kernel(
    surf_size, norm_size, names,
    amplitude_hbm, mode_patch_hbm, column_patch_hbm, wall_mask_hbm, offsets_hbm,
    modes_hbm, coupling_hbm, pivot_hbm, stiffness_hbm,
    out, *scratch,
):
    s = types.SimpleNamespace(**dict(zip(names, scratch)))
    modes, coupling, pivot, stiffness = s.modes, s.coupling, s.pivot, s.stiffness
    amplitude, mode_patch, column_patch = s.amplitude, s.mode_patch, s.column_patch
    wall_mask, offsets = s.wall_mask, s.offsets
    link, maps, part, got, wall, values, halo = s.link, s.maps, s.part, s.got, s.wall, s.values, s.halo
    S, N = surf_size, norm_size
    K, _, R, W = pivot.shape
    M = modes.shape[0]
    B = 2 * R
    blocks = modes.shape[2] // B
    chunks = W // LANES
    me = lax.axis_index("surf")
    place = lax.axis_index("norm")
    before = lax.rem(me + S - 1, S)
    after = lax.rem(me + 1, S)
    first, last = place == 0, place == N - 1
    inside = jnp.logical_not(jnp.logical_or(first, last))
    base = place * K

    def to(src, dst, send, recv, **target):
        return pltpu.make_async_remote_copy(
            src_ref=src, dst_ref=dst, send_sem=send, recv_sem=recv,
            device_id=target, device_id_type=MESH,
        )

    def toward(side):
        return after if side == 0 else before

    def settle(ref, sem):
        pltpu.make_async_copy(ref, ref, sem).wait()

    line_loads = [
        pltpu.make_async_copy(src, dst, s.load_sem.at[index])
        for index, (src, dst) in enumerate([
            (pivot_hbm, pivot), (coupling_hbm, coupling), (offsets_hbm, offsets),
        ])
    ]
    mode_loads = [
        pltpu.make_async_copy(src, dst, s.load_sem.at[3 + index])
        for index, (src, dst) in enumerate([
            (modes_hbm, modes), (column_patch_hbm, column_patch), (amplitude_hbm, amplitude),
            (mode_patch_hbm, mode_patch), (wall_mask_hbm, wall_mask), (stiffness_hbm, stiffness),
        ])
    ]
    for copy in line_loads + mode_loads:
        copy.start()

    barrier = pltpu.get_barrier_semaphore()

    def greet(**target):
        pl.semaphore_signal(barrier, inc=1, device_id=target, device_id_type=MESH)

    for hop in range(1, S):
        greet(surf=lax.rem(me + hop, S))
    for hop in range(1, N):
        other = lax.rem(place + hop, N)
        greet(norm=other)
        greet(surf=before, norm=other)
        greet(surf=after, norm=other)

    for copy in line_loads:
        copy.wait()
    cut = offsets[...]

    def link_step(k, carry):
        link[k] = jnp.where(cut == base + k, jnp.float32(0), coupling[k])
        return carry

    loop(K, link_step, 0)

    def lower_step(k, state):
        scaled = [p * link[k] for p in planes(pivot, k, 9)]
        put(s.rise, k, scaled)
        state = mat_mat(scaled, state)
        put(maps, k, state)
        return state

    first_map = [p * link[0] for p in planes(pivot, 0, 9)]
    put(maps, 0, first_map)
    ends = lax.fori_loop(1, K, lower_step, first_map)
    for c in range(9):
        s.end_map[c] = ends[c]

    def upper_step(step, state):
        k = K - 1 - step
        scaled = [p * link[k + 1] for p in planes(pivot, k, 9)]
        put(s.fall, k, scaled)
        state = added(planes(maps, k, 9), mat_mat(scaled, state[:9])) + mat_mat(scaled, state[9:])
        put(maps, k, state)
        return state

    top_state = ends + planes(pivot, K - 1, 9)
    put(maps, K - 1, top_state)
    top_state = lax.fori_loop(1, K, upper_step, top_state)
    for c in range(18):
        s.top_map[c] = link[0] * top_state[c]

    for copy in mode_loads:
        copy.wait()
    own_mode = me * M
    for b in range(blocks):
        patch = column_patch[b * B : (b + 1) * B, :]

        def mode_step(m, sums):
            weight = jnp.where(
                patch == mode_patch[own_mode + m], amplitude[own_mode + m], jnp.float32(0)
            )
            return [
                sums[c] + weight * modes[m, c, b * B : (b + 1) * B, :].astype(jnp.float32)
                for c in range(3)
            ]

        sums = loop(M, mode_step, [jnp.zeros((B, W), jnp.float32)] * 3)
        for c in range(3):
            for side in range(2):
                dest = 2 * b + side
                block = sums[c][side * R : (side + 1) * R]
                part[dest, c] = block
                part[(dest + 1) % S, 3, c : c + 1, :] = block[R - 1 : R]
                part[(dest - 1) % S, 3, 3 + c : 4 + c, :] = block[0:1]

    pl.semaphore_wait(barrier, S - 1 + 3 * (N - 1))

    def h_copy(q):
        return to(s.h_out.at[q], s.h_in.at[q], s.h_send.at[q], s.h_recv.at[q], norm=place - 1)

    full_copy = to(s.full_out, s.full_in, s.full_send, s.full_recv, norm=place - 1)

    def chunk(ref, q, start=0):
        return [ref[start + c, :, q * LANES : (q + 1) * LANES] for c in range(9)]

    def h_part(q):
        return [s.h_in[q, c].astype(jnp.float32) for c in range(9)]

    def h_full(sweep):
        if sweep > 0:
            return whole(s.full_in)
        pieces = [h_part(q) for q in range(chunks)]
        return [jnp.concatenate([p[c] for p in pieces], axis=1) for c in range(9)]

    def row_copy(slot, side, step):
        return to(
            s.row_out.at[slot, side], s.row_in.at[slot, side],
            s.row_send.at[slot], s.row_recv.at[slot],
            surf=toward(side), norm=place + step,
        )

    def send_rows(slot, step, values9):
        put_rows(s.row_out.at[slot, 0], [v[R - 1 : R] for v in values9])
        put_rows(s.row_out.at[slot, 1], [v[0:1] for v in values9])
        for side in range(2):
            row_copy(slot, side, step).start()

    UP, DOWN, ENDS, TOP = 0, N - 1, 0, N - 1

    def up_map(j):
        return to(s.up_out.at[j], s.up_in.at[j], s.up_send.at[j - 1], s.up_recv.at[j - 1], norm=place + 1)

    def down_map(j):
        return to(s.down_out.at[j], s.down_in.at[j], s.down_send.at[j - 1], s.down_recv.at[j - 1], norm=place - 1)

    def sends_up(j):
        return jnp.logical_and(place >= j, jnp.logical_not(last))

    def sends_down(j):
        return jnp.logical_and(N - 1 - place >= j, jnp.logical_not(first))

    @pl.when(last)
    def _():
        s.h_in[...] = jnp.zeros(s.h_in.shape, jnp.bfloat16)
        s.full_in[...] = jnp.zeros(s.full_in.shape, jnp.float32)
        s.row_in[TOP] = jnp.zeros(s.row_in.shape[1:], jnp.float32)
        for q in range(chunks):
            put(s.h_out, q, [v.astype(jnp.bfloat16) for v in chunk(s.top_map, q)])
            h_copy(q).start()

    def part_copy(hop):
        dest = lax.rem(me + hop, S)
        return to(part.at[dest], got.at[hop], s.part_send, s.part_recv, surf=dest)

    for hop in range(1, S):
        part_copy(hop).start()
    mask_up = to(wall_mask, s.mask_edge.at[0], s.mask_send, s.mask_recv, surf=after)
    mask_down = to(wall_mask, s.mask_edge.at[1], s.mask_send, s.mask_recv, surf=before)
    mask_up.start()
    mask_down.start()

    for j in range(1, min(2, N - 1)):

        @pl.when(sends_up(j))
        def _():
            value = whole(s.end_map)
            put(s.up_out, j, value)
            up_map(j).start()
            send_rows(UP + j, 1, value)

        @pl.when(sends_down(j))
        def _():
            value = [s.top_map[9 + c] for c in range(9)]
            put(s.down_out, j, value)
            down_map(j).start()
            send_rows(DOWN + j, -1, value)

    @pl.when(last)
    def _():
        send_rows(TOP, -1, whole(s.top_map))
        for c in range(9):
            s.full_out[c] = s.top_map[c]
        full_copy.start()

    send_rows(ENDS, 0, whole(s.end_map))

    def pack_step(k, carry):
        for c in range(18):
            value = maps[k, c]
            s.side_rows[0, c, pl.ds(k, 1), :] = value[R - 1 : R]
            s.side_rows[1, c, pl.ds(k, 1), :] = value[0:1]
        return carry

    loop(K, pack_step, 0, 2)

    def side_map_copy(side):
        return to(
            s.side_out.at[side], s.side_in.at[side], s.side_send, s.side_recv,
            surf=toward(side),
        )

    for side in range(2):
        for c in range(18):
            s.side_out[side, c] = s.side_rows[side, c].astype(jnp.bfloat16)
        side_map_copy(side).start()

    def relay():
        for q in range(chunks):
            h_copy(q).wait_recv()
            inner = mat_mat(h_part(q), chunk(s.end_map, q))
            value = added(chunk(s.top_map, q), mat_mat(chunk(s.top_map, q, 9), inner))
            put(s.h_out, q, [v.astype(jnp.bfloat16) for v in value])
            h_copy(q).start()
            for c in range(9):
                s.row_out[TOP, 0, c : c + 1, q * LANES : (q + 1) * LANES] = value[c][R - 1 : R]
                s.row_out[TOP, 1, c : c + 1, q * LANES : (q + 1) * LANES] = value[c][0:1]
        for side in range(2):
            row_copy(TOP, side, -1).start()

    def full_relay():
        full_copy.wait_recv()
        inner = mat_mat(whole(s.full_in), whole(s.end_map))
        outer = mat_mat([s.top_map[9 + c] for c in range(9)], inner)
        for c in range(9):
            s.full_out[c] = s.top_map[c] + outer[c]
        full_copy.start()

    early = jnp.logical_and(inside, place == N - 2)

    @pl.when(early)
    def _():
        relay()

    for j in range(2, N - 1):

        @pl.when(sends_up(j))
        def _():
            up_map(j - 1).wait_recv()
            value = mat_mat(whole(s.end_map), planes(s.up_in, j - 1, 9))
            put(s.up_out, j, value)
            up_map(j).start()
            send_rows(UP + j, 1, value)

        @pl.when(sends_down(j))
        def _():
            down_map(j - 1).wait_recv()
            value = mat_mat([s.top_map[9 + c] for c in range(9)], planes(s.down_in, j - 1, 9))
            put(s.down_out, j, value)
            down_map(j).start()
            send_rows(DOWN + j, -1, value)

    total = [part[me, c] for c in range(4)]
    settle(s.mask_edge, s.mask_recv)
    settle(got.at[pl.ds(0, S - 1)], s.part_recv)
    for hop in range(1, S):
        total = [total[c] + got[hop, c] for c in range(4)]
    mask = wall_mask[...].astype(jnp.float32)
    low_mask = s.mask_edge[0, R - 1 : R, :].astype(jnp.float32)
    high_mask = s.mask_edge[1, 0:1, :].astype(jnp.float32)
    row = lax.broadcasted_iota(jnp.int32, (R, W), 0)
    lane = lax.broadcasted_iota(jnp.int32, (R, W), 1)

    def around(x, low, high):
        nearby = jnp.where(row == 0, low, pltpu.roll(x, 1, 0))
        nearby += jnp.where(row == R - 1, high, pltpu.roll(x, R - 1, 0))
        nearby += jnp.where(lane == 0, jnp.float32(0), pltpu.roll(x, 1, 1))
        return nearby + jnp.where(lane == W - 1, jnp.float32(0), pltpu.roll(x, W - 1, 1))

    at_wall = jnp.where(first, jnp.float32(1), jnp.float32(0))
    for c in range(3):
        shift = total[c] * mask
        wall[c] = link[0] * shift * at_wall
        wall[3 + c] = around(
            shift, total[3][c : c + 1] * low_mask, total[3][3 + c : 4 + c] * high_mask
        )

    def edge_copy(sweep, side):
        return to(
            s.edge_out.at[sweep, side], s.edge_in.at[sweep, side],
            s.edge_send, s.edge_recv.at[sweep], surf=toward(side),
        )

    def up_copy(sweep, j):
        return to(
            s.f_out.at[sweep], s.z_in.at[sweep, place], s.z_send, s.z_recv.at[sweep],
            norm=place + j,
        )

    def down_copy(sweep, j):
        return to(
            s.o_out.at[sweep], s.z_in.at[sweep, place], s.z_send, s.z_recv.at[sweep],
            norm=place - j,
        )

    def up_edge(sweep, side, j):
        return to(
            s.fe_out.at[sweep, side], s.e_in.at[sweep, side, place],
            s.e_send, s.e_recv.at[sweep],
            surf=toward(side), norm=place + j,
        )

    def down_edge(sweep, side, j):
        return to(
            s.oe_out.at[sweep, side], s.e_in.at[sweep, side, place],
            s.e_send, s.e_recv.at[sweep],
            surf=toward(side), norm=place - j,
        )

    def change(send, sent, sweep, values3):
        for c in range(3):
            known = sent[c] if sweep > 0 else jnp.float32(0)
            step = (values3[c] - known).astype(jnp.bfloat16)
            send[sweep, c] = step
            sent[c] = known + step.astype(jnp.float32)

    def wide(ref, index):
        return [v.astype(jnp.float32) for v in planes(ref, index)]

    for sweep in range(SWEEPS):
        shared = sweep < SWEEPS - 1

        def source(k, sweep=sweep):
            if sweep == 0:
                blend = 1.0 - (base + k).astype(jnp.float32) / (K * N)
                factor = stiffness[k] * blend
                return [factor * wall[3 + c] for c in range(3)]
            return [
                stiffness[k]
                * around(out[k, c], halo[0, c, pl.ds(k, 1), :], halo[1, c, pl.ds(k, 1), :])
                for c in range(3)
            ]

        def forward(k, state):
            state = fold(
                mat_vec(planes(pivot, k, 9), source(k)), planes(s.rise, k, 9), state
            )
            put(values, k, state)
            return state

        start = mat_vec(
            planes(pivot, 0, 9), added(source(0), [wall[c] for c in range(3)])
        )
        put(values, 0, start)
        ends = later(K, forward, start, K - 1)
        if shared:
            put_rows(s.fe_out.at[sweep, 0], [v[R - 1 : R] for v in ends])
            put_rows(s.fe_out.at[sweep, 1], [v[0:1] for v in ends])
            for j in range(N - 1, 0, -1):

                @pl.when(place + j < N)
                def _():
                    for side in range(2):
                        up_edge(sweep, side, j).start()

        change(s.f_out, s.f_sent, sweep, ends)
        for j in range(N - 1, 0, -1):

            @pl.when(place + j < N)
            def _():
                up_copy(sweep, j).start()

        def keep(k, state):
            put(values, k, state)
            if shared:
                for c in range(3):
                    halo[0, c, pl.ds(k, 1), :] = state[c][R - 1 : R]
                    halo[1, c, pl.ds(k, 1), :] = state[c][0:1]

        def backward(step, state):
            k = K - 1 - step
            state = fold(planes(values, k), planes(s.fall, k, 9), state)
            keep(k, state)
            return state

        keep(K - 1, ends)
        tops = later(K, backward, ends, K - 1)

        if sweep == 0:

            @pl.when(jnp.logical_and(inside, jnp.logical_not(early)))
            def _():
                relay()

        @pl.when(jnp.logical_not(first))
        def _():
            top = added(
                [link[0] * v for v in tops],
                mat_vec([s.top_map[9 + c] for c in range(9)], mat_vec(h_full(sweep), ends)),
            )
            if shared:
                put_rows(s.oe_out.at[sweep, 0], [v[R - 1 : R] for v in top])
                put_rows(s.oe_out.at[sweep, 1], [v[0:1] for v in top])
                for j in range(N - 1, 0, -1):

                    @pl.when(place - j >= 0)
                    def _():
                        for side in range(2):
                            down_edge(sweep, side, j).start()

            change(s.o_out, s.o_sent, sweep, top)
            for j in range(N - 1, 0, -1):

                @pl.when(place - j >= 0)
                def _():
                    down_copy(sweep, j).start()

        if shared:
            for side in range(2):
                s.edge_out[sweep, side] = halo[side].astype(jnp.bfloat16)
                edge_copy(sweep, side).start()
                up_edge(sweep, side, 0).start()

        if sweep == 0:

            @pl.when(early)
            def _():
                full_relay()

            s.enter[...] = jnp.zeros(s.enter.shape, jnp.float32)

        settle(s.z_in.at[sweep, pl.ds(0, N - 1)], s.z_recv.at[sweep])
        for j in range(1, N):
            if sweep == 0 and j > 1:

                @pl.when(jnp.logical_and(last, place >= j))
                def _():
                    up_map(j - 1).wait_recv()

                @pl.when(jnp.logical_and(first, N - 1 - place >= j))
                def _():
                    down_map(j - 1).wait_recv()

            @pl.when(place - j >= 0)
            def _():
                moved = wide(s.z_in.at[sweep], place - j)
                if j > 1:
                    moved = mat_vec(planes(s.up_in, j - 1, 9), moved)
                put(s.enter, 0, added(planes(s.enter, 0), moved))

            @pl.when(place + j < N)
            def _():
                moved = wide(s.z_in.at[sweep], place + j)
                if j > 1:
                    moved = mat_vec(planes(s.down_in, j - 1, 9), moved)
                put(s.enter, 1, added(planes(s.enter, 1), moved))

        if sweep < 2:

            @pl.when(first)
            def _():
                if sweep == 0:
                    for q in range(chunks):
                        h_copy(q).wait_recv()
                else:
                    full_copy.wait_recv()

        entering = planes(s.enter, 0)
        state = added(ends, mat_vec(whole(s.end_map), entering))
        above = added(planes(s.enter, 1), mat_vec(h_full(sweep), state))

        def finish(k, carry):
            state = added(planes(values, k), mat_vec(planes(maps, k, 9), entering))
            state = added(state, mat_vec([maps[k, 9 + c] for c in range(9)], above))
            put(out, k, state)
            return carry

        loop(K, finish, 0, 8)

        if sweep == 0:

            @pl.when(jnp.logical_and(inside, jnp.logical_not(early)))
            def _():
                full_relay()

        if shared:
            if sweep == 0:
                settle(s.side_in, s.side_recv)
                settle(s.row_in.at[ENDS], s.row_recv.at[ENDS])

                @pl.when(jnp.logical_not(last))
                def _():
                    settle(s.row_in.at[TOP], s.row_recv.at[TOP])

                for j in range(2, N):

                    @pl.when(place >= j)
                    def _():
                        settle(s.row_in.at[UP + j - 1], s.row_recv.at[UP + j - 1])

                    @pl.when(N - 1 - place >= j)
                    def _():
                        settle(s.row_in.at[DOWN + j - 1], s.row_recv.at[DOWN + j - 1])

            settle(s.e_in.at[sweep], s.e_recv.at[sweep])
            settle(s.edge_in.at[sweep], s.edge_recv.at[sweep])
            s.enter_row[...] = jnp.zeros(s.enter_row.shape, jnp.float32)
            for j in range(1, N):

                @pl.when(place - j >= 0)
                def _():
                    for side in range(2):
                        moved = rows(s.e_in.at[sweep, side, place - j])
                        if j > 1:
                            moved = mat_vec(rows(s.row_in.at[UP + j - 1, side], 9), moved)
                        put_rows(s.enter_row.at[side, 0], added(rows(s.enter_row.at[side, 0]), moved))

                @pl.when(place + j < N)
                def _():
                    for side in range(2):
                        moved = rows(s.e_in.at[sweep, side, place + j])
                        if j > 1:
                            moved = mat_vec(rows(s.row_in.at[DOWN + j - 1, side], 9), moved)
                        put_rows(s.enter_row.at[side, 1], added(rows(s.enter_row.at[side, 1]), moved))

            for side in range(2):
                entered = rows(s.enter_row.at[side, 0])
                state = added(
                    rows(s.e_in.at[sweep, side, place]),
                    mat_vec(rows(s.row_in.at[ENDS, side], 9), entered),
                )
                higher = added(
                    rows(s.enter_row.at[side, 1]), mat_vec(rows(s.row_in.at[TOP, side], 9), state)
                )
                for c in range(3):
                    value = s.edge_in[sweep, side, c].astype(jnp.float32)
                    for b in range(3):
                        value += s.side_in[side, 3 * c + b].astype(jnp.float32) * entered[b]
                        value += s.side_in[side, 9 + 3 * c + b].astype(jnp.float32) * higher[b]
                    halo[side, c] = value

    settle(got.at[pl.ds(0, S - 1)], s.part_send)
    settle(s.mask_edge, s.mask_send)
    settle(s.side_out, s.side_send)
    settle(s.row_out.at[ENDS], s.row_send.at[ENDS])
    settle(s.z_in.at[:, pl.ds(0, N - 1)], s.z_send)
    settle(s.edge_out, s.edge_send)
    settle(s.e_in, s.e_send)

    @pl.when(jnp.logical_not(first))
    def _():
        full_copy.wait_send()
        for q in range(chunks):
            h_copy(q).wait_send()
        settle(s.row_out.at[TOP], s.row_send.at[TOP])

    for j in range(1, N - 1):

        @pl.when(sends_up(j))
        def _():
            up_map(j).wait_send()
            settle(s.row_out.at[UP + j], s.row_send.at[UP + j])

        @pl.when(sends_down(j))
        def _():
            down_map(j).wait_send()
            settle(s.row_out.at[DOWN + j], s.row_send.at[DOWN + j])


def per_device(
    surf_size, norm_size, mode_shapes, amplitude, mode_patch, column_patch, wall_mask, offsets,
    coupling, pivot_inv, stiffness,
):
    S, N = surf_size, norm_size
    modes = mode_shapes.transpose(0, 2, 1, 3)
    pivot = pivot_inv.transpose(0, 2, 1, 3)
    K, _, R, W = pivot.shape
    C = W // LANES
    f32, bf16 = jnp.float32, jnp.bfloat16
    vmem = pl.BlockSpec(memory_space=pltpu.VMEM)
    hbm = pl.BlockSpec(memory_space=pltpu.HBM)
    dma = pltpu.SemaphoreType.DMA

    def room(*shape):
        return pltpu.VMEM(shape, f32)

    def half(*shape):
        return pltpu.VMEM(shape, bf16)

    G = SWEEPS - 1
    scratch = dict(
        modes=half(*modes.shape),
        coupling=room(K, R, W),
        pivot=room(K, 9, R, W),
        stiffness=room(K, R, W),
        link=room(K, R, W),
        rise=room(K, 9, R, W),
        fall=room(K, 9, R, W),
        maps=room(K, 18, R, W),
        end_map=room(9, R, W),
        top_map=room(18, R, W),
        part=room(S, 4, R, W),
        got=room(S, 4, R, W),
        mask_edge=pltpu.VMEM((2, R, W), jnp.int32),
        wall=room(6, R, W),
        values=room(K, 3, R, W),
        enter=room(2, 3, R, W),
        enter_row=room(2, 2, 3, W),
        halo=room(2, 3, K, W),
        edge_out=half(G, 2, 3, K, W),
        edge_in=half(G, 2, 3, K, W),
        side_rows=room(2, 18, K, W),
        side_out=half(2, 18, K, W),
        side_in=half(2, 18, K, W),
        row_out=room(2 * N - 2, 2, 9, W),
        row_in=room(2 * N - 2, 2, 9, W),
        z_in=half(SWEEPS, N, 3, R, W),
        f_out=half(SWEEPS, 3, R, W),
        f_sent=room(3, R, W),
        o_out=half(SWEEPS, 3, R, W),
        o_sent=room(3, R, W),
        e_in=room(G, 2, N, 3, W),
        fe_out=room(G, 2, 3, W),
        oe_out=room(G, 2, 3, W),
        h_in=half(C, 9, R, LANES),
        h_out=half(C, 9, R, LANES),
        full_in=room(9, R, W),
        full_out=room(9, R, W),
        up_in=room(N, 9, R, W),
        up_out=room(N, 9, R, W),
        down_in=room(N, 9, R, W),
        down_out=room(N, 9, R, W),
        load_sem=dma((9,)),
        amplitude=pltpu.SMEM(amplitude.shape, f32),
        mode_patch=pltpu.SMEM(mode_patch.shape, jnp.int32),
        column_patch=pltpu.VMEM(column_patch.shape, jnp.int32),
        wall_mask=pltpu.VMEM(wall_mask.shape, jnp.int32),
        offsets=pltpu.VMEM(offsets.shape, jnp.int32),
    )
    sems = dict(
        part=(), mask=(), h=(C,), full=(), row=(2 * N - 2,), side=(), up=(max(N - 2, 1),),
        down=(max(N - 2, 1),), z=(SWEEPS,), e=(G,), edge=(G,),
    )
    for name, shape in sems.items():
        scratch[name + "_send"] = dma(shape) if shape and name not in ("z", "e", "edge") else dma
        scratch[name + "_recv"] = dma(shape) if shape else dma
    out = pl.pallas_call(
        functools.partial(kernel, S, N, tuple(scratch)),
        out_shape=pltpu.VMEM((K, 3, R, W), f32),
        in_specs=[hbm] * 9,
        out_specs=vmem,
        scratch_shapes=list(scratch.values()),
        compiler_params=pltpu.CompilerParams(
            collective_id=0, has_side_effects=True, vmem_limit_bytes=62 * 1024 * 1024
        ),
        name="line_sweeps",
    )(amplitude, mode_patch, column_patch, wall_mask, offsets, modes, coupling, pivot, stiffness)
    return out.transpose(0, 2, 1, 3)


def solution(mesh):
    return jax.shard_map(
        functools.partial(per_device, mesh.shape["surf"], mesh.shape["norm"]),
        mesh=mesh,
        in_specs=(
            P("surf", None, None, None),
            P(),
            P(),
            P(),
            P("surf", None),
            P("surf", None),
            P("norm", "surf", None),
            P("norm", "surf", None, None),
            P("norm", "surf", None),
        ),
        out_specs=P("norm", "surf", None, None),
        check_vma=False,
    )
```

```python
import functools
import types

import jax
import jax.numpy as jnp
from jax import lax
from jax.experimental import pallas as pl
from jax.experimental.pallas import tpu as pltpu
from jax.sharding import PartitionSpec as P

SWEEPS = 3
LANES = 128
MESH = pl.DeviceIdType.MESH


def loop(count, body, init, unroll=4):
    if count % unroll:
        unroll = 1

    def outer(step, carry):
        for part in range(unroll):
            carry = body(step * unroll + part, carry)
        return carry

    return lax.fori_loop(0, count // unroll, outer, init)


def later(count, body, init, unroll=5):
    return loop(count - 1, lambda step, carry: body(step + 1, carry), init, unroll)


def mat_vec(matrix, vector):
    return [
        matrix[3 * a] * vector[0] + matrix[3 * a + 1] * vector[1] + matrix[3 * a + 2] * vector[2]
        for a in range(3)
    ]


def fold(start, matrix, vector):
    return [
        (start[a] + matrix[3 * a] * vector[0])
        + (matrix[3 * a + 1] * vector[1] + matrix[3 * a + 2] * vector[2])
        for a in range(3)
    ]


def mat_mat(left, right):
    return [
        left[3 * a] * right[b] + left[3 * a + 1] * right[3 + b] + left[3 * a + 2] * right[6 + b]
        for a in range(3)
        for b in range(3)
    ]


def added(left, right):
    return [a + b for a, b in zip(left, right)]


def planes(ref, index, count=3):
    return [ref[index, c] for c in range(count)]


def whole(ref, count=9):
    return [ref[c] for c in range(count)]


def rows(ref, count=3):
    return [ref[c : c + 1, :] for c in range(count)]


def put(ref, index, values):
    for c, value in enumerate(values):
        ref[index, c] = value


def put_rows(ref, values):
    for c, value in enumerate(values):
        ref[c : c + 1, :] = value


def kernel(
    surf_size, norm_size, names,
    amplitude_hbm, mode_patch_hbm, column_patch_hbm, wall_mask_hbm, offsets_hbm,
    modes_hbm, coupling_hbm, pivot_hbm, stiffness_hbm,
    out, *scratch,
):
    s = types.SimpleNamespace(**dict(zip(names, scratch)))
    modes, coupling, pivot, stiffness = s.modes, s.coupling, s.pivot, s.stiffness
    amplitude, mode_patch, column_patch = s.amplitude, s.mode_patch, s.column_patch
    wall_mask, offsets = s.wall_mask, s.offsets
    link, maps, part, got, wall, values, halo = s.link, s.maps, s.part, s.got, s.wall, s.values, s.halo
    S, N = surf_size, norm_size
    K, _, R, W = pivot.shape
    M = modes.shape[0]
    B = 2 * R
    blocks = modes.shape[2] // B
    chunks = W // LANES
    me = lax.axis_index("surf")
    place = lax.axis_index("norm")
    before = lax.rem(me + S - 1, S)
    after = lax.rem(me + 1, S)
    first, last = place == 0, place == N - 1
    inside = jnp.logical_not(jnp.logical_or(first, last))
    base = place * K

    def to(src, dst, send, recv, **target):
        return pltpu.make_async_remote_copy(
            src_ref=src, dst_ref=dst, send_sem=send, recv_sem=recv,
            device_id=target, device_id_type=MESH,
        )

    def toward(side):
        return after if side == 0 else before

    def settle(ref, sem):
        pltpu.make_async_copy(ref, ref, sem).wait()

    line_loads = [
        pltpu.make_async_copy(src, dst, s.load_sem.at[index])
        for index, (src, dst) in enumerate([
            (pivot_hbm, pivot), (coupling_hbm, coupling), (offsets_hbm, offsets),
        ])
    ]
    mode_loads = [
        pltpu.make_async_copy(src, dst, s.load_sem.at[3 + index])
        for index, (src, dst) in enumerate([
            (modes_hbm, modes), (column_patch_hbm, column_patch), (amplitude_hbm, amplitude),
            (mode_patch_hbm, mode_patch), (wall_mask_hbm, wall_mask), (stiffness_hbm, stiffness),
        ])
    ]
    for copy in line_loads + mode_loads:
        copy.start()

    barrier = pltpu.get_barrier_semaphore()

    def greet(**target):
        pl.semaphore_signal(barrier, inc=1, device_id=target, device_id_type=MESH)

    for hop in range(1, S):
        greet(surf=lax.rem(me + hop, S))
    for hop in range(1, N):
        other = lax.rem(place + hop, N)
        greet(norm=other)
        greet(surf=before, norm=other)
        greet(surf=after, norm=other)

    for copy in line_loads:
        copy.wait()
    cut = offsets[...]

    def link_step(k, carry):
        link[k] = jnp.where(cut == base + k, jnp.float32(0), coupling[k])
        return carry

    loop(K, link_step, 0)

    def lower_step(k, state):
        scaled = [p * link[k] for p in planes(pivot, k, 9)]
        put(s.rise, k, scaled)
        state = mat_mat(scaled, state)
        put(maps, k, state)
        return state

    first_map = [p * link[0] for p in planes(pivot, 0, 9)]
    put(maps, 0, first_map)
    ends = lax.fori_loop(1, K, lower_step, first_map)
    for c in range(9):
        s.end_map[c] = ends[c]

    def upper_step(step, state):
        k = K - 1 - step
        scaled = [p * link[k + 1] for p in planes(pivot, k, 9)]
        put(s.fall, k, scaled)
        state = added(planes(maps, k, 9), mat_mat(scaled, state[:9])) + mat_mat(scaled, state[9:])
        put(maps, k, state)
        return state

    top_state = ends + planes(pivot, K - 1, 9)
    put(maps, K - 1, top_state)
    top_state = lax.fori_loop(1, K, upper_step, top_state)
    for c in range(18):
        s.top_map[c] = link[0] * top_state[c]

    for copy in mode_loads:
        copy.wait()
    own_mode = me * M
    for b in range(blocks):
        patch = column_patch[b * B : (b + 1) * B, :]

        def mode_step(m, sums):
            weight = jnp.where(
                patch == mode_patch[own_mode + m], amplitude[own_mode + m], jnp.float32(0)
            )
            return [
                sums[c] + weight * modes[m, c, b * B : (b + 1) * B, :].astype(jnp.float32)
                for c in range(3)
            ]

        sums = loop(M, mode_step, [jnp.zeros((B, W), jnp.float32)] * 3)
        for c in range(3):
            for side in range(2):
                dest = 2 * b + side
                block = sums[c][side * R : (side + 1) * R]
                part[dest, c] = block
                part[(dest + 1) % S, 3, c : c + 1, :] = block[R - 1 : R]
                part[(dest - 1) % S, 3, 3 + c : 4 + c, :] = block[0:1]

    pl.semaphore_wait(barrier, S - 1 + 3 * (N - 1))

    def h_copy(q):
        return to(s.h_out.at[q], s.h_in.at[q], s.h_send.at[q], s.h_recv.at[q], norm=place - 1)

    full_copy = to(s.full_out, s.full_in, s.full_send, s.full_recv, norm=place - 1)

    def chunk(ref, q, start=0):
        return [ref[start + c, :, q * LANES : (q + 1) * LANES] for c in range(9)]

    def h_part(q):
        return [s.h_in[q, c].astype(jnp.float32) for c in range(9)]

    def h_full(sweep):
        if sweep > 0:
            return whole(s.full_in)
        pieces = [h_part(q) for q in range(chunks)]
        return [jnp.concatenate([p[c] for p in pieces], axis=1) for c in range(9)]

    def row_copy(slot, side, step):
        return to(
            s.row_out.at[slot, side], s.row_in.at[slot, side],
            s.row_send.at[slot], s.row_recv.at[slot],
            surf=toward(side), norm=place + step,
        )

    def send_rows(slot, step, values9):
        put_rows(s.row_out.at[slot, 0], [v[R - 1 : R] for v in values9])
        put_rows(s.row_out.at[slot, 1], [v[0:1] for v in values9])
        for side in range(2):
            row_copy(slot, side, step).start()

    UP, DOWN, ENDS, TOP = 0, N - 1, 0, N - 1

    def up_map(j):
        return to(s.up_out.at[j], s.up_in.at[j], s.up_send.at[j - 1], s.up_recv.at[j - 1], norm=place + 1)

    def down_map(j):
        return to(s.down_out.at[j], s.down_in.at[j], s.down_send.at[j - 1], s.down_recv.at[j - 1], norm=place - 1)

    def sends_up(j):
        return jnp.logical_and(place >= j, jnp.logical_not(last))

    def sends_down(j):
        return jnp.logical_and(N - 1 - place >= j, jnp.logical_not(first))

    def part_copy(hop):
        dest = lax.rem(me + hop, S)
        return to(part.at[dest], got.at[hop], s.part_send, s.part_recv, surf=dest)

    for hop in range(1, S):
        part_copy(hop).start()
    mask_up = to(wall_mask, s.mask_edge.at[0], s.mask_send, s.mask_recv, surf=after)
    mask_down = to(wall_mask, s.mask_edge.at[1], s.mask_send, s.mask_recv, surf=before)
    mask_up.start()
    mask_down.start()

    @pl.when(last)
    def _():
        s.h_in[...] = jnp.zeros(s.h_in.shape, jnp.bfloat16)
        s.full_in[...] = jnp.zeros(s.full_in.shape, jnp.float32)
        s.row_in[TOP] = jnp.zeros(s.row_in.shape[1:], jnp.float32)
        for q in range(chunks):
            put(s.h_out, q, [v.astype(jnp.bfloat16) for v in chunk(s.top_map, q)])
            h_copy(q).start()

    for j in range(1, min(2, N - 1)):

        @pl.when(sends_up(j))
        def _():
            value = whole(s.end_map)
            put(s.up_out, j, value)
            up_map(j).start()
            send_rows(UP + j, 1, value)

        @pl.when(sends_down(j))
        def _():
            value = [s.top_map[9 + c] for c in range(9)]
            put(s.down_out, j, value)
            down_map(j).start()
            send_rows(DOWN + j, -1, value)

    @pl.when(last)
    def _():
        send_rows(TOP, -1, whole(s.top_map))
        for c in range(9):
            s.full_out[c] = s.top_map[c]
        full_copy.start()

    send_rows(ENDS, 0, whole(s.end_map))

    def relay():
        for q in range(chunks):
            h_copy(q).wait_recv()
            inner = mat_mat(h_part(q), chunk(s.end_map, q))
            value = added(chunk(s.top_map, q), mat_mat(chunk(s.top_map, q, 9), inner))
            put(s.h_out, q, [v.astype(jnp.bfloat16) for v in value])
            h_copy(q).start()
            for c in range(9):
                s.row_out[TOP, 0, c : c + 1, q * LANES : (q + 1) * LANES] = value[c][R - 1 : R]
                s.row_out[TOP, 1, c : c + 1, q * LANES : (q + 1) * LANES] = value[c][0:1]
        for side in range(2):
            row_copy(TOP, side, -1).start()

    def full_relay():
        full_copy.wait_recv()
        inner = mat_mat(whole(s.full_in), whole(s.end_map))
        outer = mat_mat([s.top_map[9 + c] for c in range(9)], inner)
        for c in range(9):
            s.full_out[c] = s.top_map[c] + outer[c]
        full_copy.start()

    early = jnp.logical_and(inside, place == N - 2)

    @pl.when(early)
    def _():
        relay()

    for j in range(2, N - 1):

        @pl.when(sends_up(j))
        def _():
            up_map(j - 1).wait_recv()
            value = mat_mat(whole(s.end_map), planes(s.up_in, j - 1, 9))
            put(s.up_out, j, value)
            up_map(j).start()
            send_rows(UP + j, 1, value)

        @pl.when(sends_down(j))
        def _():
            down_map(j - 1).wait_recv()
            value = mat_mat([s.top_map[9 + c] for c in range(9)], planes(s.down_in, j - 1, 9))
            put(s.down_out, j, value)
            down_map(j).start()
            send_rows(DOWN + j, -1, value)

    def pack_step(k, carry):
        for c in range(18):
            value = maps[k, c]
            s.side_rows[0, c, pl.ds(k, 1), :] = value[R - 1 : R]
            s.side_rows[1, c, pl.ds(k, 1), :] = value[0:1]
        return carry

    loop(K, pack_step, 0, 2)

    def side_map_copy(side):
        return to(
            s.side_out.at[side], s.side_in.at[side], s.side_send, s.side_recv,
            surf=toward(side),
        )

    for side in range(2):
        for c in range(18):
            s.side_out[side, c] = s.side_rows[side, c].astype(jnp.bfloat16)
        side_map_copy(side).start()

    total = [part[me, c] for c in range(4)]
    settle(s.mask_edge, s.mask_recv)
    settle(got.at[pl.ds(0, S - 1)], s.part_recv)
    for hop in range(1, S):
        total = [total[c] + got[hop, c] for c in range(4)]
    mask = wall_mask[...].astype(jnp.float32)
    low_mask = s.mask_edge[0, R - 1 : R, :].astype(jnp.float32)
    high_mask = s.mask_edge[1, 0:1, :].astype(jnp.float32)
    row = lax.broadcasted_iota(jnp.int32, (R, W), 0)
    lane = lax.broadcasted_iota(jnp.int32, (R, W), 1)

    def around(x, low, high):
        nearby = jnp.where(row == 0, low, pltpu.roll(x, 1, 0))
        nearby += jnp.where(row == R - 1, high, pltpu.roll(x, R - 1, 0))
        nearby += jnp.where(lane == 0, jnp.float32(0), pltpu.roll(x, 1, 1))
        return nearby + jnp.where(lane == W - 1, jnp.float32(0), pltpu.roll(x, W - 1, 1))

    at_wall = jnp.where(first, jnp.float32(1), jnp.float32(0))
    for c in range(3):
        shift = total[c] * mask
        wall[c] = link[0] * shift * at_wall
        wall[3 + c] = around(
            shift, total[3][c : c + 1] * low_mask, total[3][3 + c : 4 + c] * high_mask
        )

    def edge_copy(sweep, side):
        return to(
            s.edge_out.at[sweep, side], s.edge_in.at[sweep, side],
            s.edge_send, s.edge_recv.at[sweep], surf=toward(side),
        )

    def up_copy(sweep, j):
        return to(
            s.f_out.at[sweep], s.z_in.at[sweep, place], s.z_send, s.z_recv.at[sweep],
            norm=place + j,
        )

    def down_copy(sweep, j):
        return to(
            s.o_out.at[sweep], s.z_in.at[sweep, place], s.z_send, s.z_recv.at[sweep],
            norm=place - j,
        )

    def up_edge(sweep, side, j):
        return to(
            s.fe_out.at[sweep, side], s.e_in.at[sweep, side, place],
            s.e_send, s.e_recv.at[sweep],
            surf=toward(side), norm=place + j,
        )

    def down_edge(sweep, side, j):
        return to(
            s.oe_out.at[sweep, side], s.e_in.at[sweep, side, place],
            s.e_send, s.e_recv.at[sweep],
            surf=toward(side), norm=place - j,
        )

    def change(send, sent, sweep, values3):
        for c in range(3):
            known = sent[c] if sweep > 0 else jnp.float32(0)
            step = (values3[c] - known).astype(jnp.bfloat16)
            send[sweep, c] = step
            sent[c] = known + step.astype(jnp.float32)

    def lower_place(j):
        return jnp.maximum(place - j, 0)

    def upper_place(j):
        return jnp.minimum(place + j, N - 1)

    def only(valid, values3):
        return [lax.select(valid, v, jnp.zeros_like(v)) for v in values3]

    def wide(ref, index):
        return [v.astype(jnp.float32) for v in planes(ref, index)]

    for sweep in range(SWEEPS):
        shared = sweep < SWEEPS - 1

        def source(k, sweep=sweep):
            if sweep == 0:
                blend = 1.0 - (base + k).astype(jnp.float32) / (K * N)
                factor = stiffness[k] * blend
                return [factor * wall[3 + c] for c in range(3)]
            return [
                stiffness[k]
                * around(out[k, c], halo[0, c, pl.ds(k, 1), :], halo[1, c, pl.ds(k, 1), :])
                for c in range(3)
            ]

        def forward(k, state):
            state = fold(
                mat_vec(planes(pivot, k, 9), source(k)), planes(s.rise, k, 9), state
            )
            put(values, k, state)
            return state

        start = mat_vec(
            planes(pivot, 0, 9), added(source(0), [wall[c] for c in range(3)])
        )
        put(values, 0, start)
        ends = later(K, forward, start, K - 1)
        if shared:
            put_rows(s.fe_out.at[sweep, 0], [v[R - 1 : R] for v in ends])
            put_rows(s.fe_out.at[sweep, 1], [v[0:1] for v in ends])
            for j in range(N - 1, 0, -1):

                @pl.when(place + j < N)
                def _():
                    for side in range(2):
                        up_edge(sweep, side, j).start()

        change(s.f_out, s.f_sent, sweep, ends)
        for j in range(N - 1, 0, -1):

            @pl.when(place + j < N)
            def _():
                up_copy(sweep, j).start()

        def keep(k, state):
            put(values, k, state)
            if shared:
                for c in range(3):
                    halo[0, c, pl.ds(k, 1), :] = state[c][R - 1 : R]
                    halo[1, c, pl.ds(k, 1), :] = state[c][0:1]

        def backward(step, state):
            k = K - 1 - step
            state = fold(planes(values, k), planes(s.fall, k, 9), state)
            keep(k, state)
            return state

        keep(K - 1, ends)
        tops = later(K, backward, ends, K - 1)

        if sweep == 0:

            @pl.when(jnp.logical_and(inside, jnp.logical_not(early)))
            def _():
                relay()

        @pl.when(jnp.logical_not(first))
        def _():
            top = added(
                [link[0] * v for v in tops],
                mat_vec([s.top_map[9 + c] for c in range(9)], mat_vec(h_full(sweep), ends)),
            )
            if shared:
                put_rows(s.oe_out.at[sweep, 0], [v[R - 1 : R] for v in top])
                put_rows(s.oe_out.at[sweep, 1], [v[0:1] for v in top])
                for j in range(N - 1, 0, -1):

                    @pl.when(place - j >= 0)
                    def _():
                        for side in range(2):
                            down_edge(sweep, side, j).start()

            change(s.o_out, s.o_sent, sweep, top)
            for j in range(N - 1, 0, -1):

                @pl.when(place - j >= 0)
                def _():
                    down_copy(sweep, j).start()

        if shared:
            for side in range(2):
                s.edge_out[sweep, side] = halo[side].astype(jnp.bfloat16)
                edge_copy(sweep, side).start()
                up_edge(sweep, side, 0).start()

        if sweep == 0:

            @pl.when(early)
            def _():
                full_relay()


        settle(s.z_in.at[sweep, pl.ds(0, N - 1)], s.z_recv.at[sweep])
        for j in range(1, N):
            if sweep == 0 and j > 1:

                @pl.when(jnp.logical_and(last, place >= j))
                def _():
                    up_map(j - 1).wait_recv()

                @pl.when(jnp.logical_and(first, N - 1 - place >= j))
                def _():
                    down_map(j - 1).wait_recv()

        rising = planes(s.enter, 0) if sweep > 0 else [jnp.zeros((R, W), jnp.float32)] * 3
        falling = planes(s.enter, 1) if sweep > 0 else [jnp.zeros((R, W), jnp.float32)] * 3
        for j in range(1, N):
            moved = wide(s.z_in.at[sweep], lower_place(j))
            if j > 1:
                moved = mat_vec(planes(s.up_in, j - 1, 9), moved)
            rising = added(rising, only(place >= j, moved))
            moved = wide(s.z_in.at[sweep], upper_place(j))
            if j > 1:
                moved = mat_vec(planes(s.down_in, j - 1, 9), moved)
            falling = added(falling, only(place + j < N, moved))
        put(s.enter, 0, rising)
        put(s.enter, 1, falling)

        if sweep < 2:

            @pl.when(first)
            def _():
                if sweep == 0:
                    for q in range(chunks):
                        h_copy(q).wait_recv()
                else:
                    full_copy.wait_recv()

        entering = rising
        state = added(ends, mat_vec(whole(s.end_map), entering))
        above = added(falling, mat_vec(h_full(sweep), state))

        def finish(k, carry):
            state = added(planes(values, k), mat_vec(planes(maps, k, 9), entering))
            state = added(state, mat_vec([maps[k, 9 + c] for c in range(9)], above))
            put(out, k, state)
            return carry

        loop(K, finish, 0, 8)

        if sweep == 0:

            @pl.when(jnp.logical_and(inside, jnp.logical_not(early)))
            def _():
                full_relay()

        if shared:
            if sweep == 0:
                settle(s.side_in, s.side_recv)
                settle(s.row_in.at[ENDS], s.row_recv.at[ENDS])

                @pl.when(jnp.logical_not(last))
                def _():
                    settle(s.row_in.at[TOP], s.row_recv.at[TOP])

                for j in range(2, N):

                    @pl.when(place >= j)
                    def _():
                        settle(s.row_in.at[UP + j - 1], s.row_recv.at[UP + j - 1])

                    @pl.when(N - 1 - place >= j)
                    def _():
                        settle(s.row_in.at[DOWN + j - 1], s.row_recv.at[DOWN + j - 1])

            settle(s.e_in.at[sweep], s.e_recv.at[sweep])
            settle(s.edge_in.at[sweep], s.edge_recv.at[sweep])
            for side in range(2):
                entered = [jnp.zeros((1, W), jnp.float32)] * 3
                leaving = [jnp.zeros((1, W), jnp.float32)] * 3
                for j in range(1, N):
                    moved = rows(s.e_in.at[sweep, side, lower_place(j)])
                    if j > 1:
                        moved = mat_vec(rows(s.row_in.at[UP + j - 1, side], 9), moved)
                    entered = added(entered, only(place >= j, moved))
                    moved = rows(s.e_in.at[sweep, side, upper_place(j)])
                    if j > 1:
                        moved = mat_vec(rows(s.row_in.at[DOWN + j - 1, side], 9), moved)
                    leaving = added(leaving, only(place + j < N, moved))
                state = added(
                    rows(s.e_in.at[sweep, side, place]),
                    mat_vec(rows(s.row_in.at[ENDS, side], 9), entered),
                )
                higher = added(
                    leaving, mat_vec(rows(s.row_in.at[TOP, side], 9), state)
                )
                for c in range(3):
                    value = s.edge_in[sweep, side, c].astype(jnp.float32)
                    for b in range(3):
                        value += s.side_in[side, 3 * c + b].astype(jnp.float32) * entered[b]
                        value += s.side_in[side, 9 + 3 * c + b].astype(jnp.float32) * higher[b]
                    halo[side, c] = value

    settle(got.at[pl.ds(0, S - 1)], s.part_send)
    settle(s.mask_edge, s.mask_send)
    settle(s.side_out, s.side_send)
    settle(s.row_out.at[ENDS], s.row_send.at[ENDS])
    settle(s.z_in.at[:, pl.ds(0, N - 1)], s.z_send)
    settle(s.edge_out, s.edge_send)
    settle(s.e_in, s.e_send)

    @pl.when(jnp.logical_not(first))
    def _():
        full_copy.wait_send()
        for q in range(chunks):
            h_copy(q).wait_send()
        settle(s.row_out.at[TOP], s.row_send.at[TOP])

    for j in range(1, N - 1):

        @pl.when(sends_up(j))
        def _():
            up_map(j).wait_send()
            settle(s.row_out.at[UP + j], s.row_send.at[UP + j])

        @pl.when(sends_down(j))
        def _():
            down_map(j).wait_send()
            settle(s.row_out.at[DOWN + j], s.row_send.at[DOWN + j])


def per_device(
    surf_size, norm_size, mode_shapes, amplitude, mode_patch, column_patch, wall_mask, offsets,
    coupling, pivot_inv, stiffness,
):
    S, N = surf_size, norm_size
    modes = mode_shapes.transpose(0, 2, 1, 3)
    pivot = pivot_inv.transpose(0, 2, 1, 3)
    K, _, R, W = pivot.shape
    C = W // LANES
    f32, bf16 = jnp.float32, jnp.bfloat16
    vmem = pl.BlockSpec(memory_space=pltpu.VMEM)
    hbm = pl.BlockSpec(memory_space=pltpu.HBM)
    dma = pltpu.SemaphoreType.DMA

    def room(*shape):
        return pltpu.VMEM(shape, f32)

    def half(*shape):
        return pltpu.VMEM(shape, bf16)

    G = SWEEPS - 1
    scratch = dict(
        modes=half(*modes.shape),
        coupling=room(K, R, W),
        pivot=room(K, 9, R, W),
        stiffness=room(K, R, W),
        link=room(K, R, W),
        rise=room(K, 9, R, W),
        fall=room(K, 9, R, W),
        maps=room(K, 18, R, W),
        end_map=room(9, R, W),
        top_map=room(18, R, W),
        part=room(S, 4, R, W),
        got=room(S, 4, R, W),
        mask_edge=pltpu.VMEM((2, R, W), jnp.int32),
        wall=room(6, R, W),
        values=room(K, 3, R, W),
        enter=room(2, 3, R, W),
        halo=room(2, 3, K, W),
        edge_out=half(G, 2, 3, K, W),
        edge_in=half(G, 2, 3, K, W),
        side_rows=room(2, 18, K, W),
        side_out=half(2, 18, K, W),
        side_in=half(2, 18, K, W),
        row_out=room(2 * N - 2, 2, 9, W),
        row_in=room(2 * N - 2, 2, 9, W),
        z_in=half(SWEEPS, N, 3, R, W),
        f_out=half(SWEEPS, 3, R, W),
        f_sent=room(3, R, W),
        o_out=half(SWEEPS, 3, R, W),
        o_sent=room(3, R, W),
        e_in=room(G, 2, N, 3, W),
        fe_out=room(G, 2, 3, W),
        oe_out=room(G, 2, 3, W),
        h_in=half(C, 9, R, LANES),
        h_out=half(C, 9, R, LANES),
        full_in=room(9, R, W),
        full_out=room(9, R, W),
        up_in=room(N, 9, R, W),
        up_out=room(N, 9, R, W),
        down_in=room(N, 9, R, W),
        down_out=room(N, 9, R, W),
        load_sem=dma((9,)),
        amplitude=pltpu.SMEM(amplitude.shape, f32),
        mode_patch=pltpu.SMEM(mode_patch.shape, jnp.int32),
        column_patch=pltpu.VMEM(column_patch.shape, jnp.int32),
        wall_mask=pltpu.VMEM(wall_mask.shape, jnp.int32),
        offsets=pltpu.VMEM(offsets.shape, jnp.int32),
    )
    sems = dict(
        part=(), mask=(), h=(C,), full=(), row=(2 * N - 2,), side=(), up=(max(N - 2, 1),),
        down=(max(N - 2, 1),), z=(SWEEPS,), e=(G,), edge=(G,),
    )
    for name, shape in sems.items():
        scratch[name + "_send"] = dma(shape) if shape and name not in ("z", "e", "edge") else dma
        scratch[name + "_recv"] = dma(shape) if shape else dma
    out = pl.pallas_call(
        functools.partial(kernel, S, N, tuple(scratch)),
        out_shape=pltpu.VMEM((K, 3, R, W), f32),
        in_specs=[hbm] * 9,
        out_specs=vmem,
        scratch_shapes=list(scratch.values()),
        compiler_params=pltpu.CompilerParams(
            collective_id=0, has_side_effects=True, vmem_limit_bytes=62 * 1024 * 1024
        ),
        name="line_sweeps",
    )(amplitude, mode_patch, column_patch, wall_mask, offsets, modes, coupling, pivot, stiffness)
    return out.transpose(0, 2, 1, 3)


def solution(mesh):
    return jax.shard_map(
        functools.partial(per_device, mesh.shape["surf"], mesh.shape["norm"]),
        mesh=mesh,
        in_specs=(
            P("surf", None, None, None),
            P(),
            P(),
            P(),
            P("surf", None),
            P("surf", None),
            P("norm", "surf", None),
            P("norm", "surf", None, None),
            P("norm", "surf", None),
        ),
        out_specs=P("norm", "surf", None, None),
        check_vma=False,
    )
```

```python
import functools
import types

import jax
import jax.numpy as jnp
from jax import lax
from jax.experimental import pallas as pl
from jax.experimental.pallas import tpu as pltpu
from jax.sharding import PartitionSpec as P

SWEEPS = 3
LANES = 128
MESH = pl.DeviceIdType.MESH


def loop(count, body, init, unroll=4):
    if count % unroll:
        unroll = 1

    def outer(step, carry):
        for part in range(unroll):
            carry = body(step * unroll + part, carry)
        return carry

    return lax.fori_loop(0, count // unroll, outer, init)


def later(count, body, init, unroll=5):
    return loop(count - 1, lambda step, carry: body(step + 1, carry), init, unroll)


def mat_vec(matrix, vector):
    return [
        matrix[3 * a] * vector[0] + matrix[3 * a + 1] * vector[1] + matrix[3 * a + 2] * vector[2]
        for a in range(3)
    ]


def fold(start, matrix, vector):
    return [
        (start[a] + matrix[3 * a] * vector[0])
        + (matrix[3 * a + 1] * vector[1] + matrix[3 * a + 2] * vector[2])
        for a in range(3)
    ]


def mat_mat(left, right):
    return [
        left[3 * a] * right[b] + left[3 * a + 1] * right[3 + b] + left[3 * a + 2] * right[6 + b]
        for a in range(3)
        for b in range(3)
    ]


def added(left, right):
    return [a + b for a, b in zip(left, right)]


def planes(ref, index, count=3):
    return [ref[index, c] for c in range(count)]


def whole(ref, count=9):
    return [ref[c] for c in range(count)]


def rows(ref, count=3):
    return [ref[c : c + 1, :] for c in range(count)]


def put(ref, index, values):
    for c, value in enumerate(values):
        ref[index, c] = value


def put_rows(ref, values):
    for c, value in enumerate(values):
        ref[c : c + 1, :] = value


def kernel(
    surf_size, norm_size, names,
    amplitude_hbm, mode_patch_hbm, column_patch_hbm, wall_mask_hbm, offsets_hbm,
    modes_hbm, coupling_hbm, pivot_hbm, stiffness_hbm,
    out, *scratch,
):
    s = types.SimpleNamespace(**dict(zip(names, scratch)))
    modes, coupling, pivot, stiffness = s.modes, s.coupling, s.pivot, s.stiffness
    amplitude, mode_patch, column_patch = s.amplitude, s.mode_patch, s.column_patch
    wall_mask, offsets = s.wall_mask, s.offsets
    link, maps, part, got, wall, values, halo = s.link, s.maps, s.part, s.got, s.wall, s.values, s.halo
    S, N = surf_size, norm_size
    K, _, R, W = pivot.shape
    M = modes.shape[0]
    B = 2 * R
    blocks = modes.shape[2] // B
    chunks = W // LANES
    me = lax.axis_index("surf")
    place = lax.axis_index("norm")
    before = lax.rem(me + S - 1, S)
    after = lax.rem(me + 1, S)
    first, last = place == 0, place == N - 1
    inside = jnp.logical_not(jnp.logical_or(first, last))
    base = place * K

    def to(src, dst, send, recv, **target):
        return pltpu.make_async_remote_copy(
            src_ref=src, dst_ref=dst, send_sem=send, recv_sem=recv,
            device_id=target, device_id_type=MESH,
        )

    def toward(side):
        return after if side == 0 else before

    def settle(ref, sem):
        pltpu.make_async_copy(ref, ref, sem).wait()

    line_loads = [
        pltpu.make_async_copy(src, dst, s.load_sem.at[index])
        for index, (src, dst) in enumerate([
            (pivot_hbm, pivot), (coupling_hbm, coupling), (offsets_hbm, offsets),
        ])
    ]
    mode_loads = [
        pltpu.make_async_copy(src, dst, s.load_sem.at[3 + index])
        for index, (src, dst) in enumerate([
            (modes_hbm, modes), (column_patch_hbm, column_patch), (amplitude_hbm, amplitude),
            (mode_patch_hbm, mode_patch), (wall_mask_hbm, wall_mask), (stiffness_hbm, stiffness),
        ])
    ]
    for copy in line_loads + mode_loads:
        copy.start()

    barrier = pltpu.get_barrier_semaphore()

    def greet(**target):
        pl.semaphore_signal(barrier, inc=1, device_id=target, device_id_type=MESH)

    for hop in range(1, S):
        greet(surf=lax.rem(me + hop, S))
    for hop in range(1, N):
        other = lax.rem(place + hop, N)
        greet(norm=other)
        greet(surf=before, norm=other)
        greet(surf=after, norm=other)

    for copy in line_loads:
        copy.wait()
    cut = offsets[...]

    def link_step(k, carry):
        link[k] = jnp.where(cut == base + k, jnp.float32(0), coupling[k])
        return carry

    loop(K, link_step, 0)

    def lower_step(k, state):
        scaled = [p * link[k] for p in planes(pivot, k, 9)]
        put(s.rise, k, scaled)
        state = mat_mat(scaled, state)
        put(maps, k, state)
        return state

    first_map = [p * link[0] for p in planes(pivot, 0, 9)]
    put(maps, 0, first_map)
    ends = lax.fori_loop(1, K, lower_step, first_map)
    for c in range(9):
        s.end_map[c] = ends[c]

    def upper_step(step, state):
        k = K - 1 - step
        scaled = [p * link[k + 1] for p in planes(pivot, k, 9)]
        put(s.fall, k, scaled)
        state = added(planes(maps, k, 9), mat_mat(scaled, state[:9])) + mat_mat(scaled, state[9:])
        put(maps, k, state)
        return state

    top_state = ends + planes(pivot, K - 1, 9)
    put(maps, K - 1, top_state)
    top_state = lax.fori_loop(1, K, upper_step, top_state)
    for c in range(18):
        s.top_map[c] = link[0] * top_state[c]

    for copy in mode_loads:
        copy.wait()
    own_mode = me * M
    for b in range(blocks):
        patch = column_patch[b * B : (b + 1) * B, :]

        def mode_step(m, sums):
            weight = jnp.where(
                patch == mode_patch[own_mode + m], amplitude[own_mode + m], jnp.float32(0)
            )
            return [
                sums[c] + weight * modes[m, c, b * B : (b + 1) * B, :].astype(jnp.float32)
                for c in range(3)
            ]

        sums = loop(M, mode_step, [jnp.zeros((B, W), jnp.float32)] * 3)
        for c in range(3):
            for side in range(2):
                dest = 2 * b + side
                block = sums[c][side * R : (side + 1) * R]
                part[dest, c] = block
                part[(dest + 1) % S, 3, c : c + 1, :] = block[R - 1 : R]
                part[(dest - 1) % S, 3, 3 + c : 4 + c, :] = block[0:1]

    pl.semaphore_wait(barrier, S - 1 + 3 * (N - 1))

    def h_copy(q):
        return to(s.h_out.at[q], s.h_in.at[q], s.h_send.at[q], s.h_recv.at[q], norm=place - 1)

    full_copy = to(s.full_out, s.full_in, s.full_send, s.full_recv, norm=place - 1)

    def chunk(ref, q, start=0):
        return [ref[start + c, :, q * LANES : (q + 1) * LANES] for c in range(9)]

    def h_part(q):
        return [s.h_in[q, c].astype(jnp.float32) for c in range(9)]

    def h_full(sweep):
        if sweep > 0:
            return whole(s.full_in)
        pieces = [h_part(q) for q in range(chunks)]
        return [jnp.concatenate([p[c] for p in pieces], axis=1) for c in range(9)]

    def row_copy(slot, side, step):
        return to(
            s.row_out.at[slot, side], s.row_in.at[slot, side],
            s.row_send.at[slot], s.row_recv.at[slot],
            surf=toward(side), norm=place + step,
        )

    def send_rows(slot, step, values9):
        put_rows(s.row_out.at[slot, 0], [v[R - 1 : R] for v in values9])
        put_rows(s.row_out.at[slot, 1], [v[0:1] for v in values9])
        for side in range(2):
            row_copy(slot, side, step).start()

    UP, DOWN, ENDS, TOP = 0, N - 1, 0, N - 1

    def up_map(j):
        return to(s.up_out.at[j], s.up_in.at[j], s.up_send.at[j - 1], s.up_recv.at[j - 1], norm=place + 1)

    def down_map(j):
        return to(s.down_out.at[j], s.down_in.at[j], s.down_send.at[j - 1], s.down_recv.at[j - 1], norm=place - 1)

    def sends_up(j):
        return jnp.logical_and(place >= j, jnp.logical_not(last))

    def sends_down(j):
        return jnp.logical_and(N - 1 - place >= j, jnp.logical_not(first))

    def part_copy(hop):
        dest = lax.rem(me + hop, S)
        return to(part.at[dest], got.at[hop], s.part_send, s.part_recv, surf=dest)

    for hop in range(1, S):
        part_copy(hop).start()
    mask_up = to(wall_mask, s.mask_edge.at[0], s.mask_send, s.mask_recv, surf=after)
    mask_down = to(wall_mask, s.mask_edge.at[1], s.mask_send, s.mask_recv, surf=before)
    mask_up.start()
    mask_down.start()

    @pl.when(last)
    def _():
        s.h_in[...] = jnp.zeros(s.h_in.shape, jnp.bfloat16)
        s.full_in[...] = jnp.zeros(s.full_in.shape, jnp.float32)
        s.row_in[TOP] = jnp.zeros(s.row_in.shape[1:], jnp.float32)
        for q in range(chunks):
            put(s.h_out, q, [v.astype(jnp.bfloat16) for v in chunk(s.top_map, q)])
            h_copy(q).start()

    for j in range(1, min(2, N - 1)):

        @pl.when(sends_up(j))
        def _():
            value = whole(s.end_map)
            put(s.up_out, j, value)
            up_map(j).start()
            send_rows(UP + j, 1, value)

        @pl.when(sends_down(j))
        def _():
            value = [s.top_map[9 + c] for c in range(9)]
            put(s.down_out, j, value)
            down_map(j).start()
            send_rows(DOWN + j, -1, value)

    @pl.when(last)
    def _():
        send_rows(TOP, -1, whole(s.top_map))
        for c in range(9):
            s.full_out[c] = s.top_map[c]
        full_copy.start()

    send_rows(ENDS, 0, whole(s.end_map))

    def relay():
        for q in range(chunks):
            h_copy(q).wait_recv()
            inner = mat_mat(h_part(q), chunk(s.end_map, q))
            value = added(chunk(s.top_map, q), mat_mat(chunk(s.top_map, q, 9), inner))
            put(s.h_out, q, [v.astype(jnp.bfloat16) for v in value])
            h_copy(q).start()
            for c in range(9):
                s.row_out[TOP, 0, c : c + 1, q * LANES : (q + 1) * LANES] = value[c][R - 1 : R]
                s.row_out[TOP, 1, c : c + 1, q * LANES : (q + 1) * LANES] = value[c][0:1]
        for side in range(2):
            row_copy(TOP, side, -1).start()

    def full_relay():
        full_copy.wait_recv()
        inner = mat_mat(whole(s.full_in), whole(s.end_map))
        outer = mat_mat([s.top_map[9 + c] for c in range(9)], inner)
        for c in range(9):
            s.full_out[c] = s.top_map[c] + outer[c]
        full_copy.start()

    early = jnp.logical_and(inside, place == N - 2)

    @pl.when(early)
    def _():
        relay()

    for j in range(2, N - 1):

        @pl.when(sends_up(j))
        def _():
            up_map(j - 1).wait_recv()
            value = mat_mat(whole(s.end_map), planes(s.up_in, j - 1, 9))
            put(s.up_out, j, value)
            up_map(j).start()
            send_rows(UP + j, 1, value)

        @pl.when(sends_down(j))
        def _():
            down_map(j - 1).wait_recv()
            value = mat_mat([s.top_map[9 + c] for c in range(9)], planes(s.down_in, j - 1, 9))
            put(s.down_out, j, value)
            down_map(j).start()
            send_rows(DOWN + j, -1, value)

    def pack_step(k, carry):
        for c in range(18):
            value = maps[k, c]
            s.side_rows[0, c, pl.ds(k, 1), :] = value[R - 1 : R]
            s.side_rows[1, c, pl.ds(k, 1), :] = value[0:1]
        return carry

    loop(K, pack_step, 0, 2)

    def side_map_copy(side):
        return to(
            s.side_out.at[side], s.side_in.at[side], s.side_send, s.side_recv,
            surf=toward(side),
        )

    for side in range(2):
        for c in range(18):
            s.side_out[side, c] = s.side_rows[side, c].astype(jnp.bfloat16)
        side_map_copy(side).start()

    total = [part[me, c] for c in range(4)]
    settle(s.mask_edge, s.mask_recv)
    settle(got.at[pl.ds(0, S - 1)], s.part_recv)
    for hop in range(1, S):
        total = [total[c] + got[hop, c] for c in range(4)]
    mask = wall_mask[...].astype(jnp.float32)
    low_mask = s.mask_edge[0, R - 1 : R, :].astype(jnp.float32)
    high_mask = s.mask_edge[1, 0:1, :].astype(jnp.float32)
    row = lax.broadcasted_iota(jnp.int32, (R, W), 0)
    lane = lax.broadcasted_iota(jnp.int32, (R, W), 1)

    def around(x, low, high):
        nearby = jnp.where(row == 0, low, pltpu.roll(x, 1, 0))
        nearby += jnp.where(row == R - 1, high, pltpu.roll(x, R - 1, 0))
        nearby += jnp.where(lane == 0, jnp.float32(0), pltpu.roll(x, 1, 1))
        return nearby + jnp.where(lane == W - 1, jnp.float32(0), pltpu.roll(x, W - 1, 1))

    at_wall = jnp.where(first, jnp.float32(1), jnp.float32(0))
    for c in range(3):
        shift = total[c] * mask
        wall[c] = link[0] * shift * at_wall
        wall[3 + c] = around(
            shift, total[3][c : c + 1] * low_mask, total[3][3 + c : 4 + c] * high_mask
        )

    def edge_copy(sweep, side):
        return to(
            s.edge_out.at[sweep, side], s.edge_in.at[sweep, side],
            s.edge_send, s.edge_recv.at[sweep], surf=toward(side),
        )

    def up_copy(sweep, j):
        return to(
            s.f_out.at[sweep], s.z_in.at[sweep, place], s.z_send, s.z_recv.at[sweep],
            norm=place + j,
        )

    def down_copy(sweep, j):
        return to(
            s.o_out.at[sweep], s.z_in.at[sweep, place], s.z_send, s.z_recv.at[sweep],
            norm=place - j,
        )

    def up_edge(sweep, side, j):
        return to(
            s.fe_out.at[sweep, side], s.e_in.at[sweep, side, place],
            s.e_send, s.e_recv.at[sweep],
            surf=toward(side), norm=place + j,
        )

    def down_edge(sweep, side, j):
        return to(
            s.oe_out.at[sweep, side], s.e_in.at[sweep, side, place],
            s.e_send, s.e_recv.at[sweep],
            surf=toward(side), norm=place - j,
        )

    def change(send, sent, sweep, values3):
        for c in range(3):
            known = sent[c] if sweep > 0 else jnp.float32(0)
            step = (values3[c] - known).astype(jnp.bfloat16)
            send[sweep, c] = step
            sent[c] = known + step.astype(jnp.float32)

    def lower_place(j):
        return jnp.maximum(place - j, 0)

    def upper_place(j):
        return jnp.minimum(place + j, N - 1)

    def only(valid, values3):
        return [lax.select(valid, v, jnp.zeros_like(v)) for v in values3]

    def wide(ref, index):
        return [v.astype(jnp.float32) for v in planes(ref, index)]

    for sweep in range(SWEEPS):
        shared = sweep < SWEEPS - 1

        def source(k, sweep=sweep):
            if sweep == 0:
                blend = 1.0 - (base + k).astype(jnp.float32) / (K * N)
                factor = stiffness[k] * blend
                return [factor * wall[3 + c] for c in range(3)]
            return [
                stiffness[k]
                * around(out[k, c], halo[0, c, pl.ds(k, 1), :], halo[1, c, pl.ds(k, 1), :])
                for c in range(3)
            ]

        def forward(k, state):
            state = fold(
                mat_vec(planes(pivot, k, 9), source(k)), planes(s.rise, k, 9), state
            )
            put(values, k, state)
            return state

        start = mat_vec(
            planes(pivot, 0, 9), added(source(0), [wall[c] for c in range(3)])
        )
        put(values, 0, start)
        ends = later(K, forward, start, K - 1)
        if shared:
            put_rows(s.fe_out.at[sweep, 0], [v[R - 1 : R] for v in ends])
            put_rows(s.fe_out.at[sweep, 1], [v[0:1] for v in ends])
            for j in range(N - 1, 0, -1):

                @pl.when(place + j < N)
                def _():
                    for side in range(2):
                        up_edge(sweep, side, j).start()

        change(s.f_out, s.f_sent, sweep, ends)
        for j in range(N - 1, 0, -1):

            @pl.when(place + j < N)
            def _():
                up_copy(sweep, j).start()

        def keep(k, state):
            put(values, k, state)
            if shared:
                for c in range(3):
                    halo[0, c, pl.ds(k, 1), :] = state[c][R - 1 : R]
                    halo[1, c, pl.ds(k, 1), :] = state[c][0:1]

        def backward(step, state):
            k = K - 1 - step
            state = fold(planes(values, k), planes(s.fall, k, 9), state)
            keep(k, state)
            return state

        keep(K - 1, ends)
        tops = later(K, backward, ends, K - 1)

        if sweep == 0:

            @pl.when(jnp.logical_and(inside, jnp.logical_not(early)))
            def _():
                relay()

        @pl.when(jnp.logical_not(first))
        def _():
            top = added(
                [link[0] * v for v in tops],
                mat_vec([s.top_map[9 + c] for c in range(9)], mat_vec(h_full(sweep), ends)),
            )
            if shared:
                put_rows(s.oe_out.at[sweep, 0], [v[R - 1 : R] for v in top])
                put_rows(s.oe_out.at[sweep, 1], [v[0:1] for v in top])
                for j in range(N - 1, 0, -1):

                    @pl.when(place - j >= 0)
                    def _():
                        for side in range(2):
                            down_edge(sweep, side, j).start()

            change(s.o_out, s.o_sent, sweep, top)
            for j in range(N - 1, 0, -1):

                @pl.when(place - j >= 0)
                def _():
                    down_copy(sweep, j).start()

        if shared:
            for side in range(2):
                s.edge_out[sweep, side] = halo[side].astype(jnp.bfloat16)
                edge_copy(sweep, side).start()
                up_edge(sweep, side, 0).start()

        if sweep == 0:

            @pl.when(early)
            def _():
                full_relay()


        settle(s.z_in.at[sweep, pl.ds(0, N - 1)], s.z_recv.at[sweep])
        for j in range(1, N):
            if sweep == 0 and j > 1:

                @pl.when(jnp.logical_and(last, place >= j))
                def _():
                    up_map(j - 1).wait_recv()

                @pl.when(jnp.logical_and(first, N - 1 - place >= j))
                def _():
                    down_map(j - 1).wait_recv()

        rising = planes(s.enter, 0) if sweep > 0 else [jnp.zeros((R, W), jnp.float32)] * 3
        falling = planes(s.enter, 1) if sweep > 0 else [jnp.zeros((R, W), jnp.float32)] * 3
        for j in range(1, N):
            moved = wide(s.z_in.at[sweep], lower_place(j))
            if j > 1:
                moved = mat_vec(planes(s.up_in, j - 1, 9), moved)
            rising = added(rising, only(place >= j, moved))
            moved = wide(s.z_in.at[sweep], upper_place(j))
            if j > 1:
                moved = mat_vec(planes(s.down_in, j - 1, 9), moved)
            falling = added(falling, only(place + j < N, moved))
        put(s.enter, 0, rising)
        put(s.enter, 1, falling)

        if sweep < 2:

            @pl.when(first)
            def _():
                if sweep == 0:
                    for q in range(chunks):
                        h_copy(q).wait_recv()
                else:
                    full_copy.wait_recv()

        entering = rising
        state = added(ends, mat_vec(whole(s.end_map), entering))
        above = added(falling, mat_vec(h_full(sweep), state))

        def finish(k, carry):
            state = added(planes(values, k), mat_vec(planes(maps, k, 9), entering))
            state = added(state, mat_vec([maps[k, 9 + c] for c in range(9)], above))
            put(out, k, state)
            return carry

        loop(K, finish, 0, K)

        if sweep == 0:

            @pl.when(jnp.logical_and(inside, jnp.logical_not(early)))
            def _():
                full_relay()

        if shared:
            if sweep == 0:
                settle(s.side_in, s.side_recv)
                settle(s.row_in.at[ENDS], s.row_recv.at[ENDS])

                @pl.when(jnp.logical_not(last))
                def _():
                    settle(s.row_in.at[TOP], s.row_recv.at[TOP])

                for j in range(2, N):

                    @pl.when(place >= j)
                    def _():
                        settle(s.row_in.at[UP + j - 1], s.row_recv.at[UP + j - 1])

                    @pl.when(N - 1 - place >= j)
                    def _():
                        settle(s.row_in.at[DOWN + j - 1], s.row_recv.at[DOWN + j - 1])

            settle(s.e_in.at[sweep], s.e_recv.at[sweep])
            settle(s.edge_in.at[sweep], s.edge_recv.at[sweep])
            for side in range(2):
                entered = [jnp.zeros((1, W), jnp.float32)] * 3
                leaving = [jnp.zeros((1, W), jnp.float32)] * 3
                for j in range(1, N):
                    moved = rows(s.e_in.at[sweep, side, lower_place(j)])
                    if j > 1:
                        moved = mat_vec(rows(s.row_in.at[UP + j - 1, side], 9), moved)
                    entered = added(entered, only(place >= j, moved))
                    moved = rows(s.e_in.at[sweep, side, upper_place(j)])
                    if j > 1:
                        moved = mat_vec(rows(s.row_in.at[DOWN + j - 1, side], 9), moved)
                    leaving = added(leaving, only(place + j < N, moved))
                state = added(
                    rows(s.e_in.at[sweep, side, place]),
                    mat_vec(rows(s.row_in.at[ENDS, side], 9), entered),
                )
                higher = added(
                    leaving, mat_vec(rows(s.row_in.at[TOP, side], 9), state)
                )
                for c in range(3):
                    value = s.edge_in[sweep, side, c].astype(jnp.float32)
                    for b in range(3):
                        value += s.side_in[side, 3 * c + b].astype(jnp.float32) * entered[b]
                        value += s.side_in[side, 9 + 3 * c + b].astype(jnp.float32) * higher[b]
                    halo[side, c] = value

    settle(got.at[pl.ds(0, S - 1)], s.part_send)
    settle(s.mask_edge, s.mask_send)
    settle(s.side_out, s.side_send)
    settle(s.row_out.at[ENDS], s.row_send.at[ENDS])
    settle(s.z_in.at[:, pl.ds(0, N - 1)], s.z_send)
    settle(s.edge_out, s.edge_send)
    settle(s.e_in, s.e_send)

    @pl.when(jnp.logical_not(first))
    def _():
        full_copy.wait_send()
        for q in range(chunks):
            h_copy(q).wait_send()
        settle(s.row_out.at[TOP], s.row_send.at[TOP])

    for j in range(1, N - 1):

        @pl.when(sends_up(j))
        def _():
            up_map(j).wait_send()
            settle(s.row_out.at[UP + j], s.row_send.at[UP + j])

        @pl.when(sends_down(j))
        def _():
            down_map(j).wait_send()
            settle(s.row_out.at[DOWN + j], s.row_send.at[DOWN + j])


def per_device(
    surf_size, norm_size, mode_shapes, amplitude, mode_patch, column_patch, wall_mask, offsets,
    coupling, pivot_inv, stiffness,
):
    S, N = surf_size, norm_size
    modes = mode_shapes.transpose(0, 2, 1, 3)
    pivot = pivot_inv.transpose(0, 2, 1, 3)
    K, _, R, W = pivot.shape
    C = W // LANES
    f32, bf16 = jnp.float32, jnp.bfloat16
    vmem = pl.BlockSpec(memory_space=pltpu.VMEM)
    hbm = pl.BlockSpec(memory_space=pltpu.HBM)
    dma = pltpu.SemaphoreType.DMA

    def room(*shape):
        return pltpu.VMEM(shape, f32)

    def half(*shape):
        return pltpu.VMEM(shape, bf16)

    G = SWEEPS - 1
    scratch = dict(
        modes=half(*modes.shape),
        coupling=room(K, R, W),
        pivot=room(K, 9, R, W),
        stiffness=room(K, R, W),
        link=room(K, R, W),
        rise=room(K, 9, R, W),
        fall=room(K, 9, R, W),
        maps=room(K, 18, R, W),
        end_map=room(9, R, W),
        top_map=room(18, R, W),
        part=room(S, 4, R, W),
        got=room(S, 4, R, W),
        mask_edge=pltpu.VMEM((2, R, W), jnp.int32),
        wall=room(6, R, W),
        values=room(K, 3, R, W),
        enter=room(2, 3, R, W),
        halo=room(2, 3, K, W),
        edge_out=half(G, 2, 3, K, W),
        edge_in=half(G, 2, 3, K, W),
        side_rows=room(2, 18, K, W),
        side_out=half(2, 18, K, W),
        side_in=half(2, 18, K, W),
        row_out=room(2 * N - 2, 2, 9, W),
        row_in=room(2 * N - 2, 2, 9, W),
        z_in=half(SWEEPS, N, 3, R, W),
        f_out=half(SWEEPS, 3, R, W),
        f_sent=room(3, R, W),
        o_out=half(SWEEPS, 3, R, W),
        o_sent=room(3, R, W),
        e_in=room(G, 2, N, 3, W),
        fe_out=room(G, 2, 3, W),
        oe_out=room(G, 2, 3, W),
        h_in=half(C, 9, R, LANES),
        h_out=half(C, 9, R, LANES),
        full_in=room(9, R, W),
        full_out=room(9, R, W),
        up_in=room(N, 9, R, W),
        up_out=room(N, 9, R, W),
        down_in=room(N, 9, R, W),
        down_out=room(N, 9, R, W),
        load_sem=dma((9,)),
        amplitude=pltpu.SMEM(amplitude.shape, f32),
        mode_patch=pltpu.SMEM(mode_patch.shape, jnp.int32),
        column_patch=pltpu.VMEM(column_patch.shape, jnp.int32),
        wall_mask=pltpu.VMEM(wall_mask.shape, jnp.int32),
        offsets=pltpu.VMEM(offsets.shape, jnp.int32),
    )
    sems = dict(
        part=(), mask=(), h=(C,), full=(), row=(2 * N - 2,), side=(), up=(max(N - 2, 1),),
        down=(max(N - 2, 1),), z=(SWEEPS,), e=(G,), edge=(G,),
    )
    for name, shape in sems.items():
        scratch[name + "_send"] = dma(shape) if shape and name not in ("z", "e", "edge") else dma
        scratch[name + "_recv"] = dma(shape) if shape else dma
    out = pl.pallas_call(
        functools.partial(kernel, S, N, tuple(scratch)),
        out_shape=pltpu.VMEM((K, 3, R, W), f32),
        in_specs=[hbm] * 9,
        out_specs=vmem,
        scratch_shapes=list(scratch.values()),
        compiler_params=pltpu.CompilerParams(
            collective_id=0, has_side_effects=True, vmem_limit_bytes=62 * 1024 * 1024
        ),
        name="line_sweeps",
    )(amplitude, mode_patch, column_patch, wall_mask, offsets, modes, coupling, pivot, stiffness)
    return out.transpose(0, 2, 1, 3)


def solution(mesh):
    return jax.shard_map(
        functools.partial(per_device, mesh.shape["surf"], mesh.shape["norm"]),
        mesh=mesh,
        in_specs=(
            P("surf", None, None, None),
            P(),
            P(),
            P(),
            P("surf", None),
            P("surf", None),
            P("norm", "surf", None),
            P("norm", "surf", None, None),
            P("norm", "surf", None),
        ),
        out_specs=P("norm", "surf", None, None),
        check_vma=False,
    )
```
